32 devices in a mesh: dp: 16 (over z, y, x), inner: 2 (over core).
Axes of the slice: x: 2, y: 2, z: 4, core: 2. Of those that a mesh axis runs over, the one named last changes fastest.
Arguments:
- features: bfloat16 [8192, 2048], P(('dp', 'inner')), may hold values from -12 to 12
- kv_cotangent: bfloat16 [8192, 512], P(('dp', 'inner')), may hold values from -0.0625 to 0.0625
- owner_of_block: int32 [64], replicated, may hold values from 0 to 15, as said below
- first_moment: float32 [16, 4, 128, 128], P('dp'), may hold values from -1.25 to 1.25
- second_moment: float32 [16, 4, 128, 128], P('dp'), may hold values from 0.05 to 1
- left_stat: float32 [16, 4, 128, 128], P('dp')
- right_stat: float32 [16, 4, 128, 128], P('dp')
- left_basis: bfloat16 [16, 4, 128, 128], P('dp')
- right_basis: bfloat16 [16, 4, 128, 128], P('dp')
Outputs:
- update: bfloat16 [2048, 512], replicated
- new_left_basis: bfloat16 [16, 4, 128, 128], P('dp')
- new_right_basis: bfloat16 [16, 4, 128, 128], P('dp')
The draws below stay inside these ranges and needn't reach their ends.
Inputs may be any that keep to these rules, and one draw needn't show every extreme that they name: `owner_of_block`: each index of dp owns at most 4 tiles, and one index owns exactly 4.
All inputs are finite; a program needn't handle non-finite values.
Results may differ from the reference program's by a relative error of at most 0.001.
Values may be sent and summed in bfloat16 or wider, within the bound.
No kernel may reach another device: no remote copies, remote signals or barrier semaphores. Data moves between devices by JAX's collectives and lax.ppermute only.
A program may use at most 64 MiB of HBM per device.

```python
import math
import jax
import jax.numpy as jnp
from jax import lax

D_WIN = 2048
KV_COLS = 512
BLK = 128
NS_STEPS = 12
BLOCKS = 64
CAPACITY = 4
TOKENS = 8192
N_DP = 16


def definite_stat(key):
    key_diag, key_noise = jax.random.split(key)
    spread = jnp.exp(jax.random.uniform(key_diag, (N_DP, CAPACITY, BLK), jnp.float32, jnp.log(0.3), jnp.log(3.0)))
    diagonal = BLK * spread
    noise = jax.random.uniform(key_noise, (N_DP, CAPACITY, BLK, BLK), jnp.float32, -0.2, 0.2)
    symmetric = 0.5 * (noise + jnp.swapaxes(noise, 2, 3))
    positions = jnp.arange(BLK)
    distance = jnp.abs(positions[:, None] - positions[None, :])
    shape_part = jnp.where(distance == 0, 1.0, jnp.where(distance <= 2, symmetric, symmetric * (0.75 / BLK)))
    root = jnp.sqrt(diagonal)
    return (root[..., :, None] * shape_part * root[..., None, :]).astype(jnp.float32)


def near_identity(key):
    noise = jax.random.uniform(key, (N_DP, CAPACITY, BLK, BLK), jnp.float32, -0.15, 0.15)
    return (jnp.eye(BLK, dtype=jnp.float32) + noise).astype(jnp.bfloat16)


def draw_left_stat(key, part):
    return definite_stat(jax.random.fold_in(key, 11))


def draw_right_stat(key, part):
    return definite_stat(jax.random.fold_in(key, 23))


def draw_left_basis(key, part):
    return near_identity(jax.random.fold_in(key, 37))


def draw_right_basis(key, part):
    return near_identity(jax.random.fold_in(key, 41))


def draw_owner_of_block(key, part):
    total_slots = N_DP * CAPACITY
    key_perm, key_shuffle = jax.random.split(jax.random.fold_in(key, 53))
    permuted = jax.random.permutation(key_perm, total_slots)
    picked = permuted[0] // CAPACITY
    order_key = jnp.where(permuted // CAPACITY == picked, permuted % CAPACITY - CAPACITY, jnp.arange(total_slots))
    order = jnp.argsort(order_key, stable=True)
    chosen = permuted[order][:BLOCKS]
    shuffle = jax.random.permutation(key_shuffle, BLOCKS)
    return (chosen // CAPACITY)[shuffle].astype(jnp.int32)


def raised(array, key, source, target, shards_of, factor):
    def block_of(axis_at):
        return (jnp.arange(array.shape[axis_at]) // (array.shape[axis_at] // shards_of)).reshape((-1,) + (1,) * (array.ndim - 1 - axis_at))

    near = jax.random.permutation(key, shards_of)[block_of(target)]
    second = (block_of(target) + shards_of // 2) % shards_of
    return jnp.where((block_of(source) == near) | (block_of(source) == second), factor * array, array)


def shard_levels(key, extent, cuts, least, high):
    def one(dim, blocks):
        heights = jax.random.uniform(jax.random.fold_in(jax.random.fold_in(key, 6), dim), (blocks,), jnp.float32, least / len(cuts), high / len(cuts))
        return jnp.repeat(jnp.exp(heights), extent[dim] // blocks).reshape((-1,) + (1,) * (len(extent) - dim - 1))

    loudness = one(*cuts[0])
    for cut in cuts[1:]:
        loudness = loudness * one(*cut)
    return loudness


def scatter_about(rng, dims, deviation, limit, cuts=(), held_as=jnp.bfloat16):
    drawn = deviation * jax.random.normal(rng, dims, jnp.float32)
    if cuts:
        drawn = drawn * shard_levels(rng, dims, cuts, -0.22, 0.18)
    return jnp.clip(drawn, -limit, limit).astype(held_as)


def heavy_noise(key, shape, scale, bound, pieces, heavy, kind=jnp.bfloat16):
    array = scale * jax.random.normal(key, shape, jnp.float32)
    if pieces:
        array = array * shard_levels(key, shape, pieces, -0.22, 0.18)
    return jnp.clip(raised(array, jax.random.fold_in(key, 3), *heavy), -bound, bound).astype(kind)


def setup_inputs(seed: int = 0) -> dict:
    key_of = jax.random.split(jax.random.key(seed), 10)
    return {
        "features": heavy_noise(key_of[0], (TOKENS, D_WIN), 1.0, 12.0, ((0, 32),), (0, 1, 32, 2.75)),
        "kv_cotangent": scatter_about(key_of[1], (TOKENS, KV_COLS), (1.0 / TOKENS ** 0.5), 0.0625, ((0, 32),)),
        "owner_of_block": draw_owner_of_block(jax.random.fold_in(key_of[9], 71), 0),
        "first_moment": scatter_about(key_of[3], (N_DP, CAPACITY, BLK, BLK), 0.2, 1.25, ((0, 16),), jnp.float32),
        "second_moment": jnp.clip(jnp.exp(math.log(1.0) - 2.9957323 * jax.random.uniform(key_of[4], (N_DP, CAPACITY, BLK, BLK), jnp.float32) ** shard_levels(key_of[4], (N_DP, CAPACITY, BLK, BLK), ((0, 16),), -0.2, 0.2)), 0.05, 1.0),
        "left_stat": draw_left_stat(jax.random.fold_in(key_of[9], 71), 0),
        "right_stat": draw_right_stat(jax.random.fold_in(key_of[9], 71), 0),
        "left_basis": draw_left_basis(jax.random.fold_in(key_of[9], 71), 0),
        "right_basis": draw_right_basis(jax.random.fold_in(key_of[9], 71), 0),
    }


highest = lax.Precision.HIGHEST

def rotate_in(basis_left, matrix, basis_right):
    half = jnp.einsum('sji,sjk->sik', basis_left, matrix, precision=highest)
    return jnp.einsum('sij,sjk->sik', half, basis_right, precision=highest)

def rotate_out(basis_left, matrix, basis_right):
    half = jnp.einsum('sij,sjk->sik', basis_left, matrix, precision=highest)
    return jnp.einsum('sij,skj->sik', half, basis_right, precision=highest)

def orthogonalize(stat, basis):
    power = jnp.einsum('sij,sjk->sik', stat, basis, precision=highest)
    scale = jnp.sqrt(lax.optimization_barrier(jnp.sum(power * power, axis=(1, 2), keepdims=True)) + 1e-06)
    iterate = power / scale
    for sweep in range(NS_STEPS):
        gram = jnp.einsum('sji,sjk->sik', iterate, iterate, precision=highest)
        iterate = 1.5 * iterate - 0.5 * jnp.einsum('sij,sjk->sik', iterate, gram, precision=highest)
    return iterate

def soap_tiles(grads, first, second, stat_left, stat_right, basis_left, basis_right):
    rotated = rotate_in(basis_left, grads, basis_right)
    moment = 0.95 * first + 0.05 * grads
    moment_rot = rotate_in(basis_left, moment, basis_right)
    second_new = 0.95 * second + 0.05 * rotated * rotated
    direction = rotate_out(basis_left, moment_rot / (jnp.sqrt(second_new) + 1e-08), basis_right)
    left_new = 0.95 * stat_left + 0.05 * jnp.einsum('sij,skj->sik', grads, grads, precision=highest)
    right_new = 0.95 * stat_right + 0.05 * jnp.einsum('sji,sjk->sik', grads, grads, precision=highest)
    return (direction, orthogonalize(left_new, basis_left), orthogonalize(right_new, basis_right))

def reference(features, kv_cotangent, owner_of_block, first_moment, second_moment, left_stat, right_stat, left_basis, right_basis):
    token_block = math.gcd(TOKENS, 8192)
    count = TOKENS // token_block

    def add_rows(total, index):
        start = (index * token_block).astype(jnp.int32)
        rows = lax.dynamic_slice_in_dim(features, start, token_block, 0).astype(jnp.float32)
        cots = lax.dynamic_slice_in_dim(kv_cotangent, start, token_block, 0).astype(jnp.float32)
        term = lax.dot_general(rows, cots, (((0,), (0,)), ((), ())), precision=highest, preferred_element_type=jnp.float32)
        return (total + term, None)
    grad, unused = lax.scan(add_rows, jnp.zeros((D_WIN, KV_COLS), jnp.float32), jnp.arange(count, dtype=jnp.int32))
    row_tiles = D_WIN // BLK
    col_tiles = KV_COLS // BLK
    grads = grad.reshape(row_tiles, BLK, col_tiles, BLK).transpose(0, 2, 1, 3).reshape(BLOCKS, BLK, BLK)
    block_ids = jnp.arange(BLOCKS, dtype=jnp.int32)
    same = owner_of_block[:, None] == owner_of_block[None, :]
    earlier = block_ids[None, :] < block_ids[:, None]
    slot = lax.optimization_barrier(jnp.sum((same & earlier).astype(jnp.int32), axis=1)).astype(jnp.int32)
    owner = owner_of_block
    direction, left_iter, right_iter = soap_tiles(grads, first_moment[owner, slot], second_moment[owner, slot], left_stat[owner, slot], right_stat[owner, slot], left_basis[owner, slot].astype(jnp.float32), right_basis[owner, slot].astype(jnp.float32))
    update = direction.astype(jnp.bfloat16).reshape(row_tiles, col_tiles, BLK, BLK).transpose(0, 2, 1, 3).reshape(D_WIN, KV_COLS)
    new_left = left_basis.at[owner, slot].set(left_iter.astype(jnp.bfloat16))
    new_right = right_basis.at[owner, slot].set(right_iter.astype(jnp.bfloat16))
    return (update, new_left, new_right)
```

```python
import functools

import jax
import jax.numpy as jnp
from jax import lax
from jax.experimental import pallas as pl
from jax.experimental.pallas import tpu as pltpu
from jax.sharding import PartitionSpec as P

NS_STEPS = 12


highest = lax.Precision.HIGHEST


def rotate_in(basis_left, matrix, basis_right):
    half = jnp.einsum("sji,sjk->sik", basis_left, matrix, precision=highest)
    return jnp.einsum("sij,sjk->sik", half, basis_right, precision=highest)


def rotate_out(basis_left, matrix, basis_right):
    half = jnp.einsum("sij,sjk->sik", basis_left, matrix, precision=highest)
    return jnp.einsum("sij,skj->sik", half, basis_right, precision=highest)


def orthogonalize(stat, basis):
    power = jnp.einsum("sij,sjk->sik", stat, basis, precision=highest)
    scale = jnp.sqrt(jnp.sum(power * power, axis=(1, 2), keepdims=True) + 1e-06)
    iterate = power / scale
    for sweep in range(NS_STEPS):
        gram = jnp.einsum("sji,sjk->sik", iterate, iterate, precision=highest)
        iterate = 1.5 * iterate - 0.5 * jnp.einsum("sij,sjk->sik", iterate, gram, precision=highest)
    return iterate


def soap_tiles(grads, first, second, stat_left, stat_right, basis_left, basis_right):
    rotated = rotate_in(basis_left, grads, basis_right)
    moment = 0.95 * first + 0.05 * grads
    moment_rot = rotate_in(basis_left, moment, basis_right)
    second_new = 0.95 * second + 0.05 * rotated * rotated
    direction = rotate_out(basis_left, moment_rot / (jnp.sqrt(second_new) + 1e-08), basis_right)
    left_new = 0.95 * stat_left + 0.05 * jnp.einsum("sij,skj->sik", grads, grads, precision=highest)
    right_new = 0.95 * stat_right + 0.05 * jnp.einsum(
        "sji,sjk->sik", grads, grads, precision=highest
    )
    return (direction, orthogonalize(left_new, basis_left), orthogonalize(right_new, basis_right))


def per_device_plain(
    features,
    kv_cotangent,
    owner_of_block,
    first_moment,
    second_moment,
    left_stat,
    right_stat,
    left_basis,
    right_basis,
):
    tile = left_basis.shape[-1]
    capacity = left_basis.shape[1]
    d_win = features.shape[1]
    width = kv_cotangent.shape[1]
    row_tiles = d_win // tile
    col_tiles = width // tile
    nblocks = owner_of_block.shape[0]
    owner_here = lax.axis_index("dp")
    block_ids = jnp.arange(nblocks, dtype=jnp.int32)
    same = owner_of_block[:, None] == owner_of_block[None, :]
    earlier = block_ids[None, :] < block_ids[:, None]
    slot = jnp.sum((same & earlier).astype(jnp.int32), axis=1)
    slot_ids = jnp.arange(capacity, dtype=jnp.int32)
    match = (owner_of_block[None, :] == owner_here) & (slot[None, :] == slot_ids[:, None])
    live = jnp.any(match, axis=1)
    which = jnp.sum(jnp.where(match, block_ids[None, :], 0), axis=1)
    row_start = which // col_tiles * tile
    col_start = which % col_tiles * tile
    partial_grad = lax.dot_general(
        features, kv_cotangent, (((0,), (0,)), ((), ())), preferred_element_type=jnp.float32
    )
    grad = lax.psum(partial_grad, ("dp", "inner"))
    fetched = [
        lax.dynamic_slice(grad, (row_start[slot_index], col_start[slot_index]), (tile, tile))
        for slot_index in range(capacity)
    ]
    grads = jnp.stack(fetched)
    basis_left = left_basis[0].astype(jnp.float32)
    basis_right = right_basis[0].astype(jnp.float32)
    direction, left_iter, right_iter = soap_tiles(
        grads,
        first_moment[0],
        second_moment[0],
        left_stat[0],
        right_stat[0],
        basis_left,
        basis_right,
    )
    direction_low = direction.astype(jnp.bfloat16)
    everyone = lax.all_gather(direction_low[None], "dp", axis=0, tiled=True)
    tiles = everyone[owner_of_block, slot]
    update = (
        tiles.reshape(row_tiles, col_tiles, tile, tile).transpose(0, 2, 1, 3).reshape(d_win, width)
    )
    keep = live[:, None, None]
    new_left = jnp.where(keep, left_iter.astype(jnp.bfloat16), left_basis[0])
    new_right = jnp.where(keep, right_iter.astype(jnp.bfloat16), right_basis[0])
    return (update, new_left[None], new_right[None])


def swap_along(values, axis, size, bit):
    return lax.ppermute(values, axis, [(i, i ^ bit) for i in range(size)])


def product(left, right, dims):
    return lax.dot_general(
        left, right, (dims, ((), ())), precision=highest, preferred_element_type=jnp.float32
    )


MM = ((1,), (0,))
MT = ((1,), (1,))
TM = ((0,), (0,))


def grad_kernel(col_tiles, near, order_ref, f_own, f_sib, kv_own, kv_sib, *outs):
    tile = outs[0].shape[-1]
    rows = f_own.shape[0]
    kv_rows = outs[-1]
    kv_rows[:, :rows] = kv_own[...].T
    kv_rows[:, rows:] = kv_sib[...].T
    half = outs[0].shape[0]
    for part, out in enumerate(outs[:-1]):

        def one(index, carry, part=part, out=out):
            block = order_ref[part * half + index]
            row = pl.multiple_of(block // col_tiles * tile, tile)
            col = pl.multiple_of(block % col_tiles * tile, tile)
            cots = kv_rows[pl.ds(col, tile), :]
            total = jnp.dot(
                cots[:, :rows], f_own[:, pl.ds(row, tile)], preferred_element_type=jnp.float32
            )
            total += jnp.dot(
                cots[:, rows:], f_sib[:, pl.ds(row, tile)], preferred_element_type=jnp.float32
            )
            out[index] = total
            return carry

        lax.fori_loop(0, half, one, 0, unroll=4)


def grad_parts(order, f_own, f_sib, kv_own, kv_sib, tile, col_tiles, owners):
    shape = jax.ShapeDtypeStruct((owners // 2, tile, tile), jnp.float32)
    vmem = pl.BlockSpec(memory_space=pltpu.VMEM)
    rows, width = kv_own.shape
    return pl.pallas_call(
        functools.partial(grad_kernel, col_tiles, None),
        out_shape=(shape,) * 4,
        in_specs=[pl.BlockSpec(memory_space=pltpu.SMEM)] + [vmem] * 4,
        out_specs=(vmem,) * 4,
        scratch_shapes=[pltpu.VMEM((width, 2 * rows), jnp.bfloat16)],
        compiler_params=pltpu.CompilerParams(vmem_limit_bytes=32 * 2**20),
        name="grad_parts",
    )(order, f_own, f_sib, kv_own, kv_sib)


def direction_kernel(side_ref, a_ref, b_ref, m_ref, v_ref, ql_ref, qr_ref, dir_ref, grad_ref):
    for k in range(2):
        grad_t = a_ref[k] + b_ref[k]
        grad = grad_t.T
        grad_ref[k] = grad
        left = ql_ref[0, k].astype(jnp.float32)
        right = qr_ref[0, k].astype(jnp.float32)
        rotated = product(product(left, grad, TM), right, MM)
        moment = 0.95 * m_ref[0, k] + 0.05 * grad
        moment_rot = product(product(left, moment, TM), right, MM)
        second = 0.95 * v_ref[0, k] + 0.05 * rotated * rotated
        scaled = moment_rot / (jnp.sqrt(second) + 1e-08)
        out = product(product(left, scaled, MM), right, MT)
        dir_ref[k] = out.astype(dir_ref.dtype)


def slots_of(side, *arrays):
    tile = arrays[0].shape[-1]
    return [pl.BlockSpec((1, 2, tile, tile), lambda i, s: (0, s[0], 0, 0)) for _ in arrays]


def whole(shape):
    return pl.BlockSpec(shape, lambda i, s: (0,) * len(shape))


def directions(side, kept, got, first, second, basis_left, basis_right):
    tile = first.shape[-1]
    pair = (2, tile, tile)
    return pl.pallas_call(
        direction_kernel,
        out_shape=(
            jax.ShapeDtypeStruct(pair, jnp.bfloat16),
            jax.ShapeDtypeStruct(pair, jnp.float32),
        ),
        grid_spec=pltpu.PrefetchScalarGridSpec(
            num_scalar_prefetch=1,
            grid=(1,),
            in_specs=[whole(pair), whole(pair)]
            + slots_of(side, first, second, basis_left, basis_right),
            out_specs=(whole(pair), whole(pair)),
        ),
        name="directions",
    )(side, kept, got, first, second, basis_left, basis_right)


def refresh_kernel(side_ref, g_ref, l_ref, r_ref, ql_ref, qr_ref, left_ref, right_ref):
    iterates = []
    for k in range(2):
        grad = g_ref[k]
        for stat, basis, dims in ((l_ref, ql_ref, MT), (r_ref, qr_ref, TM)):
            new = 0.95 * stat[0, k] + 0.05 * product(grad, grad, dims)
            power = product(new, basis[0, k].astype(jnp.float32), MM)
            iterates.append(power / jnp.sqrt(jnp.sum(power * power) + 1e-06))

    def sweep(step, values):
        grams = [product(x, x, TM) for x in values]
        return tuple(1.5 * x - 0.5 * product(x, g, MM) for x, g in zip(values, grams))

    values = lax.fori_loop(0, NS_STEPS, sweep, tuple(iterates))
    for k in range(2):
        left_ref[k] = values[2 * k].astype(left_ref.dtype)
        right_ref[k] = values[2 * k + 1].astype(right_ref.dtype)


def refreshed(side, grads, stat_left, stat_right, basis_left, basis_right):
    tile = stat_left.shape[-1]
    pair = (2, tile, tile)
    return pl.pallas_call(
        refresh_kernel,
        out_shape=(jax.ShapeDtypeStruct(pair, jnp.bfloat16),) * 2,
        grid_spec=pltpu.PrefetchScalarGridSpec(
            num_scalar_prefetch=1,
            grid=(1,),
            in_specs=[whole(pair)]
            + slots_of(side, stat_left, stat_right, basis_left, basis_right),
            out_specs=(whole(pair), whole(pair)),
        ),
        cost_estimate=pl.CostEstimate(
            flops=4 * 26 * 6 * 2 * tile**3, bytes_accessed=800_000, transcendentals=0
        ),
        name="refreshed",
    )(side, grads, stat_left, stat_right, basis_left, basis_right)


def place_kernel(col_tiles, order_ref, live_ref, *refs):
    sources, out, sems = refs[:-2], refs[-2], refs[-1]
    tile = sources[0].shape[-1]
    half = sources[0].shape[0]

    def copy(source, index, entry):
        block = order_ref[entry]
        row = pl.multiple_of(block // col_tiles * tile, tile)
        col = pl.multiple_of(block % col_tiles * tile, tile)
        return pltpu.make_async_copy(
            source.at[index], out.at[pl.ds(row, tile), pl.ds(col, tile)], sems.at[entry]
        )

    for number, source in enumerate(sources):
        for index in range(half):
            entry = number * half + index

            @pl.when(live_ref[entry] == 1)
            def _():
                copy(source, index, entry).start()

    for number, source in enumerate(sources):
        for index in range(half):
            entry = number * half + index

            @pl.when(live_ref[entry] == 1)
            def _():
                copy(source, index, entry).wait()


def placed(order, live, sources, d_win, width):
    tile = sources[0].shape[-1]
    smem = pl.BlockSpec(memory_space=pltpu.SMEM)
    anywhere = pl.BlockSpec(memory_space=pl.ANY)
    return pl.pallas_call(
        functools.partial(place_kernel, width // tile),
        out_shape=jax.ShapeDtypeStruct((d_win, width), jnp.bfloat16),
        in_specs=[smem, smem] + [anywhere] * len(sources),
        out_specs=anywhere,
        scratch_shapes=[pltpu.SemaphoreType.DMA((order.shape[0],))],
        name="placed",
    )(order, live, *sources)


def per_device_dealt(
    owners,
    features,
    kv_cotangent,
    owner_of_block,
    first_moment,
    second_moment,
    left_stat,
    right_stat,
    left_basis,
    right_basis,
):
    tile = left_basis.shape[-1]
    capacity = left_basis.shape[1]
    d_win = features.shape[1]
    width = kv_cotangent.shape[1]
    nblocks = owner_of_block.shape[0]
    here = lax.axis_index("dp")
    core = lax.axis_index("inner")
    bits = owners.bit_length() - 1
    orders = ([0, 1] + list(range(2, bits)), [1, 0] + list(range(2, bits)))

    f_sib = swap_along(features, "inner", 2, 1)
    kv_sib = swap_along(kv_cotangent, "inner", 2, 1)

    offsets = []
    for order in orders:
        offsets.append(
            [
                sum(((p >> (bits - 1 - i)) & 1) << bit for i, bit in enumerate(order))
                for p in range(owners)
            ]
        )
    block_ids = jnp.arange(nblocks, dtype=jnp.int32)
    same = owner_of_block[:, None] == owner_of_block[None, :]
    earlier = block_ids[None, :] < block_ids[:, None]
    slot = jnp.sum((same & earlier).astype(jnp.int32), axis=1)
    offset = jnp.array(offsets, dtype=jnp.int32)[None, :, :]
    owner_at = jnp.broadcast_to(here ^ offset, (2, 2, owners))
    side_at = core ^ lax.broadcasted_iota(jnp.int32, (2, 2, owners), 0)
    slot_at = 2 * side_at + lax.broadcasted_iota(jnp.int32, (2, 2, owners), 1)
    match = (owner_of_block == owner_at[..., None]) & (slot == slot_at[..., None])
    which = jnp.sum(jnp.where(match, block_ids, 0), axis=-1)
    live = jnp.sum(match.astype(jnp.int32), axis=-1)

    near = owners // 2
    kept_a, sent_a, kept_b, sent_b = grad_parts(
        which[0].reshape(-1),
        features,
        f_sib,
        kv_cotangent,
        kv_sib,
        tile,
        width // tile,
        owners,
    )
    got_a = swap_along(sent_a, "dp", owners, 1 << orders[0][0])
    got_b = swap_along(sent_b, "dp", owners, 1 << orders[1][0])
    half = near // 2
    next_a = swap_along(kept_a[half:] + got_a[half:], "dp", owners, 1 << orders[0][1])
    next_b = swap_along(kept_b[half:] + got_b[half:], "dp", owners, 1 << orders[1][1])
    kept = jnp.stack([kept_a[:half] + got_a[:half], kept_b[:half] + got_b[:half]], axis=1)
    got = jnp.stack([next_a, next_b], axis=1)
    for bit in orders[0][2:]:
        half = kept.shape[0] // 2
        sent = kept[half:] + got[half:]
        kept = kept[:half] + got[:half]
        got = swap_along(sent, "dp", owners, 1 << bit)
    side = core.reshape(1).astype(jnp.int32)
    direction, grads = directions(
        side, kept[0], got[0], first_moment, second_moment, left_basis, right_basis
    )

    tiles = direction[None]
    for bit in orders[0][:1:-1]:
        other = swap_along(tiles, "dp", owners, 1 << bit)
        tiles = jnp.concatenate([tiles, other], axis=0)
    gathered = []
    for stream, order in enumerate(orders):
        mine = tiles[:, stream]
        other = swap_along(mine, "dp", owners, 1 << order[1])
        mine = jnp.concatenate([mine, other], axis=0)
        other = swap_along(mine, "dp", owners, 1 << order[0])
        gathered += [mine, other]
    from_sib = [swap_along(part, "inner", 2, 1) for part in gathered]

    left_iter, right_iter = refreshed(
        side, grads, left_stat, right_stat, left_basis, right_basis
    )
    left_sib = swap_along(left_iter, "inner", 2, 1)
    right_sib = swap_along(right_iter, "inner", 2, 1)

    update = placed(which.reshape(-1), live.reshape(-1), gathered + from_sib, d_win, width)

    here_live = jnp.any(
        (owner_of_block == here) & (slot == jnp.arange(capacity, dtype=jnp.int32)[:, None]), axis=1
    )
    keep = here_live[:, None, None]

    def merged(own, sib, basis):
        both = jnp.where(
            core == 0, jnp.concatenate([own, sib], axis=0), jnp.concatenate([sib, own], axis=0)
        )
        return jnp.where(keep, both, basis[0])[None]

    return (
        update,
        merged(left_iter, left_sib, left_basis),
        merged(right_iter, right_sib, right_basis),
    )


def solution(mesh):
    owners = mesh.shape["dp"]
    inner = mesh.shape["inner"]

    def per_device(*args):
        capacity = args[-1].shape[1]
        if inner == 2 and capacity == 4 and owners >= 4 and owners & (owners - 1) == 0:
            return per_device_dealt(owners, *args)
        return per_device_plain(*args)

    return jax.shard_map(
        per_device,
        mesh=mesh,
        in_specs=(
            P(("dp", "inner"), None),
            P(("dp", "inner"), None),
            P(),
            P("dp", None, None, None),
            P("dp", None, None, None),
            P("dp", None, None, None),
            P("dp", None, None, None),
            P("dp", None, None, None),
            P("dp", None, None, None),
        ),
        out_specs=(P(), P("dp", None, None, None), P("dp", None, None, None)),
        check_vma=False,
    )
```

```python
import functools

import jax
import jax.numpy as jnp
from jax import lax
from jax.experimental import pallas as pl
from jax.experimental.pallas import tpu as pltpu
from jax.sharding import PartitionSpec as P

NS_STEPS = 12


highest = lax.Precision.HIGHEST


def rotate_in(basis_left, matrix, basis_right):
    half = jnp.einsum("sji,sjk->sik", basis_left, matrix, precision=highest)
    return jnp.einsum("sij,sjk->sik", half, basis_right, precision=highest)


def rotate_out(basis_left, matrix, basis_right):
    half = jnp.einsum("sij,sjk->sik", basis_left, matrix, precision=highest)
    return jnp.einsum("sij,skj->sik", half, basis_right, precision=highest)


def orthogonalize(stat, basis):
    power = jnp.einsum("sij,sjk->sik", stat, basis, precision=highest)
    scale = jnp.sqrt(jnp.sum(power * power, axis=(1, 2), keepdims=True) + 1e-06)
    iterate = power / scale
    for sweep in range(NS_STEPS):
        gram = jnp.einsum("sji,sjk->sik", iterate, iterate, precision=highest)
        iterate = 1.5 * iterate - 0.5 * jnp.einsum("sij,sjk->sik", iterate, gram, precision=highest)
    return iterate


def soap_tiles(grads, first, second, stat_left, stat_right, basis_left, basis_right):
    rotated = rotate_in(basis_left, grads, basis_right)
    moment = 0.95 * first + 0.05 * grads
    moment_rot = rotate_in(basis_left, moment, basis_right)
    second_new = 0.95 * second + 0.05 * rotated * rotated
    direction = rotate_out(basis_left, moment_rot / (jnp.sqrt(second_new) + 1e-08), basis_right)
    left_new = 0.95 * stat_left + 0.05 * jnp.einsum("sij,skj->sik", grads, grads, precision=highest)
    right_new = 0.95 * stat_right + 0.05 * jnp.einsum(
        "sji,sjk->sik", grads, grads, precision=highest
    )
    return (direction, orthogonalize(left_new, basis_left), orthogonalize(right_new, basis_right))


def per_device_plain(
    features,
    kv_cotangent,
    owner_of_block,
    first_moment,
    second_moment,
    left_stat,
    right_stat,
    left_basis,
    right_basis,
):
    tile = left_basis.shape[-1]
    capacity = left_basis.shape[1]
    d_win = features.shape[1]
    width = kv_cotangent.shape[1]
    row_tiles = d_win // tile
    col_tiles = width // tile
    nblocks = owner_of_block.shape[0]
    owner_here = lax.axis_index("dp")
    block_ids = jnp.arange(nblocks, dtype=jnp.int32)
    same = owner_of_block[:, None] == owner_of_block[None, :]
    earlier = block_ids[None, :] < block_ids[:, None]
    slot = jnp.sum((same & earlier).astype(jnp.int32), axis=1)
    slot_ids = jnp.arange(capacity, dtype=jnp.int32)
    match = (owner_of_block[None, :] == owner_here) & (slot[None, :] == slot_ids[:, None])
    live = jnp.any(match, axis=1)
    which = jnp.sum(jnp.where(match, block_ids[None, :], 0), axis=1)
    row_start = which // col_tiles * tile
    col_start = which % col_tiles * tile
    partial_grad = lax.dot_general(
        features, kv_cotangent, (((0,), (0,)), ((), ())), preferred_element_type=jnp.float32
    )
    grad = lax.psum(partial_grad, ("dp", "inner"))
    fetched = [
        lax.dynamic_slice(grad, (row_start[slot_index], col_start[slot_index]), (tile, tile))
        for slot_index in range(capacity)
    ]
    grads = jnp.stack(fetched)
    basis_left = left_basis[0].astype(jnp.float32)
    basis_right = right_basis[0].astype(jnp.float32)
    direction, left_iter, right_iter = soap_tiles(
        grads,
        first_moment[0],
        second_moment[0],
        left_stat[0],
        right_stat[0],
        basis_left,
        basis_right,
    )
    direction_low = direction.astype(jnp.bfloat16)
    everyone = lax.all_gather(direction_low[None], "dp", axis=0, tiled=True)
    tiles = everyone[owner_of_block, slot]
    update = (
        tiles.reshape(row_tiles, col_tiles, tile, tile).transpose(0, 2, 1, 3).reshape(d_win, width)
    )
    keep = live[:, None, None]
    new_left = jnp.where(keep, left_iter.astype(jnp.bfloat16), left_basis[0])
    new_right = jnp.where(keep, right_iter.astype(jnp.bfloat16), right_basis[0])
    return (update, new_left[None], new_right[None])


MM = ((1,), (0,))
MT = ((1,), (1,))
TM = ((0,), (0,))


def swap_along(values, axis, size, bit):
    return lax.ppermute(values, axis, [(i, i ^ bit) for i in range(size)])


def dot(left, right, dims):
    return lax.dot_general(left, right, (dims, ((), ())), preferred_element_type=jnp.float32)


def halves(x):
    high = x.astype(jnp.bfloat16)
    return high, (x - high.astype(jnp.float32)).astype(jnp.bfloat16)


def beside(a, b):
    return jnp.concatenate([a, b], axis=1)


def above(a, b):
    return jnp.concatenate([a, b], axis=0)


def folded(both):
    n = both.shape[1] // 2
    return both[:, :n] + both[:, n:]


def pair_product(left, right, dims):
    if dims == TM:
        rows = above(*left)
    else:
        rows = beside(*left)
    if dims == MT:
        return folded(dot(rows, above(beside(right[0], right[0]), beside(right[1], right[1])), MT))
    return folded(dot(rows, above(beside(*right), beside(*right)), dims))


def low_times(low, x, dims):
    high, rest = halves(x)
    if dims == MT:
        return dot(beside(low, low), beside(high, rest), MT)
    return dot(beside(low, low), above(high, rest), MM)


def times_low(x, low):
    high, rest = halves(x)
    return dot(beside(high, rest), above(low, low), MM)


def stream_offsets(owners):
    bits = owners.bit_length() - 1
    orders = ([0, 1] + list(range(2, bits)), [1, 0] + list(range(2, bits)))
    offsets = [
        [sum(((p >> (bits - 1 - i)) & 1) << bit for i, bit in enumerate(order)) for p in range(owners)]
        for order in orders
    ]
    return orders, offsets


def tile_terms(block, col_tiles, kv_rows, f_ref):
    tile = kv_rows.shape[0] // col_tiles
    row = pl.multiple_of(block // col_tiles * tile, tile)
    col = pl.multiple_of(block % col_tiles * tile, tile)
    return dot(kv_rows[pl.ds(col, tile), :], f_ref[:, pl.ds(row, tile)], MM)


def first_kernel(owners, capacity, col_tiles, place_ref, owner_ref, f_ref, kv_ref, *rest):
    table_ref, sent_a, sent_b, kv_rows, count, held = rest
    nblocks = owner_ref.shape[0]
    for o in range(owners):
        count[o] = 0

    def enter(b, carry):
        o = owner_ref[b]
        s = count[o]
        count[o] = s + 1
        held[o * capacity + s] = b
        return carry

    lax.fori_loop(0, nblocks, enter, 0, unroll=8)
    here, core = place_ref[0], place_ref[1]
    offsets = stream_offsets(owners)[1]
    for side in range(2):
        first_slot = 2 * (core ^ side)
        for stream in range(2):
            for p in range(owners):
                entry = (side * 2 + stream) * owners + p
                table_ref[entry] = held[(here ^ offsets[stream][p]) * capacity + first_slot + stream]
    kv_rows[...] = kv_ref[...].T
    near = owners // 2
    for stream, out in enumerate((sent_a, sent_b)):

        def one(i, carry, stream=stream, out=out):
            block = table_ref[stream * owners + near + i]
            out[i] = tile_terms(block, col_tiles, kv_rows, f_ref)
            return carry

        lax.fori_loop(0, near, one, 0, unroll=4)


def second_kernel(owners, col_tiles, table_ref, f_ref, kv_ref, part_a, part_b, sent_a, sent_b, kv_rows):
    kv_rows[...] = kv_ref[...].T
    near = owners // 2
    for stream, (part, out) in enumerate(((part_a, sent_a), (part_b, sent_b))):

        def one(i, carry, stream=stream, part=part, out=out):
            block = table_ref[stream * owners + near + i]
            out[i] = part[i] + tile_terms(block, col_tiles, kv_rows, f_ref)
            return carry

        lax.fori_loop(0, near, one, 0, unroll=4)


def third_kernel(owners, col_tiles, table_ref, f_own, f_sib, kv_own, kv_sib, kept_a, kept_b, *rows):
    rows[0][...] = kv_own[...].T
    rows[1][...] = kv_sib[...].T
    near = owners // 2
    for stream, out in enumerate((kept_a, kept_b)):

        def one(i, carry, stream=stream, out=out):
            block = table_ref[stream * owners + i]
            out[i] = tile_terms(block, col_tiles, rows[0], f_own) + tile_terms(
                block, col_tiles, rows[1], f_sib
            )
            return carry

        lax.fori_loop(0, near, one, 0, unroll=4)


SMEM = pl.BlockSpec(memory_space=pltpu.SMEM)


def whole(shape):
    return pl.BlockSpec(shape, lambda *g: (0,) * len(shape))


def wholes(arrays):
    return [whole(a.shape) for a in arrays]


BIG = pltpu.CompilerParams(vmem_limit_bytes=40 * 2**20)


def rotated_kernel(side_ref, m_ref, v_ref, ql_ref, qr_ref, rot_ref, second_ref):
    for k in range(2):
        half = times_low(m_ref[0, k].T, ql_ref[0, k])
        rot_ref[k] = 0.95 * low_times(qr_ref[0, k].T, half, MM)
        second_ref[k] = 0.95 * v_ref[0, k].T


def direction_kernel(side_ref, a_ref, b_ref, m_ref, v_ref, ql_ref, qr_ref, dir_ref, grad_ref):
    for k in range(2):
        grad = a_ref[k] + b_ref[k]
        grad_ref[k] = grad
        left = ql_ref[0, k]
        right = qr_ref[0, k]
        rotated = low_times(right.T, times_low(grad, left), MM)
        moment_rot = m_ref[k] + 0.05 * rotated
        second = v_ref[k] + 0.05 * rotated * rotated
        scaled = moment_rot / (jnp.sqrt(second) + 1e-08)
        out = low_times(left, low_times(right, scaled, MM), MT)
        dir_ref[k] = out.astype(dir_ref.dtype)


def slots_of(*arrays):
    tile = arrays[0].shape[-1]
    return [pl.BlockSpec((1, 2, tile, tile), lambda i, s: (0, s[0], 0, 0)) for _ in arrays]


def on_slots(kernel, side, plain, slotted, outs, flops):
    return pl.pallas_call(
        kernel,
        out_shape=tuple(outs),
        grid_spec=pltpu.PrefetchScalarGridSpec(
            num_scalar_prefetch=1,
            grid=(1,),
            in_specs=wholes(plain) + slots_of(*slotted),
            out_specs=tuple(wholes(outs)),
        ),
        cost_estimate=pl.CostEstimate(flops=flops, bytes_accessed=800_000, transcendentals=0),
        name=kernel.__name__.removesuffix("_kernel"),
    )(side, *plain, *slotted)


def sweep(values):
    pairs = [halves(y) for y in values]
    grams = [halves(pair_product(p, p, MT)) for p in pairs]
    return tuple(
        1.5 * y - 0.5 * pair_product(g, p, MM) for y, g, p in zip(values, grams, pairs)
    )


def sweeps(values, count):
    return lax.fori_loop(0, count, lambda i, v: sweep(v), tuple(values), unroll=2)


def refresh_kernel(side_ref, g_ref, l_ref, r_ref, ql_ref, qr_ref, iter_ref):
    values = []
    for k in range(2):
        grad = halves(g_ref[k])
        for stat, basis, dims in ((l_ref, ql_ref, TM), (r_ref, qr_ref, MT)):
            new = 0.95 * stat[0, k] + 0.05 * pair_product(grad, grad, dims)
            power = times_low(new, basis[0, k])
            values.append((power / jnp.sqrt(jnp.sum(power * power) + 1e-06)).T)
    for i, y in enumerate(sweeps(values, NS_STEPS // 2)):
        iter_ref[i] = y


def finish_kernel(iter_ref, out_ref):
    values = [iter_ref[i] for i in range(4)]
    for i, y in enumerate(sweeps(values, NS_STEPS - NS_STEPS // 2)):
        out_ref[i] = y.T.astype(out_ref.dtype)


def bases_kernel(place_ref, own_ref, sib_ref, left_ref, right_ref):
    core = place_ref[1]
    for source, first in ((own_ref, 2 * core), (sib_ref, 2 - 2 * core)):
        for k in range(2):
            left_ref[0, first + k] = source[2 * k]
            right_ref[0, first + k] = source[2 * k + 1]


def place_kernel(col_tiles, table_ref, *refs):
    sources, out = refs[:-1], refs[-1]
    half, tile = sources[0].shape[:2]
    for number, source in enumerate(sources):
        for i in range(half):
            block = table_ref[number * half + i]
            row = pl.multiple_of(block // col_tiles * tile, tile)
            col = pl.multiple_of(block % col_tiles * tile, tile)
            out[pl.ds(row, tile), pl.ds(col, tile)] = source[i]


def per_device_dealt(
    owners,
    features,
    kv_cotangent,
    owner_of_block,
    first_moment,
    second_moment,
    left_stat,
    right_stat,
    left_basis,
    right_basis,
):
    tile = left_basis.shape[-1]
    capacity = left_basis.shape[1]
    rows, d_win = features.shape
    width = kv_cotangent.shape[1]
    col_tiles = width // tile
    here = lax.axis_index("dp")
    core = lax.axis_index("inner")
    place = jnp.stack([here, core]).astype(jnp.int32)
    side = core.reshape(1).astype(jnp.int32)
    orders = stream_offsets(owners)[0]
    near = owners // 2

    f_sib = swap_along(features, "inner", 2, 1)
    kv_sib = swap_along(kv_cotangent, "inner", 2, 1)
    flipped = pltpu.VMEM((width, rows), jnp.bfloat16)
    part = jax.ShapeDtypeStruct((near, tile, tile), jnp.float32)
    f32_pair = jax.ShapeDtypeStruct((2, tile, tile), jnp.float32)
    term_flops = 2 * near * 2 * tile * tile * rows

    table, part_a, part_b = pl.pallas_call(
        functools.partial(first_kernel, owners, capacity, col_tiles),
        out_shape=(jax.ShapeDtypeStruct((4 * owners,), jnp.int32), part, part),
        grid=(1,),
        in_specs=[SMEM, SMEM] + wholes((features, kv_cotangent)),
        out_specs=(SMEM, whole(part.shape), whole(part.shape)),
        scratch_shapes=[
            flipped,
            pltpu.SMEM((owners,), jnp.int32),
            pltpu.SMEM((owners * capacity,), jnp.int32),
        ],
        compiler_params=BIG,
        cost_estimate=pl.CostEstimate(
            flops=term_flops, bytes_accessed=2_500_000, transcendentals=0
        ),
        name="first",
    )(place, owner_of_block, features, kv_cotangent)
    sent_a, sent_b = pl.pallas_call(
        functools.partial(second_kernel, owners, col_tiles),
        out_shape=(part, part),
        grid=(1,),
        in_specs=[SMEM] + wholes((f_sib, kv_sib, part_a, part_b)),
        out_specs=(whole(part.shape), whole(part.shape)),
        scratch_shapes=[flipped],
        compiler_params=BIG,
        cost_estimate=pl.CostEstimate(
            flops=term_flops, bytes_accessed=3_500_000, transcendentals=0
        ),
        name="second",
    )(table, f_sib, kv_sib, part_a, part_b)
    got_a = swap_along(sent_a, "dp", owners, 1 << orders[0][0])
    got_b = swap_along(sent_b, "dp", owners, 1 << orders[1][0])
    kept_a, kept_b = pl.pallas_call(
        functools.partial(third_kernel, owners, col_tiles),
        out_shape=(part, part),
        grid=(1,),
        in_specs=[SMEM] + wholes((features, f_sib, kv_cotangent, kv_sib)),
        out_specs=(whole(part.shape), whole(part.shape)),
        scratch_shapes=[flipped, flipped],
        compiler_params=BIG,
        cost_estimate=pl.CostEstimate(
            flops=2 * term_flops, bytes_accessed=3_500_000, transcendentals=0
        ),
        name="third",
    )(table, features, f_sib, kv_cotangent, kv_sib)
    moment_rot, second = on_slots(
        rotated_kernel,
        side,
        (),
        (first_moment, second_moment, left_basis, right_basis),
        (f32_pair, f32_pair),
        8 * 2 * tile**3,
    )

    half = near // 2
    next_a = swap_along(kept_a[half:] + got_a[half:], "dp", owners, 1 << orders[0][1])
    next_b = swap_along(kept_b[half:] + got_b[half:], "dp", owners, 1 << orders[1][1])
    kept = jnp.stack([kept_a[:half] + got_a[:half], kept_b[:half] + got_b[:half]], axis=1)
    got = jnp.stack([next_a, next_b], axis=1)
    for bit in orders[0][2:]:
        half = kept.shape[0] // 2
        sent = kept[half:] + got[half:]
        kept = kept[:half] + got[:half]
        got = swap_along(sent, "dp", owners, 1 << bit)
    direction, grads = on_slots(
        direction_kernel,
        side,
        (kept[0], got[0], moment_rot, second),
        (left_basis, right_basis),
        (jax.ShapeDtypeStruct(f32_pair.shape, jnp.bfloat16), f32_pair),
        16 * 2 * tile**3,
    )

    bits = len(orders[0])
    high = owners // 4
    tiles = []
    for p in range(high):
        offset = sum(((p >> (bits - 3 - i)) & 1) << bit for i, bit in enumerate(orders[0][2:]))
        tiles.append(swap_along(direction, "dp", owners, offset) if offset else direction)
    iterates = on_slots(
        refresh_kernel,
        side,
        (grads,),
        (left_stat, right_stat, left_basis, right_basis),
        (jax.ShapeDtypeStruct((4, tile, tile), jnp.float32),),
        4 * 14 * 4 * 2 * tile**3,
    )[0]
    fresh = pl.pallas_call(
        finish_kernel,
        out_shape=jax.ShapeDtypeStruct(iterates.shape, jnp.bfloat16),
        cost_estimate=pl.CostEstimate(
            flops=4 * 12 * 4 * 2 * tile**3, bytes_accessed=400_000, transcendentals=0
        ),
        name="finish",
    )(iterates)
    fresh_sib = swap_along(fresh, "inner", 2, 1)
    basis = jax.ShapeDtypeStruct(left_basis.shape, left_basis.dtype)
    new_left, new_right = pl.pallas_call(
        bases_kernel,
        out_shape=(basis, basis),
        grid=(1,),
        in_specs=[SMEM] + wholes((fresh, fresh_sib)),
        out_specs=tuple(wholes((basis, basis))),
        cost_estimate=pl.CostEstimate(flops=0, bytes_accessed=600_000, transcendentals=0),
        name="bases",
    )(place, fresh, fresh_sib)

    gathered = []
    for stream, order in enumerate(orders):
        mine = jnp.stack([t[stream] for t in tiles])
        other = swap_along(mine, "dp", owners, 1 << order[1])
        mine = jnp.concatenate([mine, other], axis=0)
        other = swap_along(mine, "dp", owners, 1 << order[0])
        gathered += [mine, other]
    sources = gathered + [swap_along(g, "inner", 2, 1) for g in gathered]
    update = pl.pallas_call(
        functools.partial(place_kernel, col_tiles),
        out_shape=jax.ShapeDtypeStruct((d_win, width), jnp.bfloat16),
        grid=(1,),
        in_specs=[SMEM] + wholes(sources),
        out_specs=whole((d_win, width)),
        compiler_params=BIG,
        name="placed",
    )(table, *sources)
    return update, new_left, new_right


def solution(mesh):
    owners = mesh.shape["dp"]
    inner = mesh.shape["inner"]

    def per_device(*args):
        capacity = args[-1].shape[1]
        full = args[2].shape[0] == owners * capacity
        if full and inner == 2 and capacity == 4 and owners >= 8 and owners & (owners - 1) == 0:
            return per_device_dealt(owners, *args)
        return per_device_plain(*args)

    return jax.shard_map(
        per_device,
        mesh=mesh,
        in_specs=(
            P(("dp", "inner"), None),
            P(("dp", "inner"), None),
            P(),
            P("dp", None, None, None),
            P("dp", None, None, None),
            P("dp", None, None, None),
            P("dp", None, None, None),
            P("dp", None, None, None),
            P("dp", None, None, None),
        ),
        out_specs=(P(), P("dp", None, None, None), P("dp", None, None, None)),
        check_vma=False,
    )
```

```python
import functools

import jax
import jax.numpy as jnp
from jax import lax
from jax.experimental import pallas as pl
from jax.experimental.pallas import tpu as pltpu
from jax.sharding import PartitionSpec as P

NS_STEPS = 12


highest = lax.Precision.HIGHEST


def rotate_in(basis_left, matrix, basis_right):
    half = jnp.einsum("sji,sjk->sik", basis_left, matrix, precision=highest)
    return jnp.einsum("sij,sjk->sik", half, basis_right, precision=highest)


def rotate_out(basis_left, matrix, basis_right):
    half = jnp.einsum("sij,sjk->sik", basis_left, matrix, precision=highest)
    return jnp.einsum("sij,skj->sik", half, basis_right, precision=highest)


def orthogonalize(stat, basis):
    power = jnp.einsum("sij,sjk->sik", stat, basis, precision=highest)
    scale = jnp.sqrt(jnp.sum(power * power, axis=(1, 2), keepdims=True) + 1e-06)
    iterate = power / scale
    for sweep in range(NS_STEPS):
        gram = jnp.einsum("sji,sjk->sik", iterate, iterate, precision=highest)
        iterate = 1.5 * iterate - 0.5 * jnp.einsum("sij,sjk->sik", iterate, gram, precision=highest)
    return iterate


def soap_tiles(grads, first, second, stat_left, stat_right, basis_left, basis_right):
    rotated = rotate_in(basis_left, grads, basis_right)
    moment = 0.95 * first + 0.05 * grads
    moment_rot = rotate_in(basis_left, moment, basis_right)
    second_new = 0.95 * second + 0.05 * rotated * rotated
    direction = rotate_out(basis_left, moment_rot / (jnp.sqrt(second_new) + 1e-08), basis_right)
    left_new = 0.95 * stat_left + 0.05 * jnp.einsum("sij,skj->sik", grads, grads, precision=highest)
    right_new = 0.95 * stat_right + 0.05 * jnp.einsum(
        "sji,sjk->sik", grads, grads, precision=highest
    )
    return (direction, orthogonalize(left_new, basis_left), orthogonalize(right_new, basis_right))


def per_device_plain(
    features,
    kv_cotangent,
    owner_of_block,
    first_moment,
    second_moment,
    left_stat,
    right_stat,
    left_basis,
    right_basis,
):
    tile = left_basis.shape[-1]
    capacity = left_basis.shape[1]
    d_win = features.shape[1]
    width = kv_cotangent.shape[1]
    row_tiles = d_win // tile
    col_tiles = width // tile
    nblocks = owner_of_block.shape[0]
    owner_here = lax.axis_index("dp")
    block_ids = jnp.arange(nblocks, dtype=jnp.int32)
    same = owner_of_block[:, None] == owner_of_block[None, :]
    earlier = block_ids[None, :] < block_ids[:, None]
    slot = jnp.sum((same & earlier).astype(jnp.int32), axis=1)
    slot_ids = jnp.arange(capacity, dtype=jnp.int32)
    match = (owner_of_block[None, :] == owner_here) & (slot[None, :] == slot_ids[:, None])
    live = jnp.any(match, axis=1)
    which = jnp.sum(jnp.where(match, block_ids[None, :], 0), axis=1)
    row_start = which // col_tiles * tile
    col_start = which % col_tiles * tile
    partial_grad = lax.dot_general(
        features, kv_cotangent, (((0,), (0,)), ((), ())), preferred_element_type=jnp.float32
    )
    grad = lax.psum(partial_grad, ("dp", "inner"))
    fetched = [
        lax.dynamic_slice(grad, (row_start[slot_index], col_start[slot_index]), (tile, tile))
        for slot_index in range(capacity)
    ]
    grads = jnp.stack(fetched)
    basis_left = left_basis[0].astype(jnp.float32)
    basis_right = right_basis[0].astype(jnp.float32)
    direction, left_iter, right_iter = soap_tiles(
        grads,
        first_moment[0],
        second_moment[0],
        left_stat[0],
        right_stat[0],
        basis_left,
        basis_right,
    )
    direction_low = direction.astype(jnp.bfloat16)
    everyone = lax.all_gather(direction_low[None], "dp", axis=0, tiled=True)
    tiles = everyone[owner_of_block, slot]
    update = (
        tiles.reshape(row_tiles, col_tiles, tile, tile).transpose(0, 2, 1, 3).reshape(d_win, width)
    )
    keep = live[:, None, None]
    new_left = jnp.where(keep, left_iter.astype(jnp.bfloat16), left_basis[0])
    new_right = jnp.where(keep, right_iter.astype(jnp.bfloat16), right_basis[0])
    return (update, new_left[None], new_right[None])


MM = ((1,), (0,))
MT = ((1,), (1,))
TM = ((0,), (0,))


def swap_along(values, axis, size, bit):
    return lax.ppermute(values, axis, [(i, i ^ bit) for i in range(size)])


def dot(left, right, dims):
    return lax.dot_general(left, right, (dims, ((), ())), preferred_element_type=jnp.float32)


def halves(x):
    high = x.astype(jnp.bfloat16)
    return high, (x - high.astype(jnp.float32)).astype(jnp.bfloat16)


def beside(a, b):
    return jnp.concatenate([a, b], axis=1)


def above(a, b):
    return jnp.concatenate([a, b], axis=0)


def folded(both):
    n = both.shape[1] // 2
    return both[:, :n] + both[:, n:]


def pair_product(left, right, dims):
    if dims == TM:
        rows = above(*left)
    else:
        rows = beside(*left)
    if dims == MT:
        return folded(dot(rows, above(beside(right[0], right[0]), beside(right[1], right[1])), MT))
    return folded(dot(rows, above(beside(*right), beside(*right)), dims))


def low_times(low, x, dims):
    high, rest = halves(x)
    if dims == MT:
        return dot(beside(low, low), beside(high, rest), MT)
    return dot(beside(low, low), above(high, rest), MM)


def times_low(x, low):
    high, rest = halves(x)
    return dot(beside(high, rest), above(low, low), MM)


def stream_offsets(owners):
    bits = owners.bit_length() - 1
    orders = ([0, 1] + list(range(2, bits)), [1, 0] + list(range(2, bits)))
    offsets = [
        [sum(((p >> (bits - 1 - i)) & 1) << bit for i, bit in enumerate(order)) for p in range(owners)]
        for order in orders
    ]
    return orders, offsets


def tile_terms(block, col_tiles, kv_rows, f_ref):
    tile = kv_rows.shape[0] // col_tiles
    row = pl.multiple_of(block // col_tiles * tile, tile)
    col = pl.multiple_of(block % col_tiles * tile, tile)
    return dot(kv_rows[pl.ds(col, tile), :], f_ref[:, pl.ds(row, tile)], MM)


def chunked(source, target, sems, first, count):
    rows = source.shape[0] // count
    return [
        pltpu.make_async_copy(
            source.at[pl.ds(i * rows, rows)], target.at[pl.ds(i * rows, rows)], sems.at[first + i]
        )
        for i in range(count)
    ]


def table_kernel(owners, capacity, meta_ref, table_ref, count, held):
    for o in range(owners):
        count[o] = 0

    def enter(b, carry):
        o = meta_ref[2 + b]
        s = count[o]
        count[o] = s + 1
        held[o * capacity + s] = b
        return carry

    lax.fori_loop(0, owners * capacity, enter, 0, unroll=8)
    here, core = meta_ref[0], meta_ref[1]
    offsets = stream_offsets(owners)[1]
    for side in range(2):
        first_slot = 2 * (core ^ side)
        for stream in range(2):
            for p in range(owners):
                entry = (side * 2 + stream) * owners + p
                table_ref[entry] = held[(here ^ offsets[stream][p]) * capacity + first_slot + stream]


def tiles_kernel(owners, col_tiles, first, table_ref, f_own, f_sib, kv_own, kv_sib, *rest):
    out_a, out_b, own_rows, sib_rows = rest
    own_rows[...] = kv_own[...].T
    sib_rows[...] = kv_sib[...].T
    for stream, out in enumerate((out_a, out_b)):

        def one(i, carry, stream=stream, out=out):
            block = table_ref[stream * owners + first + i]
            out[i] = tile_terms(block, col_tiles, own_rows, f_own) + tile_terms(
                block, col_tiles, sib_rows, f_sib
            )
            return carry

        lax.fori_loop(0, owners // 2, one, 0, unroll=4)


SMEM = pl.BlockSpec(memory_space=pltpu.SMEM)
HBM = pl.BlockSpec(memory_space=pltpu.HBM)


def whole(shape):
    return pl.BlockSpec(shape, lambda *g: (0,) * len(shape))


def wholes(arrays):
    return [whole(a.shape) for a in arrays]


BIG = pltpu.CompilerParams(vmem_limit_bytes=40 * 2**20)


def rotated_kernel(side_ref, m_ref, v_ref, l_ref, r_ref, ql_ref, qr_ref, *outs):
    rot_ref, second_ref, power_ref = outs
    for k in range(2):
        left = ql_ref[0, k]
        right = qr_ref[0, k]
        half = times_low(m_ref[0, k].T, left)
        rot_ref[k] = 0.95 * low_times(right.T, half, MM)
        second_ref[k] = 0.95 * v_ref[0, k].T
        power_ref[2 * k] = 0.95 * times_low(l_ref[0, k], left)
        power_ref[2 * k + 1] = 0.95 * times_low(r_ref[0, k], right)


def direction_kernel(side_ref, a_ref, b_ref, m_ref, v_ref, ql_ref, qr_ref, dir_ref, grad_ref):
    pair = range(2)
    lefts = [ql_ref[0, k] for k in pair]
    rights = [qr_ref[0, k] for k in pair]
    turned = [right.T for right in rights]
    grads = [a_ref[k] + b_ref[k] for k in pair]
    rots = [times_low(grads[k], lefts[k]) for k in pair]
    rots = [low_times(turned[k], rots[k], MM) for k in pair]
    scaled = []
    for k in pair:
        moment_rot = m_ref[k] + 0.05 * rots[k]
        second = v_ref[k] + 0.05 * rots[k] * rots[k]
        scaled.append(moment_rot / (jnp.sqrt(second) + 1e-08))
    outs = [low_times(rights[k], scaled[k], MM) for k in pair]
    outs = [low_times(lefts[k], outs[k], MT) for k in pair]
    for k in pair:
        dir_ref[k] = outs[k].astype(dir_ref.dtype)
        grad_ref[k] = grads[k]


def slots_of(*arrays):
    tile = arrays[0].shape[-1]
    return [pl.BlockSpec((1, 2, tile, tile), lambda i, s: (0, s[0], 0, 0)) for _ in arrays]


def on_slots(kernel, side, plain, slotted, outs, flops):
    return pl.pallas_call(
        kernel,
        out_shape=tuple(outs),
        grid_spec=pltpu.PrefetchScalarGridSpec(
            num_scalar_prefetch=1,
            grid=(1,),
            in_specs=wholes(plain) + slots_of(*slotted),
            out_specs=tuple(wholes(outs)),
        ),
        cost_estimate=pl.CostEstimate(flops=flops, bytes_accessed=800_000, transcendentals=0),
        name=kernel.__name__.removesuffix("_kernel"),
    )(side, *plain, *slotted)


def sweep(values):
    pairs = [halves(y) for y in values]
    grams = [halves(pair_product(p, p, MT)) for p in pairs]
    return tuple(
        1.5 * y - 0.5 * pair_product(g, p, MM) for y, g, p in zip(values, grams, pairs)
    )


def sweeps(values, count):
    return lax.fori_loop(0, count, lambda i, v: sweep(v), tuple(values), unroll=2)


STAGES = (3, 4, NS_STEPS - 7)


def refresh_kernel(side_ref, g_ref, power_ref, ql_ref, qr_ref, iter_ref):
    values = []
    for k in range(2):
        turned = g_ref[k]
        grad = turned.T
        for i, rows, columns, basis in ((0, grad, turned, ql_ref), (1, turned, grad, qr_ref)):
            half = times_low(columns, basis[0, k])
            power = power_ref[2 * k + i] + 0.05 * pair_product(halves(rows), halves(half), MM)
            values.append((power / jnp.sqrt(jnp.sum(power * power) + 1e-06)).T)
    for i, y in enumerate(sweeps(values, STAGES[0])):
        iter_ref[i] = y


def middle_kernel(iter_ref, out_ref):
    for i, y in enumerate(sweeps([iter_ref[i] for i in range(4)], STAGES[1])):
        out_ref[i] = y


def finish_kernel(iter_ref, out_ref):
    for i, y in enumerate(sweeps([iter_ref[i] for i in range(4)], STAGES[2])):
        out_ref[i] = y.T.astype(out_ref.dtype)


def sweeping(kernel, values, dtype, count):
    tile = values.shape[-1]
    return pl.pallas_call(
        kernel,
        out_shape=jax.ShapeDtypeStruct(values.shape, dtype),
        cost_estimate=pl.CostEstimate(
            flops=4 * 2 * count * 4 * 2 * tile**3, bytes_accessed=400_000, transcendentals=0
        ),
        name=kernel.__name__.removesuffix("_kernel"),
    )(values)


def place_kernel(col_tiles, table_ref, place_ref, own_ref, sib_ref, *refs):
    sources = refs[:-5]
    out_hbm, left_ref, right_ref, out, sems = refs[-5:]
    half, tile = sources[0].shape[:2]
    for number, source in enumerate(sources):
        for i in range(half):
            block = table_ref[number * half + i]
            row = pl.multiple_of(block // col_tiles * tile, tile)
            col = pl.multiple_of(block % col_tiles * tile, tile)
            out[pl.ds(row, tile), pl.ds(col, tile)] = source[i]
    copies = chunked(out, out_hbm, sems, 0, 8)
    for copy in copies:
        copy.start()
    core = place_ref[1]
    for source, first in ((own_ref, 2 * core), (sib_ref, 2 - 2 * core)):
        for k in range(2):
            left_ref[0, first + k] = source[2 * k]
            right_ref[0, first + k] = source[2 * k + 1]
    for copy in copies:
        copy.wait()


def per_device_dealt(
    owners,
    features,
    kv_cotangent,
    owner_of_block,
    first_moment,
    second_moment,
    left_stat,
    right_stat,
    left_basis,
    right_basis,
):
    tile = left_basis.shape[-1]
    capacity = left_basis.shape[1]
    rows, d_win = features.shape
    width = kv_cotangent.shape[1]
    col_tiles = width // tile
    here = lax.axis_index("dp")
    core = lax.axis_index("inner")
    meta = jnp.concatenate([jnp.stack([here, core]).astype(jnp.int32), owner_of_block])
    side = core.reshape(1).astype(jnp.int32)
    orders = stream_offsets(owners)[0]
    near = owners // 2

    f_sib = swap_along(features, "inner", 2, 1)
    kv_sib = swap_along(kv_cotangent, "inner", 2, 1)
    flipped = pltpu.VMEM((width, rows), jnp.bfloat16)
    part = jax.ShapeDtypeStruct((near, tile, tile), jnp.float32)
    f32_pair = jax.ShapeDtypeStruct((2, tile, tile), jnp.float32)
    table = pl.pallas_call(
        functools.partial(table_kernel, owners, capacity),
        out_shape=jax.ShapeDtypeStruct((4 * owners,), jnp.int32),
        in_specs=[SMEM],
        out_specs=SMEM,
        scratch_shapes=[
            pltpu.SMEM((owners,), jnp.int32),
            pltpu.SMEM((owners * capacity,), jnp.int32),
        ],
        cost_estimate=pl.CostEstimate(flops=0, bytes_accessed=1_000_000, transcendentals=0),
        name="table",
    )(meta)

    def tiles_from(first):
        inputs = (features, f_sib, kv_cotangent, kv_sib)
        return pl.pallas_call(
            functools.partial(tiles_kernel, owners, col_tiles, first),
            out_shape=(part, part),
            grid=(1,),
            in_specs=[SMEM] + wholes(inputs),
            out_specs=(whole(part.shape), whole(part.shape)),
            scratch_shapes=[flipped, flipped],
            compiler_params=BIG,
            cost_estimate=pl.CostEstimate(
                flops=2 * owners * 2 * tile * tile * 2 * rows,
                bytes_accessed=3_500_000,
                transcendentals=0,
            ),
            name="tiles",
        )(table, *inputs)

    sent_a, sent_b = tiles_from(near)
    got_a = swap_along(sent_a, "dp", owners, 1 << orders[0][0])
    got_b = swap_along(sent_b, "dp", owners, 1 << orders[1][0])
    kept_a, kept_b = tiles_from(0)
    quad = jax.ShapeDtypeStruct((4, tile, tile), jnp.float32)
    moment_rot, second, power = on_slots(
        rotated_kernel,
        side,
        (),
        (first_moment, second_moment, left_stat, right_stat, left_basis, right_basis),
        (f32_pair, f32_pair, quad),
        16 * 2 * tile**3,
    )

    half = near // 2
    next_a = swap_along(kept_a[half:] + got_a[half:], "dp", owners, 1 << orders[0][1])
    next_b = swap_along(kept_b[half:] + got_b[half:], "dp", owners, 1 << orders[1][1])
    kept = jnp.stack([kept_a[:half] + got_a[:half], kept_b[:half] + got_b[:half]], axis=1)
    got = jnp.stack([next_a, next_b], axis=1)
    for bit in orders[0][2:]:
        half = kept.shape[0] // 2
        sent = kept[half:] + got[half:]
        kept = kept[:half] + got[:half]
        if half == 1:
            sent, kept = sent[0], kept[0]
        got = swap_along(sent, "dp", owners, 1 << bit)
    direction, grads = on_slots(
        direction_kernel,
        side,
        (kept, got, moment_rot, second),
        (left_basis, right_basis),
        (jax.ShapeDtypeStruct(f32_pair.shape, jnp.bfloat16), f32_pair),
        16 * 2 * tile**3,
    )

    bits = len(orders[0])
    high = owners // 4
    tiles = []
    for p in range(high):
        offset = sum(((p >> (bits - 3 - i)) & 1) << bit for i, bit in enumerate(orders[0][2:]))
        tiles.append(swap_along(direction, "dp", owners, offset) if offset else direction)
    values = on_slots(
        refresh_kernel,
        side,
        (grads, power),
        (left_basis, right_basis),
        (quad,),
        4 * (4 + 2 * STAGES[0]) * 4 * 2 * tile**3,
    )[0]
    mine = [jnp.stack([t[stream] for t in tiles]) for stream in range(2)]
    mine, values = lax.optimization_barrier((mine, values))
    other = [swap_along(m, "dp", owners, 1 << order[1]) for m, order in zip(mine, orders)]
    values = sweeping(middle_kernel, values, jnp.float32, STAGES[1])
    mine = [jnp.concatenate(both, axis=0) for both in zip(mine, other)]
    mine, values = lax.optimization_barrier((mine, values))
    other = [swap_along(m, "dp", owners, 1 << order[0]) for m, order in zip(mine, orders)]
    fresh = sweeping(finish_kernel, values, jnp.bfloat16, STAGES[2])
    other, fresh = lax.optimization_barrier((other, fresh))
    fresh_sib = swap_along(fresh, "inner", 2, 1)
    gathered = [part for both in zip(mine, other) for part in both]
    sources = gathered + [swap_along(g, "inner", 2, 1) for g in gathered]
    basis = jax.ShapeDtypeStruct(left_basis.shape, left_basis.dtype)
    return pl.pallas_call(
        functools.partial(place_kernel, col_tiles),
        out_shape=(jax.ShapeDtypeStruct((d_win, width), jnp.bfloat16), basis, basis),
        grid=(1,),
        in_specs=[SMEM, SMEM] + wholes([fresh, fresh_sib] + sources),
        out_specs=(HBM, whole(basis.shape), whole(basis.shape)),
        scratch_shapes=[
            pltpu.VMEM((d_win, width), jnp.bfloat16),
            pltpu.SemaphoreType.DMA((8,)),
        ],
        compiler_params=BIG,
        name="placed",
    )(table, meta, fresh, fresh_sib, *sources)


def solution(mesh):
    owners = mesh.shape["dp"]
    inner = mesh.shape["inner"]

    def per_device(*args):
        capacity = args[-1].shape[1]
        full = args[2].shape[0] == owners * capacity
        if full and inner == 2 and capacity == 4 and owners >= 8 and owners & (owners - 1) == 0:
            return per_device_dealt(owners, *args)
        return per_device_plain(*args)

    return jax.shard_map(
        per_device,
        mesh=mesh,
        in_specs=(
            P(("dp", "inner"), None),
            P(("dp", "inner"), None),
            P(),
            P("dp", None, None, None),
            P("dp", None, None, None),
            P("dp", None, None, None),
            P("dp", None, None, None),
            P("dp", None, None, None),
            P("dp", None, None, None),
        ),
        out_specs=(P(), P("dp", None, None, None), P("dp", None, None, None)),
        check_vma=False,
    )
```

```python
import functools

import jax
import jax.numpy as jnp
from jax import lax
from jax.experimental import pallas as pl
from jax.experimental.pallas import tpu as pltpu
from jax.sharding import PartitionSpec as P

NS_STEPS = 12


highest = lax.Precision.HIGHEST


def rotate_in(basis_left, matrix, basis_right):
    half = jnp.einsum("sji,sjk->sik", basis_left, matrix, precision=highest)
    return jnp.einsum("sij,sjk->sik", half, basis_right, precision=highest)


def rotate_out(basis_left, matrix, basis_right):
    half = jnp.einsum("sij,sjk->sik", basis_left, matrix, precision=highest)
    return jnp.einsum("sij,skj->sik", half, basis_right, precision=highest)


def orthogonalize(stat, basis):
    power = jnp.einsum("sij,sjk->sik", stat, basis, precision=highest)
    scale = jnp.sqrt(jnp.sum(power * power, axis=(1, 2), keepdims=True) + 1e-06)
    iterate = power / scale
    for sweep in range(NS_STEPS):
        gram = jnp.einsum("sji,sjk->sik", iterate, iterate, precision=highest)
        iterate = 1.5 * iterate - 0.5 * jnp.einsum("sij,sjk->sik", iterate, gram, precision=highest)
    return iterate


def soap_tiles(grads, first, second, stat_left, stat_right, basis_left, basis_right):
    rotated = rotate_in(basis_left, grads, basis_right)
    moment = 0.95 * first + 0.05 * grads
    moment_rot = rotate_in(basis_left, moment, basis_right)
    second_new = 0.95 * second + 0.05 * rotated * rotated
    direction = rotate_out(basis_left, moment_rot / (jnp.sqrt(second_new) + 1e-08), basis_right)
    left_new = 0.95 * stat_left + 0.05 * jnp.einsum("sij,skj->sik", grads, grads, precision=highest)
    right_new = 0.95 * stat_right + 0.05 * jnp.einsum(
        "sji,sjk->sik", grads, grads, precision=highest
    )
    return (direction, orthogonalize(left_new, basis_left), orthogonalize(right_new, basis_right))


def per_device_plain(
    features,
    kv_cotangent,
    owner_of_block,
    first_moment,
    second_moment,
    left_stat,
    right_stat,
    left_basis,
    right_basis,
):
    tile = left_basis.shape[-1]
    capacity = left_basis.shape[1]
    d_win = features.shape[1]
    width = kv_cotangent.shape[1]
    row_tiles = d_win // tile
    col_tiles = width // tile
    nblocks = owner_of_block.shape[0]
    owner_here = lax.axis_index("dp")
    block_ids = jnp.arange(nblocks, dtype=jnp.int32)
    same = owner_of_block[:, None] == owner_of_block[None, :]
    earlier = block_ids[None, :] < block_ids[:, None]
    slot = jnp.sum((same & earlier).astype(jnp.int32), axis=1)
    slot_ids = jnp.arange(capacity, dtype=jnp.int32)
    match = (owner_of_block[None, :] == owner_here) & (slot[None, :] == slot_ids[:, None])
    live = jnp.any(match, axis=1)
    which = jnp.sum(jnp.where(match, block_ids[None, :], 0), axis=1)
    row_start = which // col_tiles * tile
    col_start = which % col_tiles * tile
    partial_grad = lax.dot_general(
        features, kv_cotangent, (((0,), (0,)), ((), ())), preferred_element_type=jnp.float32
    )
    grad = lax.psum(partial_grad, ("dp", "inner"))
    fetched = [
        lax.dynamic_slice(grad, (row_start[slot_index], col_start[slot_index]), (tile, tile))
        for slot_index in range(capacity)
    ]
    grads = jnp.stack(fetched)
    basis_left = left_basis[0].astype(jnp.float32)
    basis_right = right_basis[0].astype(jnp.float32)
    direction, left_iter, right_iter = soap_tiles(
        grads,
        first_moment[0],
        second_moment[0],
        left_stat[0],
        right_stat[0],
        basis_left,
        basis_right,
    )
    direction_low = direction.astype(jnp.bfloat16)
    everyone = lax.all_gather(direction_low[None], "dp", axis=0, tiled=True)
    tiles = everyone[owner_of_block, slot]
    update = (
        tiles.reshape(row_tiles, col_tiles, tile, tile).transpose(0, 2, 1, 3).reshape(d_win, width)
    )
    keep = live[:, None, None]
    new_left = jnp.where(keep, left_iter.astype(jnp.bfloat16), left_basis[0])
    new_right = jnp.where(keep, right_iter.astype(jnp.bfloat16), right_basis[0])
    return (update, new_left[None], new_right[None])


MM = ((1,), (0,))
MT = ((1,), (1,))
TM = ((0,), (0,))


def swap_along(values, axis, size, bit):
    return lax.ppermute(values, axis, [(i, i ^ bit) for i in range(size)])


def dot(left, right, dims):
    return lax.dot_general(left, right, (dims, ((), ())), preferred_element_type=jnp.float32)


def halves(x):
    high = x.astype(jnp.bfloat16)
    return high, (x - high.astype(jnp.float32)).astype(jnp.bfloat16)


def beside(a, b):
    return jnp.concatenate([a, b], axis=1)


def above(a, b):
    return jnp.concatenate([a, b], axis=0)


def folded(both):
    n = both.shape[1] // 2
    return both[:, :n] + both[:, n:]


def pair_product(left, right, dims):
    if dims == TM:
        rows = above(*left)
    else:
        rows = beside(*left)
    if dims == MT:
        return folded(dot(rows, above(beside(right[0], right[0]), beside(right[1], right[1])), MT))
    return folded(dot(rows, above(beside(*right), beside(*right)), dims))


def low_times(low, x, dims):
    high, rest = halves(x)
    if dims == MT:
        return dot(beside(low, low), beside(high, rest), MT)
    return dot(beside(low, low), above(high, rest), MM)


def times_low(x, low):
    high, rest = halves(x)
    return dot(beside(high, rest), above(low, low), MM)


def stream_offsets(owners):
    bits = owners.bit_length() - 1
    orders = ([0, 1] + list(range(2, bits)), [1, 0] + list(range(2, bits)))
    offsets = [
        [sum(((p >> (bits - 1 - i)) & 1) << bit for i, bit in enumerate(order)) for p in range(owners)]
        for order in orders
    ]
    return orders, offsets


def chunked(source, target, sems, first, count):
    rows = source.shape[0] // count
    return [
        pltpu.make_async_copy(
            source.at[pl.ds(i * rows, rows)], target.at[pl.ds(i * rows, rows)], sems.at[first + i]
        )
        for i in range(count)
    ]


def table_kernel(owners, capacity, place_ref, owner_ref, kv_ref, *rest):
    table_ref, own_rows, count, held = rest
    own_rows[...] = kv_ref[...].T

    for o in range(owners):
        count[o] = 0

    def enter(b, carry):
        o = owner_ref[b]
        s = count[o]
        count[o] = s + 1
        held[o * capacity + s] = b
        return carry

    lax.fori_loop(0, owners * capacity, enter, 0, unroll=8)
    here, core = place_ref[0], place_ref[1]
    offsets = stream_offsets(owners)[1]
    for side in range(2):
        first_slot = 2 * (core ^ side)
        for stream in range(2):
            for p in range(owners):
                entry = (side * 2 + stream) * owners + p
                table_ref[entry] = held[(here ^ offsets[stream][p]) * capacity + first_slot + stream]


def tiles_kernel(owners, first, table_ref, f_own, f_sib, own_rows, kv_sib, *rest):
    out_a, out_b, sib_rows = rest
    tile = out_a.shape[-1]
    col_tiles = own_rows.shape[0] // tile
    sib_rows[...] = kv_sib[...].T
    for stream, out in enumerate((out_a, out_b)):

        def one(i, carry, stream=stream, out=out):
            block = table_ref[stream * owners + first + i]
            at = pl.ds(pl.multiple_of(block // col_tiles * tile, tile), tile)
            cots = pl.ds(pl.multiple_of(block % col_tiles * tile, tile), tile)
            out[i] = dot(own_rows[cots, :], f_own[:, at], MM) + dot(
                sib_rows[cots, :], f_sib[:, at], MM
            )
            return carry

        lax.fori_loop(0, owners // 2, one, 0, unroll=4)


SMEM = pl.BlockSpec(memory_space=pltpu.SMEM)
HBM = pl.BlockSpec(memory_space=pltpu.HBM)
VMEM = pl.BlockSpec(memory_space=pltpu.VMEM)


def whole(shape):
    return pl.BlockSpec(shape, lambda *g: (0,) * len(shape))


def wholes(arrays):
    return [whole(a.shape) for a in arrays]


BIG = pltpu.CompilerParams(vmem_limit_bytes=24 * 2**20)
SMALL = pltpu.CompilerParams(vmem_limit_bytes=12 * 2**20)


def rotated_kernel(side_ref, m_ref, v_ref, l_ref, r_ref, ql_ref, qr_ref, *outs):
    rot_ref, second_ref, power_ref = outs
    for k in range(2):
        left = ql_ref[0, k]
        right = qr_ref[0, k]
        half = times_low(m_ref[0, k].T, left)
        rot_ref[k] = 0.95 * low_times(right.T, half, MM)
        second_ref[k] = 0.95 * v_ref[0, k].T
        power_ref[2 * k] = 0.95 * times_low(l_ref[0, k], left)
        power_ref[2 * k + 1] = 0.95 * times_low(r_ref[0, k], right)


def direction_kernel(side_ref, a_ref, b_ref, m_ref, v_ref, ql_ref, qr_ref, dir_ref, grad_ref):
    pair = range(2)
    lefts = [ql_ref[0, k] for k in pair]
    rights = [qr_ref[0, k] for k in pair]
    turned = [right.T for right in rights]
    grads = [a_ref[k] + b_ref[k] for k in pair]
    rots = [times_low(grads[k], lefts[k]) for k in pair]
    rots = [low_times(turned[k], rots[k], MM) for k in pair]
    scaled = []
    for k in pair:
        moment_rot = m_ref[k] + 0.05 * rots[k]
        second = v_ref[k] + 0.05 * rots[k] * rots[k]
        scaled.append(moment_rot / (jnp.sqrt(second) + 1e-08))
    outs = [low_times(rights[k], scaled[k], MM) for k in pair]
    outs = [low_times(lefts[k], outs[k], MT) for k in pair]
    for k in pair:
        dir_ref[k] = outs[k].astype(dir_ref.dtype)
        grad_ref[k] = grads[k]


def slots_of(*arrays):
    tile = arrays[0].shape[-1]
    return [pl.BlockSpec((1, 2, tile, tile), lambda i, s: (0, s[0], 0, 0)) for _ in arrays]


def on_slots(kernel, side, plain, slotted, outs, flops):
    return pl.pallas_call(
        kernel,
        out_shape=tuple(outs),
        grid_spec=pltpu.PrefetchScalarGridSpec(
            num_scalar_prefetch=1,
            grid=(1,),
            in_specs=wholes(plain) + slots_of(*slotted),
            out_specs=tuple(wholes(outs)),
        ),
        compiler_params=SMALL,
        cost_estimate=pl.CostEstimate(flops=flops, bytes_accessed=800_000, transcendentals=0),
        name=kernel.__name__.removesuffix("_kernel"),
    )(side, *plain, *slotted)


def sweep(values):
    pairs = [halves(y) for y in values]
    grams = [halves(pair_product(p, p, MT)) for p in pairs]
    return tuple(
        1.5 * y - 0.5 * pair_product(g, p, MM) for y, g, p in zip(values, grams, pairs)
    )


def sweeps(values, count):
    return lax.fori_loop(0, count, lambda i, v: sweep(v), tuple(values), unroll=2)


STAGES = (3, 4, NS_STEPS - 7)


def refresh_kernel(side_ref, g_ref, power_ref, ql_ref, qr_ref, iter_ref):
    values = []
    for k in range(2):
        turned = g_ref[k]
        grad = turned.T
        for i, rows, columns, basis in ((0, grad, turned, ql_ref), (1, turned, grad, qr_ref)):
            half = times_low(columns, basis[0, k])
            power = power_ref[2 * k + i] + 0.05 * pair_product(halves(rows), halves(half), MM)
            values.append((power / jnp.sqrt(jnp.sum(power * power) + 1e-06)).T)
    for i, y in enumerate(sweeps(values, STAGES[0])):
        iter_ref[i] = y


def middle_kernel(iter_ref, out_ref):
    for i, y in enumerate(sweeps([iter_ref[i] for i in range(4)], STAGES[1])):
        out_ref[i] = y


def finish_kernel(iter_ref, out_ref):
    for i, y in enumerate(sweeps([iter_ref[i] for i in range(4)], STAGES[2])):
        out_ref[i] = y.T.astype(out_ref.dtype)


def sweeping(kernel, values, dtype, count):
    tile = values.shape[-1]
    return pl.pallas_call(
        kernel,
        out_shape=jax.ShapeDtypeStruct(values.shape, dtype),
        compiler_params=SMALL,
        cost_estimate=pl.CostEstimate(
            flops=4 * 2 * count * 4 * 2 * tile**3, bytes_accessed=400_000, transcendentals=0
        ),
        name=kernel.__name__.removesuffix("_kernel"),
    )(values)


def place_kernel(col_tiles, table_ref, place_ref, own_ref, sib_ref, *refs):
    sources = refs[:-5]
    out_hbm, left_ref, right_ref, out, sems = refs[-5:]
    half, tile = sources[0].shape[:2]
    for number, source in enumerate(sources):
        for i in range(half):
            block = table_ref[number * half + i]
            row = pl.multiple_of(block // col_tiles * tile, tile)
            col = pl.multiple_of(block % col_tiles * tile, tile)
            out[pl.ds(row, tile), pl.ds(col, tile)] = source[i]
    copies = chunked(out, out_hbm, sems, 0, 8)
    for copy in copies:
        copy.start()
    core = place_ref[1]
    for source, first in ((own_ref, 2 * core), (sib_ref, 2 - 2 * core)):
        for k in range(2):
            left_ref[0, first + k] = source[2 * k]
            right_ref[0, first + k] = source[2 * k + 1]
    for copy in copies:
        copy.wait()


def per_device_dealt(
    owners,
    features,
    kv_cotangent,
    owner_of_block,
    first_moment,
    second_moment,
    left_stat,
    right_stat,
    left_basis,
    right_basis,
):
    tile = left_basis.shape[-1]
    capacity = left_basis.shape[1]
    rows, d_win = features.shape
    width = kv_cotangent.shape[1]
    col_tiles = width // tile
    here = lax.axis_index("dp")
    core = lax.axis_index("inner")
    place = jnp.stack([here, core]).astype(jnp.int32)
    side = core.reshape(1).astype(jnp.int32)
    orders = stream_offsets(owners)[0]
    near = owners // 2

    f_sib = swap_along(features, "inner", 2, 1)
    kv_sib = swap_along(kv_cotangent, "inner", 2, 1)
    flipped = pltpu.VMEM((width, rows), jnp.bfloat16)
    part = jax.ShapeDtypeStruct((near, tile, tile), jnp.float32)
    f32_pair = jax.ShapeDtypeStruct((2, tile, tile), jnp.float32)
    table, own_rows = pl.pallas_call(
        functools.partial(table_kernel, owners, capacity),
        out_shape=(
            jax.ShapeDtypeStruct((4 * owners,), jnp.int32),
            jax.ShapeDtypeStruct((width, rows), jnp.bfloat16),
        ),
        in_specs=[SMEM, SMEM, VMEM],
        out_specs=(SMEM, VMEM),
        compiler_params=SMALL,
        scratch_shapes=[
            pltpu.SMEM((owners,), jnp.int32),
            pltpu.SMEM((owners * capacity,), jnp.int32),
        ],
        cost_estimate=pl.CostEstimate(flops=0, bytes_accessed=1_000_000, transcendentals=0),
        name="table",
    )(place, owner_of_block, kv_cotangent)

    def tiles_from(first):
        inputs = (features, f_sib, own_rows, kv_sib)
        return pl.pallas_call(
            functools.partial(tiles_kernel, owners, first),
            out_shape=(part, part),
            grid=(1,),
            in_specs=[SMEM] + wholes(inputs),
            out_specs=(whole(part.shape), whole(part.shape)),
            scratch_shapes=[flipped],
            compiler_params=BIG,
            cost_estimate=pl.CostEstimate(
                flops=2 * owners * 2 * tile * tile * 2 * rows,
                bytes_accessed=3_500_000,
                transcendentals=0,
            ),
            name="tiles",
        )(table, *inputs)

    sent_a, sent_b = tiles_from(near)
    got_a = swap_along(sent_a, "dp", owners, 1 << orders[0][0])
    got_b = swap_along(sent_b, "dp", owners, 1 << orders[1][0])
    kept_a, kept_b = tiles_from(0)
    quad = jax.ShapeDtypeStruct((4, tile, tile), jnp.float32)
    moment_rot, second, power = on_slots(
        rotated_kernel,
        side,
        (),
        (first_moment, second_moment, left_stat, right_stat, left_basis, right_basis),
        (f32_pair, f32_pair, quad),
        16 * 2 * tile**3,
    )

    half = near // 2
    next_a = swap_along(kept_a[half:] + got_a[half:], "dp", owners, 1 << orders[0][1])
    next_b = swap_along(kept_b[half:] + got_b[half:], "dp", owners, 1 << orders[1][1])
    kept = jnp.stack([kept_a[:half] + got_a[:half], kept_b[:half] + got_b[:half]], axis=1)
    got = jnp.stack([next_a, next_b], axis=1)
    for bit in orders[0][2:]:
        half = kept.shape[0] // 2
        sent = kept[half:] + got[half:]
        kept = kept[:half] + got[:half]
        if half == 1:
            sent, kept = sent[0], kept[0]
        got = swap_along(sent, "dp", owners, 1 << bit)
    direction, grads = on_slots(
        direction_kernel,
        side,
        (kept, got, moment_rot, second),
        (left_basis, right_basis),
        (jax.ShapeDtypeStruct(f32_pair.shape, jnp.bfloat16), f32_pair),
        16 * 2 * tile**3,
    )

    bits = len(orders[0])
    high = owners // 4
    tiles = []
    for p in range(high):
        offset = sum(((p >> (bits - 3 - i)) & 1) << bit for i, bit in enumerate(orders[0][2:]))
        tiles.append(swap_along(direction, "dp", owners, offset) if offset else direction)
    values = on_slots(
        refresh_kernel,
        side,
        (grads, power),
        (left_basis, right_basis),
        (quad,),
        4 * (4 + 2 * STAGES[0]) * 4 * 2 * tile**3,
    )[0]
    mine = [jnp.stack([t[stream] for t in tiles]) for stream in range(2)]
    mine, values = lax.optimization_barrier((mine, values))
    other = [swap_along(m, "dp", owners, 1 << order[1]) for m, order in zip(mine, orders)]
    values = sweeping(middle_kernel, values, jnp.float32, STAGES[1])
    mine = [jnp.concatenate(both, axis=0) for both in zip(mine, other)]
    mine, values = lax.optimization_barrier((mine, values))
    other = [swap_along(m, "dp", owners, 1 << order[0]) for m, order in zip(mine, orders)]
    fresh = sweeping(finish_kernel, values, jnp.bfloat16, STAGES[2])
    other, fresh = lax.optimization_barrier((other, fresh))
    fresh_sib = swap_along(fresh, "inner", 2, 1)
    gathered = [part for both in zip(mine, other) for part in both]
    sources = gathered + [swap_along(g, "inner", 2, 1) for g in gathered]
    basis = jax.ShapeDtypeStruct(left_basis.shape, left_basis.dtype)
    return pl.pallas_call(
        functools.partial(place_kernel, col_tiles),
        out_shape=(jax.ShapeDtypeStruct((d_win, width), jnp.bfloat16), basis, basis),
        grid=(1,),
        in_specs=[SMEM, SMEM] + wholes([fresh, fresh_sib] + sources),
        out_specs=(HBM, whole(basis.shape), whole(basis.shape)),
        scratch_shapes=[
            pltpu.VMEM((d_win, width), jnp.bfloat16),
            pltpu.SemaphoreType.DMA((8,)),
        ],
        compiler_params=BIG,
        name="placed",
    )(table, place, fresh, fresh_sib, *sources)


def solution(mesh):
    owners = mesh.shape["dp"]
    inner = mesh.shape["inner"]

    def per_device(*args):
        capacity = args[-1].shape[1]
        full = args[2].shape[0] == owners * capacity
        if full and inner == 2 and capacity == 4 and owners >= 8 and owners & (owners - 1) == 0:
            return per_device_dealt(owners, *args)
        return per_device_plain(*args)

    return jax.shard_map(
        per_device,
        mesh=mesh,
        in_specs=(
            P(("dp", "inner"), None),
            P(("dp", "inner"), None),
            P(),
            P("dp", None, None, None),
            P("dp", None, None, None),
            P("dp", None, None, None),
            P("dp", None, None, None),
            P("dp", None, None, None),
            P("dp", None, None, None),
        ),
        out_specs=(P(), P("dp", None, None, None), P("dp", None, None, None)),
        check_vma=False,
    )
```

```python
import functools

import jax
import jax.numpy as jnp
from jax import lax
from jax.experimental import pallas as pl
from jax.experimental.pallas import tpu as pltpu
from jax.sharding import PartitionSpec as P

NS_STEPS = 12


highest = lax.Precision.HIGHEST


def rotate_in(basis_left, matrix, basis_right):
    half = jnp.einsum("sji,sjk->sik", basis_left, matrix, precision=highest)
    return jnp.einsum("sij,sjk->sik", half, basis_right, precision=highest)


def rotate_out(basis_left, matrix, basis_right):
    half = jnp.einsum("sij,sjk->sik", basis_left, matrix, precision=highest)
    return jnp.einsum("sij,skj->sik", half, basis_right, precision=highest)


def orthogonalize(stat, basis):
    power = jnp.einsum("sij,sjk->sik", stat, basis, precision=highest)
    scale = jnp.sqrt(jnp.sum(power * power, axis=(1, 2), keepdims=True) + 1e-06)
    iterate = power / scale
    for sweep in range(NS_STEPS):
        gram = jnp.einsum("sji,sjk->sik", iterate, iterate, precision=highest)
        iterate = 1.5 * iterate - 0.5 * jnp.einsum("sij,sjk->sik", iterate, gram, precision=highest)
    return iterate


def soap_tiles(grads, first, second, stat_left, stat_right, basis_left, basis_right):
    rotated = rotate_in(basis_left, grads, basis_right)
    moment = 0.95 * first + 0.05 * grads
    moment_rot = rotate_in(basis_left, moment, basis_right)
    second_new = 0.95 * second + 0.05 * rotated * rotated
    direction = rotate_out(basis_left, moment_rot / (jnp.sqrt(second_new) + 1e-08), basis_right)
    left_new = 0.95 * stat_left + 0.05 * jnp.einsum("sij,skj->sik", grads, grads, precision=highest)
    right_new = 0.95 * stat_right + 0.05 * jnp.einsum(
        "sji,sjk->sik", grads, grads, precision=highest
    )
    return (direction, orthogonalize(left_new, basis_left), orthogonalize(right_new, basis_right))


def per_device_plain(
    features,
    kv_cotangent,
    owner_of_block,
    first_moment,
    second_moment,
    left_stat,
    right_stat,
    left_basis,
    right_basis,
):
    tile = left_basis.shape[-1]
    capacity = left_basis.shape[1]
    d_win = features.shape[1]
    width = kv_cotangent.shape[1]
    row_tiles = d_win // tile
    col_tiles = width // tile
    nblocks = owner_of_block.shape[0]
    owner_here = lax.axis_index("dp")
    block_ids = jnp.arange(nblocks, dtype=jnp.int32)
    same = owner_of_block[:, None] == owner_of_block[None, :]
    earlier = block_ids[None, :] < block_ids[:, None]
    slot = jnp.sum((same & earlier).astype(jnp.int32), axis=1)
    slot_ids = jnp.arange(capacity, dtype=jnp.int32)
    match = (owner_of_block[None, :] == owner_here) & (slot[None, :] == slot_ids[:, None])
    live = jnp.any(match, axis=1)
    which = jnp.sum(jnp.where(match, block_ids[None, :], 0), axis=1)
    row_start = which // col_tiles * tile
    col_start = which % col_tiles * tile
    partial_grad = lax.dot_general(
        features, kv_cotangent, (((0,), (0,)), ((), ())), preferred_element_type=jnp.float32
    )
    grad = lax.psum(partial_grad, ("dp", "inner"))
    fetched = [
        lax.dynamic_slice(grad, (row_start[slot_index], col_start[slot_index]), (tile, tile))
        for slot_index in range(capacity)
    ]
    grads = jnp.stack(fetched)
    basis_left = left_basis[0].astype(jnp.float32)
    basis_right = right_basis[0].astype(jnp.float32)
    direction, left_iter, right_iter = soap_tiles(
        grads,
        first_moment[0],
        second_moment[0],
        left_stat[0],
        right_stat[0],
        basis_left,
        basis_right,
    )
    direction_low = direction.astype(jnp.bfloat16)
    everyone = lax.all_gather(direction_low[None], "dp", axis=0, tiled=True)
    tiles = everyone[owner_of_block, slot]
    update = (
        tiles.reshape(row_tiles, col_tiles, tile, tile).transpose(0, 2, 1, 3).reshape(d_win, width)
    )
    keep = live[:, None, None]
    new_left = jnp.where(keep, left_iter.astype(jnp.bfloat16), left_basis[0])
    new_right = jnp.where(keep, right_iter.astype(jnp.bfloat16), right_basis[0])
    return (update, new_left[None], new_right[None])


MM = ((1,), (0,))
MT = ((1,), (1,))
TM = ((0,), (0,))


BOTH = ("dp", "inner")


def swap_cores(values):
    return lax.ppermute(values, "inner", [(0, 1), (1, 0)])


def swap_owners(values, owners, flips):
    pairs = [(2 * o + c, 2 * (o ^ flips[c]) + c) for o in range(owners) for c in range(2)]
    return lax.ppermute(values, BOTH, pairs)


def dot(left, right, dims):
    return lax.dot_general(left, right, (dims, ((), ())), preferred_element_type=jnp.float32)


def halves(x):
    high = x.astype(jnp.bfloat16)
    return high, (x - high.astype(jnp.float32)).astype(jnp.bfloat16)


def beside(a, b):
    return jnp.concatenate([a, b], axis=1)


def above(a, b):
    return jnp.concatenate([a, b], axis=0)


def folded(both):
    n = both.shape[1] // 2
    return both[:, :n] + both[:, n:]


def pair_product(left, right, dims):
    if dims == TM:
        rows = above(*left)
    else:
        rows = beside(*left)
    if dims == MT:
        return folded(dot(rows, above(beside(right[0], right[0]), beside(right[1], right[1])), MT))
    return folded(dot(rows, above(beside(*right), beside(*right)), dims))


def low_times(low, x, dims):
    high, rest = halves(x)
    if dims == MT:
        return dot(beside(low, low), beside(high, rest), MT)
    return dot(beside(low, low), above(high, rest), MM)


def times_low(x, low):
    high, rest = halves(x)
    return dot(beside(high, rest), above(low, low), MM)


def core_orders(owners):
    bits = owners.bit_length() - 1
    orders = ([0, 1] + list(range(2, bits)), [1, 0] + list(range(2, bits)))
    offsets = [
        [sum(((p >> (bits - 1 - i)) & 1) << bit for i, bit in enumerate(order)) for p in range(owners)]
        for order in orders
    ]
    return orders, offsets


def chunked(source, target, sems, first, count):
    rows = source.shape[0] // count
    return [
        pltpu.make_async_copy(
            source.at[pl.ds(i * rows, rows)], target.at[pl.ds(i * rows, rows)], sems.at[first + i]
        )
        for i in range(count)
    ]


def table_kernel(owners, capacity, place_ref, owner_ref, kv_ref, *rest):
    table_ref, own_rows, count, held = rest
    own_rows[...] = kv_ref[...].T

    for o in range(owners):
        count[o] = 0

    def enter(b, carry):
        o = owner_ref[b]
        s = count[o]
        count[o] = s + 1
        held[o * capacity + s] = b
        return carry

    lax.fori_loop(0, owners * capacity, enter, 0, unroll=8)
    here, core = place_ref[0], place_ref[1]
    offsets = core_orders(owners)[1]
    for side in range(2):
        at = core ^ side
        for p in range(owners):
            offset = offsets[0][p] + at * (offsets[1][p] - offsets[0][p])
            first = (here ^ offset) * capacity + 2 * at
            for k in range(2):
                table_ref[(side * owners + p) * 2 + k] = held[first + k]


def tiles_kernel(first, table_ref, f_own, f_sib, own_rows, kv_sib, out_ref, sib_rows):
    tile = out_ref.shape[-1]
    col_tiles = own_rows.shape[0] // tile
    sib_rows[...] = kv_sib[...].T

    def one(i, carry):
        block = table_ref[first + i]
        at = pl.ds(pl.multiple_of(block // col_tiles * tile, tile), tile)
        cots = pl.ds(pl.multiple_of(block % col_tiles * tile, tile), tile)
        out_ref[i] = dot(own_rows[cots, :], f_own[:, at], MM) + dot(
            sib_rows[cots, :], f_sib[:, at], MM
        )
        return carry

    lax.fori_loop(0, out_ref.shape[0], one, 0, unroll=8)


SMEM = pl.BlockSpec(memory_space=pltpu.SMEM)
HBM = pl.BlockSpec(memory_space=pltpu.HBM)
VMEM = pl.BlockSpec(memory_space=pltpu.VMEM)


def whole(shape):
    return pl.BlockSpec(shape, lambda *g: (0,) * len(shape))


def wholes(arrays):
    return [whole(a.shape) for a in arrays]


BIG = pltpu.CompilerParams(vmem_limit_bytes=24 * 2**20)
SMALL = pltpu.CompilerParams(vmem_limit_bytes=12 * 2**20)


def rotated_kernel(side_ref, m_ref, v_ref, l_ref, r_ref, ql_ref, qr_ref, *outs):
    rot_ref, second_ref, power_ref = outs
    for k in range(2):
        left = ql_ref[0, k]
        right = qr_ref[0, k]
        half = times_low(m_ref[0, k].T, left)
        rot_ref[k] = 0.95 * low_times(right.T, half, MM)
        second_ref[k] = 0.95 * v_ref[0, k].T
        power_ref[2 * k] = 0.95 * times_low(l_ref[0, k], left)
        power_ref[2 * k + 1] = 0.95 * times_low(r_ref[0, k], right)


def direction_kernel(side_ref, a_ref, b_ref, m_ref, v_ref, ql_ref, qr_ref, dir_ref, grad_ref):
    pair = range(2)
    lefts = [ql_ref[0, k] for k in pair]
    rights = [qr_ref[0, k] for k in pair]
    turned = [right.T for right in rights]
    grads = [a_ref[k] + b_ref[k] for k in pair]
    rots = [times_low(grads[k], lefts[k]) for k in pair]
    rots = [low_times(turned[k], rots[k], MM) for k in pair]
    scaled = []
    for k in pair:
        moment_rot = m_ref[k] + 0.05 * rots[k]
        second = v_ref[k] + 0.05 * rots[k] * rots[k]
        scaled.append(moment_rot / (jnp.sqrt(second) + 1e-08))
    outs = [low_times(rights[k], scaled[k], MM) for k in pair]
    outs = [low_times(lefts[k], outs[k], MT) for k in pair]
    for k in pair:
        dir_ref[k] = outs[k].astype(dir_ref.dtype)
        grad_ref[k] = grads[k]


def slots_of(*arrays):
    tile = arrays[0].shape[-1]
    return [pl.BlockSpec((1, 2, tile, tile), lambda i, s: (0, s[0], 0, 0)) for _ in arrays]


def on_slots(kernel, side, plain, slotted, outs, flops):
    return pl.pallas_call(
        kernel,
        out_shape=tuple(outs),
        grid_spec=pltpu.PrefetchScalarGridSpec(
            num_scalar_prefetch=1,
            grid=(1,),
            in_specs=wholes(plain) + slots_of(*slotted),
            out_specs=tuple(wholes(outs)),
        ),
        compiler_params=SMALL,
        cost_estimate=pl.CostEstimate(flops=flops, bytes_accessed=800_000, transcendentals=0),
        name=kernel.__name__.removesuffix("_kernel"),
    )(side, *plain, *slotted)


def sweep(values):
    pairs = [halves(y) for y in values]
    grams = [halves(pair_product(p, p, MT)) for p in pairs]
    return tuple(
        1.5 * y - 0.5 * pair_product(g, p, MM) for y, g, p in zip(values, grams, pairs)
    )


def sweeps(values, count):
    return lax.fori_loop(0, count, lambda i, v: sweep(v), tuple(values), unroll=2)


STAGES = (3, 4, NS_STEPS - 7)


def refresh_kernel(side_ref, g_ref, power_ref, ql_ref, qr_ref, iter_ref):
    values = []
    for k in range(2):
        turned = g_ref[k]
        grad = turned.T
        for i, rows, columns, basis in ((0, grad, turned, ql_ref), (1, turned, grad, qr_ref)):
            half = times_low(columns, basis[0, k])
            power = power_ref[2 * k + i] + 0.05 * pair_product(halves(rows), halves(half), MM)
            values.append((power / jnp.sqrt(jnp.sum(power * power) + 1e-06)).T)
    for i, y in enumerate(sweeps(values, STAGES[0])):
        iter_ref[i] = y


def middle_kernel(iter_ref, out_ref):
    for i, y in enumerate(sweeps([iter_ref[i] for i in range(4)], STAGES[1])):
        out_ref[i] = y


def finish_kernel(iter_ref, out_ref):
    for i, y in enumerate(sweeps([iter_ref[i] for i in range(4)], STAGES[2])):
        out_ref[i] = y.T.astype(out_ref.dtype)


def sweeping(kernel, values, dtype, count):
    tile = values.shape[-1]
    return pl.pallas_call(
        kernel,
        out_shape=jax.ShapeDtypeStruct(values.shape, dtype),
        compiler_params=SMALL,
        cost_estimate=pl.CostEstimate(
            flops=4 * 2 * count * 4 * 2 * tile**3, bytes_accessed=400_000, transcendentals=0
        ),
        name=kernel.__name__.removesuffix("_kernel"),
    )(values)


def place_kernel(col_tiles, table_ref, place_ref, own_ref, sib_ref, *refs):
    sources = refs[:-5]
    out_hbm, left_ref, right_ref, out, sems = refs[-5:]
    half, tile = sources[0].shape[:2]
    for number, source in enumerate(sources):
        for i in range(half):
            block = table_ref[number * half + i]
            row = pl.multiple_of(block // col_tiles * tile, tile)
            col = pl.multiple_of(block % col_tiles * tile, tile)
            out[pl.ds(row, tile), pl.ds(col, tile)] = source[i]
    copies = chunked(out, out_hbm, sems, 0, 8)
    for copy in copies:
        copy.start()
    core = place_ref[1]
    for source, first in ((own_ref, 2 * core), (sib_ref, 2 - 2 * core)):
        for k in range(2):
            left_ref[0, first + k] = source[2 * k]
            right_ref[0, first + k] = source[2 * k + 1]
    for copy in copies:
        copy.wait()


def per_device_dealt(
    owners,
    features,
    kv_cotangent,
    owner_of_block,
    first_moment,
    second_moment,
    left_stat,
    right_stat,
    left_basis,
    right_basis,
):
    tile = left_basis.shape[-1]
    capacity = left_basis.shape[1]
    rows, d_win = features.shape
    width = kv_cotangent.shape[1]
    col_tiles = width // tile
    here = lax.axis_index("dp")
    core = lax.axis_index("inner")
    place = jnp.stack([here, core]).astype(jnp.int32)
    side = core.reshape(1).astype(jnp.int32)
    orders = core_orders(owners)[0]
    bits = len(orders[0])

    f_sib = swap_cores(features)
    kv_sib = swap_cores(kv_cotangent)
    flipped = pltpu.VMEM((width, rows), jnp.bfloat16)
    part = jax.ShapeDtypeStruct((owners, tile, tile), jnp.float32)
    f32_pair = jax.ShapeDtypeStruct((2, tile, tile), jnp.float32)
    table, own_rows = pl.pallas_call(
        functools.partial(table_kernel, owners, capacity),
        out_shape=(
            jax.ShapeDtypeStruct((4 * owners,), jnp.int32),
            jax.ShapeDtypeStruct((width, rows), jnp.bfloat16),
        ),
        in_specs=[SMEM, SMEM, VMEM],
        out_specs=(SMEM, VMEM),
        compiler_params=SMALL,
        scratch_shapes=[
            pltpu.SMEM((owners,), jnp.int32),
            pltpu.SMEM((owners * capacity,), jnp.int32),
        ],
        cost_estimate=pl.CostEstimate(flops=0, bytes_accessed=1_000_000, transcendentals=0),
        name="table",
    )(place, owner_of_block, kv_cotangent)

    def tiles_from(first):
        inputs = (features, f_sib, own_rows, kv_sib)
        return pl.pallas_call(
            functools.partial(tiles_kernel, first),
            out_shape=part,
            grid=(1,),
            in_specs=[SMEM] + wholes(inputs),
            out_specs=whole(part.shape),
            scratch_shapes=[flipped],
            compiler_params=BIG,
            cost_estimate=pl.CostEstimate(
                flops=2 * owners * 2 * tile * tile * 2 * rows,
                bytes_accessed=3_500_000,
                transcendentals=0,
            ),
            name="tiles",
        )(table, *inputs)

    def exchanged(values, step):
        return swap_owners(values, owners, [1 << order[step] for order in orders])

    got = exchanged(tiles_from(owners), 0)
    kept = tiles_from(0)
    quad = jax.ShapeDtypeStruct((4, tile, tile), jnp.float32)
    moment_rot, second, power = on_slots(
        rotated_kernel,
        side,
        (),
        (first_moment, second_moment, left_stat, right_stat, left_basis, right_basis),
        (f32_pair, f32_pair, quad),
        16 * 2 * tile**3,
    )

    for step in range(1, bits):
        half = kept.shape[0] // 2
        sent = kept[half:] + got[half:]
        kept = kept[:half] + got[:half]
        got = exchanged(sent, step)
    direction, grads = on_slots(
        direction_kernel,
        side,
        (kept, got, moment_rot, second),
        (left_basis, right_basis),
        (jax.ShapeDtypeStruct(f32_pair.shape, jnp.bfloat16), f32_pair),
        16 * 2 * tile**3,
    )

    mine = []
    for p in range(owners // 4):
        offset = core_orders(owners)[1][0][p]
        mine.append(swap_owners(direction, owners, (offset, offset)) if p else direction)
    values = on_slots(
        refresh_kernel,
        side,
        (grads, power),
        (left_basis, right_basis),
        (quad,),
        4 * (4 + 2 * STAGES[0]) * 4 * 2 * tile**3,
    )[0]
    mine = jnp.concatenate(mine, axis=0)
    mine, values = lax.optimization_barrier((mine, values))
    other = exchanged(mine, 1)
    values = sweeping(middle_kernel, values, jnp.float32, STAGES[1])
    mine = jnp.concatenate([mine, other], axis=0)
    mine, values = lax.optimization_barrier((mine, values))
    other = exchanged(mine, 0)
    fresh = sweeping(finish_kernel, values, jnp.bfloat16, STAGES[2])
    other, fresh = lax.optimization_barrier((other, fresh))
    fresh_sib = swap_cores(fresh)
    sources = [mine, other, swap_cores(mine), swap_cores(other)]
    basis = jax.ShapeDtypeStruct(left_basis.shape, left_basis.dtype)
    return pl.pallas_call(
        functools.partial(place_kernel, col_tiles),
        out_shape=(jax.ShapeDtypeStruct((d_win, width), jnp.bfloat16), basis, basis),
        grid=(1,),
        in_specs=[SMEM, SMEM] + wholes([fresh, fresh_sib] + sources),
        out_specs=(HBM, whole(basis.shape), whole(basis.shape)),
        scratch_shapes=[
            pltpu.VMEM((d_win, width), jnp.bfloat16),
            pltpu.SemaphoreType.DMA((8,)),
        ],
        compiler_params=BIG,
        name="placed",
    )(table, place, fresh, fresh_sib, *sources)


def solution(mesh):
    owners = mesh.shape["dp"]
    inner = mesh.shape["inner"]

    def per_device(*args):
        capacity = args[-1].shape[1]
        full = args[2].shape[0] == owners * capacity
        if full and inner == 2 and capacity == 4 and owners >= 8 and owners & (owners - 1) == 0:
            return per_device_dealt(owners, *args)
        return per_device_plain(*args)

    return jax.shard_map(
        per_device,
        mesh=mesh,
        in_specs=(
            P(("dp", "inner"), None),
            P(("dp", "inner"), None),
            P(),
            P("dp", None, None, None),
            P("dp", None, None, None),
            P("dp", None, None, None),
            P("dp", None, None, None),
            P("dp", None, None, None),
            P("dp", None, None, None),
        ),
        out_specs=(P(), P("dp", None, None, None), P("dp", None, None, None)),
        check_vma=False,
    )
```

```python
import functools

import jax
import jax.numpy as jnp
from jax import lax
from jax.experimental import pallas as pl
from jax.experimental.pallas import tpu as pltpu
from jax.sharding import PartitionSpec as P

NS_STEPS = 12


highest = lax.Precision.HIGHEST


def rotate_in(basis_left, matrix, basis_right):
    half = jnp.einsum("sji,sjk->sik", basis_left, matrix, precision=highest)
    return jnp.einsum("sij,sjk->sik", half, basis_right, precision=highest)


def rotate_out(basis_left, matrix, basis_right):
    half = jnp.einsum("sij,sjk->sik", basis_left, matrix, precision=highest)
    return jnp.einsum("sij,skj->sik", half, basis_right, precision=highest)


def orthogonalize(stat, basis):
    power = jnp.einsum("sij,sjk->sik", stat, basis, precision=highest)
    scale = jnp.sqrt(jnp.sum(power * power, axis=(1, 2), keepdims=True) + 1e-06)
    iterate = power / scale
    for sweep in range(NS_STEPS):
        gram = jnp.einsum("sji,sjk->sik", iterate, iterate, precision=highest)
        iterate = 1.5 * iterate - 0.5 * jnp.einsum("sij,sjk->sik", iterate, gram, precision=highest)
    return iterate


def soap_tiles(grads, first, second, stat_left, stat_right, basis_left, basis_right):
    rotated = rotate_in(basis_left, grads, basis_right)
    moment = 0.95 * first + 0.05 * grads
    moment_rot = rotate_in(basis_left, moment, basis_right)
    second_new = 0.95 * second + 0.05 * rotated * rotated
    direction = rotate_out(basis_left, moment_rot / (jnp.sqrt(second_new) + 1e-08), basis_right)
    left_new = 0.95 * stat_left + 0.05 * jnp.einsum("sij,skj->sik", grads, grads, precision=highest)
    right_new = 0.95 * stat_right + 0.05 * jnp.einsum(
        "sji,sjk->sik", grads, grads, precision=highest
    )
    return (direction, orthogonalize(left_new, basis_left), orthogonalize(right_new, basis_right))


def per_device_plain(
    features,
    kv_cotangent,
    owner_of_block,
    first_moment,
    second_moment,
    left_stat,
    right_stat,
    left_basis,
    right_basis,
):
    tile = left_basis.shape[-1]
    capacity = left_basis.shape[1]
    d_win = features.shape[1]
    width = kv_cotangent.shape[1]
    row_tiles = d_win // tile
    col_tiles = width // tile
    nblocks = owner_of_block.shape[0]
    owner_here = lax.axis_index("dp")
    block_ids = jnp.arange(nblocks, dtype=jnp.int32)
    same = owner_of_block[:, None] == owner_of_block[None, :]
    earlier = block_ids[None, :] < block_ids[:, None]
    slot = jnp.sum((same & earlier).astype(jnp.int32), axis=1)
    slot_ids = jnp.arange(capacity, dtype=jnp.int32)
    match = (owner_of_block[None, :] == owner_here) & (slot[None, :] == slot_ids[:, None])
    live = jnp.any(match, axis=1)
    which = jnp.sum(jnp.where(match, block_ids[None, :], 0), axis=1)
    row_start = which // col_tiles * tile
    col_start = which % col_tiles * tile
    partial_grad = lax.dot_general(
        features, kv_cotangent, (((0,), (0,)), ((), ())), preferred_element_type=jnp.float32
    )
    grad = lax.psum(partial_grad, ("dp", "inner"))
    fetched = [
        lax.dynamic_slice(grad, (row_start[slot_index], col_start[slot_index]), (tile, tile))
        for slot_index in range(capacity)
    ]
    grads = jnp.stack(fetched)
    basis_left = left_basis[0].astype(jnp.float32)
    basis_right = right_basis[0].astype(jnp.float32)
    direction, left_iter, right_iter = soap_tiles(
        grads,
        first_moment[0],
        second_moment[0],
        left_stat[0],
        right_stat[0],
        basis_left,
        basis_right,
    )
    direction_low = direction.astype(jnp.bfloat16)
    everyone = lax.all_gather(direction_low[None], "dp", axis=0, tiled=True)
    tiles = everyone[owner_of_block, slot]
    update = (
        tiles.reshape(row_tiles, col_tiles, tile, tile).transpose(0, 2, 1, 3).reshape(d_win, width)
    )
    keep = live[:, None, None]
    new_left = jnp.where(keep, left_iter.astype(jnp.bfloat16), left_basis[0])
    new_right = jnp.where(keep, right_iter.astype(jnp.bfloat16), right_basis[0])
    return (update, new_left[None], new_right[None])


MM = ((1,), (0,))
MT = ((1,), (1,))
TM = ((0,), (0,))


def swap_along(values, axis, size, bit):
    return lax.ppermute(values, axis, [(i, i ^ bit) for i in range(size)])


def dot(left, right, dims):
    return lax.dot_general(left, right, (dims, ((), ())), preferred_element_type=jnp.float32)


def halves(x):
    high = x.astype(jnp.bfloat16)
    return high, (x - high.astype(jnp.float32)).astype(jnp.bfloat16)


def beside(a, b):
    return jnp.concatenate([a, b], axis=1)


def above(a, b):
    return jnp.concatenate([a, b], axis=0)


def folded(both):
    n = both.shape[1] // 2
    return both[:, :n] + both[:, n:]


def pair_product(left, right, dims):
    if dims == TM:
        rows = above(*left)
    else:
        rows = beside(*left)
    if dims == MT:
        return folded(dot(rows, above(beside(right[0], right[0]), beside(right[1], right[1])), MT))
    return folded(dot(rows, above(beside(*right), beside(*right)), dims))


def low_times(low, x, dims):
    high, rest = halves(x)
    if dims == MT:
        return dot(beside(low, low), beside(high, rest), MT)
    return dot(beside(low, low), above(high, rest), MM)


def times_low(x, low):
    high, rest = halves(x)
    return dot(beside(high, rest), above(low, low), MM)


def stream_offsets(owners):
    bits = owners.bit_length() - 1
    orders = ([0, 1] + list(range(2, bits)), [1, 0] + list(range(2, bits)))
    offsets = [
        [sum(((p >> (bits - 1 - i)) & 1) << bit for i, bit in enumerate(order)) for p in range(owners)]
        for order in orders
    ]
    return orders, offsets


def table_kernel(owners, capacity, place_ref, owner_ref, kv_ref, *rest):
    table_ref, own_rows, count, held = rest
    own_rows[...] = kv_ref[...].T

    for o in range(owners):
        count[o] = 0

    def enter(b, carry):
        o = owner_ref[b]
        s = count[o]
        count[o] = s + 1
        held[o * capacity + s] = b
        return carry

    lax.fori_loop(0, owners * capacity, enter, 0, unroll=8)
    here, core = place_ref[0], place_ref[1]
    offsets = stream_offsets(owners)[1]
    for side in range(2):
        first_slot = 2 * (core ^ side)
        for stream in range(2):
            for p in range(owners):
                entry = (side * 2 + stream) * owners + p
                table_ref[entry] = held[(here ^ offsets[stream][p]) * capacity + first_slot + stream]


def tiles_kernel(owners, first, table_ref, f_own, f_sib, own_rows, kv_sib, *rest):
    out_a, out_b, sib_rows = rest
    tile = out_a.shape[-1]
    col_tiles = own_rows.shape[0] // tile
    sib_rows[...] = kv_sib[...].T
    for stream, out in enumerate((out_a, out_b)):

        def one(i, carry, stream=stream, out=out):
            block = table_ref[stream * owners + first + i]
            at = pl.ds(pl.multiple_of(block // col_tiles * tile, tile), tile)
            cots = pl.ds(pl.multiple_of(block % col_tiles * tile, tile), tile)
            out[i] = dot(own_rows[cots, :], f_own[:, at], MM) + dot(
                sib_rows[cots, :], f_sib[:, at], MM
            )
            return carry

        lax.fori_loop(0, owners // 2, one, 0, unroll=8)


SMEM = pl.BlockSpec(memory_space=pltpu.SMEM)
HBM = pl.BlockSpec(memory_space=pltpu.HBM)
VMEM = pl.BlockSpec(memory_space=pltpu.VMEM)


def whole(shape):
    return pl.BlockSpec(shape, lambda *g: (0,) * len(shape))


def wholes(arrays):
    return [whole(a.shape) for a in arrays]


BIG = pltpu.CompilerParams(vmem_limit_bytes=24 * 2**20)
SMALL = pltpu.CompilerParams(vmem_limit_bytes=12 * 2**20)


def rotated_kernel(side_ref, m_ref, v_ref, l_ref, r_ref, ql_ref, qr_ref, *outs):
    rot_ref, second_ref, power_ref = outs
    for k in range(2):
        left = ql_ref[0, k]
        right = qr_ref[0, k]
        half = times_low(m_ref[0, k].T, left)
        rot_ref[k] = 0.95 * low_times(right.T, half, MM)
        second_ref[k] = 0.95 * v_ref[0, k].T
        power_ref[2 * k] = 0.95 * times_low(l_ref[0, k], left)
        power_ref[2 * k + 1] = 0.95 * times_low(r_ref[0, k], right)


def direction_kernel(side_ref, a_ref, b_ref, m_ref, v_ref, ql_ref, qr_ref, dir_ref, grad_ref):
    pair = range(2)
    lefts = [ql_ref[0, k] for k in pair]
    rights = [qr_ref[0, k] for k in pair]
    turned = [right.T for right in rights]
    grads = [a_ref[k] + b_ref[k] for k in pair]
    rots = [times_low(grads[k], lefts[k]) for k in pair]
    rots = [low_times(turned[k], rots[k], MM) for k in pair]
    scaled = []
    for k in pair:
        moment_rot = m_ref[k] + 0.05 * rots[k]
        second = v_ref[k] + 0.05 * rots[k] * rots[k]
        scaled.append(moment_rot / (jnp.sqrt(second) + 1e-08))
    outs = [low_times(rights[k], scaled[k], MM) for k in pair]
    outs = [low_times(lefts[k], outs[k], MT) for k in pair]
    for k in pair:
        dir_ref[k] = outs[k].astype(dir_ref.dtype)
        grad_ref[k] = grads[k]


def slots_of(*arrays):
    tile = arrays[0].shape[-1]
    return [pl.BlockSpec((1, 2, tile, tile), lambda i, s: (0, s[0], 0, 0)) for _ in arrays]


def on_slots(kernel, side, plain, slotted, outs, flops):
    return pl.pallas_call(
        kernel,
        out_shape=tuple(outs),
        grid_spec=pltpu.PrefetchScalarGridSpec(
            num_scalar_prefetch=1,
            grid=(1,),
            in_specs=wholes(plain) + slots_of(*slotted),
            out_specs=tuple(wholes(outs)),
        ),
        compiler_params=SMALL,
        cost_estimate=pl.CostEstimate(flops=flops, bytes_accessed=800_000, transcendentals=0),
        name=kernel.__name__.removesuffix("_kernel"),
    )(side, *plain, *slotted)


def sweep(values):
    pairs = [halves(y) for y in values]
    grams = [halves(pair_product(p, p, MT)) for p in pairs]
    return tuple(
        1.5 * y - 0.5 * pair_product(g, p, MM) for y, g, p in zip(values, grams, pairs)
    )


def sweeps(values, count):
    return lax.fori_loop(0, count, lambda i, v: sweep(v), tuple(values), unroll=2)


STAGES = (5, NS_STEPS - 5)


def refresh_kernel(side_ref, g_ref, power_ref, ql_ref, qr_ref, iter_ref):
    values = []
    for k in range(2):
        turned = g_ref[k]
        grad = turned.T
        for i, rows, columns, basis in ((0, grad, turned, ql_ref), (1, turned, grad, qr_ref)):
            half = times_low(columns, basis[0, k])
            power = power_ref[2 * k + i] + 0.05 * pair_product(halves(rows), halves(half), MM)
            values.append((power / jnp.sqrt(jnp.sum(power * power) + 1e-06)).T)
    for i, y in enumerate(sweeps(values, STAGES[0])):
        iter_ref[i] = y


def finish_kernel(iter_ref, out_ref):
    for i, y in enumerate(sweeps([iter_ref[i] for i in range(4)], STAGES[1])):
        out_ref[i] = y.T.astype(out_ref.dtype)


def sweeping(kernel, values, dtype, count):
    tile = values.shape[-1]
    return pl.pallas_call(
        kernel,
        out_shape=jax.ShapeDtypeStruct(values.shape, dtype),
        compiler_params=SMALL,
        cost_estimate=pl.CostEstimate(
            flops=4 * 2 * count * 4 * 2 * tile**3, bytes_accessed=400_000, transcendentals=0
        ),
        name=kernel.__name__.removesuffix("_kernel"),
    )(values)


def place_tiles(col_tiles, entries, table_ref, sources, out, sems):
    tile = sources[0].shape[-1]
    copies = []
    for entry, source in zip(entries, sources):
        for i in range(source.shape[0]):
            block = table_ref[entry + i]
            rows = pl.ds(pl.multiple_of(block // col_tiles * tile, tile), tile)
            columns = pl.ds(pl.multiple_of(block % col_tiles * tile, tile), tile)
            copies.append(
                pltpu.make_async_copy(source.at[i], out.at[rows, columns], sems.at[len(copies)])
            )
            copies[-1].start()
    return copies


def begin_kernel(col_tiles, entries, table_ref, place_ref, own_ref, sib_ref, *refs):
    sources = refs[:-4]
    out, left, right, sems = refs[-4:]
    copies = place_tiles(col_tiles, entries, table_ref, sources, out, sems)
    core = place_ref[1]
    for source, first in ((own_ref, 2 * core), (sib_ref, 2 - 2 * core)):
        for k in range(2):
            for i, target in enumerate((left, right)):
                copies.append(
                    pltpu.make_async_copy(
                        source.at[2 * k + i], target.at[0, first + k], sems.at[len(copies)]
                    )
                )
                copies[-1].start()
    for copy in copies:
        copy.wait()


def more_kernel(col_tiles, entries, table_ref, *refs):
    out, sems = refs[-2:]
    for copy in place_tiles(col_tiles, entries, table_ref, refs[:-3], out, sems):
        copy.wait()


def place_more(update, table, col_tiles, entries, sources):
    count = sum(x.shape[0] for x in sources)
    return pl.pallas_call(
        functools.partial(more_kernel, col_tiles, entries),
        out_shape=jax.ShapeDtypeStruct(update.shape, update.dtype),
        in_specs=[SMEM] + [VMEM] * len(sources) + [HBM],
        out_specs=HBM,
        scratch_shapes=[pltpu.SemaphoreType.DMA((count,))],
        input_output_aliases={1 + len(sources): 0},
        compiler_params=SMALL,
        cost_estimate=pl.CostEstimate(flops=0, bytes_accessed=1_000_000, transcendentals=0),
        name="more",
    )(table, *sources, update)


def per_device_dealt(
    owners,
    features,
    kv_cotangent,
    owner_of_block,
    first_moment,
    second_moment,
    left_stat,
    right_stat,
    left_basis,
    right_basis,
):
    tile = left_basis.shape[-1]
    capacity = left_basis.shape[1]
    rows, d_win = features.shape
    width = kv_cotangent.shape[1]
    col_tiles = width // tile
    here = lax.axis_index("dp")
    core = lax.axis_index("inner")
    place = jnp.stack([here, core]).astype(jnp.int32)
    side = core.reshape(1).astype(jnp.int32)
    orders = stream_offsets(owners)[0]
    near = owners // 2

    f_sib = swap_along(features, "inner", 2, 1)
    kv_sib = swap_along(kv_cotangent, "inner", 2, 1)
    flipped = pltpu.VMEM((width, rows), jnp.bfloat16)
    part = jax.ShapeDtypeStruct((near, tile, tile), jnp.float32)
    f32_pair = jax.ShapeDtypeStruct((2, tile, tile), jnp.float32)
    table, own_rows = pl.pallas_call(
        functools.partial(table_kernel, owners, capacity),
        out_shape=(
            jax.ShapeDtypeStruct((4 * owners,), jnp.int32),
            jax.ShapeDtypeStruct((width, rows), jnp.bfloat16),
        ),
        in_specs=[SMEM, SMEM, VMEM],
        out_specs=(SMEM, VMEM),
        compiler_params=SMALL,
        scratch_shapes=[
            pltpu.SMEM((owners,), jnp.int32),
            pltpu.SMEM((owners * capacity,), jnp.int32),
        ],
        cost_estimate=pl.CostEstimate(flops=0, bytes_accessed=1_000_000, transcendentals=0),
        name="table",
    )(place, owner_of_block, kv_cotangent)

    def tiles_from(first):
        inputs = (features, f_sib, own_rows, kv_sib)
        return pl.pallas_call(
            functools.partial(tiles_kernel, owners, first),
            out_shape=(part, part),
            grid=(1,),
            in_specs=[SMEM] + wholes(inputs),
            out_specs=(whole(part.shape), whole(part.shape)),
            scratch_shapes=[flipped],
            compiler_params=BIG,
            cost_estimate=pl.CostEstimate(
                flops=2 * owners * 2 * tile * tile * 2 * rows,
                bytes_accessed=3_500_000,
                transcendentals=0,
            ),
            name="tiles",
        )(table, *inputs)

    sent_a, sent_b = tiles_from(near)
    got_a = swap_along(sent_a, "dp", owners, 1 << orders[0][0])
    got_b = swap_along(sent_b, "dp", owners, 1 << orders[1][0])
    kept_a, kept_b = tiles_from(0)
    quad = jax.ShapeDtypeStruct((4, tile, tile), jnp.float32)
    moment_rot, second, power = on_slots(
        rotated_kernel,
        side,
        (),
        (first_moment, second_moment, left_stat, right_stat, left_basis, right_basis),
        (f32_pair, f32_pair, quad),
        16 * 2 * tile**3,
    )

    half = near // 2
    next_a = swap_along(kept_a[half:] + got_a[half:], "dp", owners, 1 << orders[0][1])
    next_b = swap_along(kept_b[half:] + got_b[half:], "dp", owners, 1 << orders[1][1])
    kept = jnp.stack([kept_a[:half] + got_a[:half], kept_b[:half] + got_b[:half]], axis=1)
    got = jnp.stack([next_a, next_b], axis=1)
    for bit in orders[0][2:]:
        half = kept.shape[0] // 2
        sent = kept[half:] + got[half:]
        kept = kept[:half] + got[:half]
        if half == 1:
            sent, kept = sent[0], kept[0]
        got = swap_along(sent, "dp", owners, 1 << bit)
    direction, grads = on_slots(
        direction_kernel,
        side,
        (kept, got, moment_rot, second),
        (left_basis, right_basis),
        (jax.ShapeDtypeStruct(f32_pair.shape, jnp.bfloat16), f32_pair),
        16 * 2 * tile**3,
    )

    bits = len(orders[0])
    high = owners // 4
    tiles = []
    for p in range(high):
        offset = sum(((p >> (bits - 3 - i)) & 1) << bit for i, bit in enumerate(orders[0][2:]))
        tiles.append(swap_along(direction, "dp", owners, offset) if offset else direction)
    values = on_slots(
        refresh_kernel,
        side,
        (grads, power),
        (left_basis, right_basis),
        (quad,),
        4 * (4 + 2 * STAGES[0]) * 4 * 2 * tile**3,
    )[0]
    mine = [jnp.stack([t[stream] for t in tiles]) for stream in range(2)]
    mine, values = lax.optimization_barrier((mine, values))
    other = [swap_along(m, "dp", owners, 1 << order[1]) for m, order in zip(mine, orders)]
    fresh = sweeping(finish_kernel, values, jnp.bfloat16, STAGES[1])
    mine = [jnp.concatenate(both, axis=0) for both in zip(mine, other)]
    mine, fresh = lax.optimization_barrier((mine, fresh))
    other = [swap_along(m, "dp", owners, 1 << order[0]) for m, order in zip(mine, orders)]
    fresh_sib = swap_along(fresh, "inner", 2, 1)
    mine_sib = [swap_along(m, "inner", 2, 1) for m in mine]
    basis = jax.ShapeDtypeStruct(left_basis.shape, left_basis.dtype)
    update, new_left, new_right = pl.pallas_call(
        functools.partial(
            begin_kernel, col_tiles, (0, owners, 2 * owners, 3 * owners)
        ),
        out_shape=(jax.ShapeDtypeStruct((d_win, width), jnp.bfloat16), basis, basis),
        in_specs=[SMEM, SMEM] + [VMEM] * 6,
        out_specs=(HBM, HBM, HBM),
        scratch_shapes=[pltpu.SemaphoreType.DMA((4 * near + 8,))],
        compiler_params=SMALL,
        cost_estimate=pl.CostEstimate(flops=0, bytes_accessed=1_300_000, transcendentals=0),
        name="begin",
    )(table, place, fresh, fresh_sib, *mine, *mine_sib)
    update, other = lax.optimization_barrier((update, other))
    other_sib = [swap_along(o, "inner", 2, 1) for o in other]
    update = place_more(update, table, col_tiles, (near, owners + near), other)
    update = place_more(
        update, table, col_tiles, (2 * owners + near, 3 * owners + near), other_sib
    )
    return update, new_left, new_right


def solution(mesh):
    owners = mesh.shape["dp"]
    inner = mesh.shape["inner"]

    def per_device(*args):
        capacity = args[-1].shape[1]
        full = args[2].shape[0] == owners * capacity
        if full and inner == 2 and capacity == 4 and owners >= 8 and owners & (owners - 1) == 0:
            return per_device_dealt(owners, *args)
        return per_device_plain(*args)

    return jax.shard_map(
        per_device,
        mesh=mesh,
        in_specs=(
            P(("dp", "inner"), None),
            P(("dp", "inner"), None),
            P(),
            P("dp", None, None, None),
            P("dp", None, None, None),
            P("dp", None, None, None),
            P("dp", None, None, None),
            P("dp", None, None, None),
            P("dp", None, None, None),
        ),
        out_specs=(P(), P("dp", None, None, None), P("dp", None, None, None)),
        check_vma=False,
    )
```

```python
import functools

import jax
import jax.numpy as jnp
from jax import lax
from jax.experimental import pallas as pl
from jax.experimental.pallas import tpu as pltpu
from jax.sharding import PartitionSpec as P

NS_STEPS = 12


highest = lax.Precision.HIGHEST


def rotate_in(basis_left, matrix, basis_right):
    half = jnp.einsum("sji,sjk->sik", basis_left, matrix, precision=highest)
    return jnp.einsum("sij,sjk->sik", half, basis_right, precision=highest)


def rotate_out(basis_left, matrix, basis_right):
    half = jnp.einsum("sij,sjk->sik", basis_left, matrix, precision=highest)
    return jnp.einsum("sij,skj->sik", half, basis_right, precision=highest)


def orthogonalize(stat, basis):
    power = jnp.einsum("sij,sjk->sik", stat, basis, precision=highest)
    scale = jnp.sqrt(jnp.sum(power * power, axis=(1, 2), keepdims=True) + 1e-06)
    iterate = power / scale
    for sweep in range(NS_STEPS):
        gram = jnp.einsum("sji,sjk->sik", iterate, iterate, precision=highest)
        iterate = 1.5 * iterate - 0.5 * jnp.einsum("sij,sjk->sik", iterate, gram, precision=highest)
    return iterate


def soap_tiles(grads, first, second, stat_left, stat_right, basis_left, basis_right):
    rotated = rotate_in(basis_left, grads, basis_right)
    moment = 0.95 * first + 0.05 * grads
    moment_rot = rotate_in(basis_left, moment, basis_right)
    second_new = 0.95 * second + 0.05 * rotated * rotated
    direction = rotate_out(basis_left, moment_rot / (jnp.sqrt(second_new) + 1e-08), basis_right)
    left_new = 0.95 * stat_left + 0.05 * jnp.einsum("sij,skj->sik", grads, grads, precision=highest)
    right_new = 0.95 * stat_right + 0.05 * jnp.einsum(
        "sji,sjk->sik", grads, grads, precision=highest
    )
    return (direction, orthogonalize(left_new, basis_left), orthogonalize(right_new, basis_right))


def per_device_plain(
    features,
    kv_cotangent,
    owner_of_block,
    first_moment,
    second_moment,
    left_stat,
    right_stat,
    left_basis,
    right_basis,
):
    tile = left_basis.shape[-1]
    capacity = left_basis.shape[1]
    d_win = features.shape[1]
    width = kv_cotangent.shape[1]
    row_tiles = d_win // tile
    col_tiles = width // tile
    nblocks = owner_of_block.shape[0]
    owner_here = lax.axis_index("dp")
    block_ids = jnp.arange(nblocks, dtype=jnp.int32)
    same = owner_of_block[:, None] == owner_of_block[None, :]
    earlier = block_ids[None, :] < block_ids[:, None]
    slot = jnp.sum((same & earlier).astype(jnp.int32), axis=1)
    slot_ids = jnp.arange(capacity, dtype=jnp.int32)
    match = (owner_of_block[None, :] == owner_here) & (slot[None, :] == slot_ids[:, None])
    live = jnp.any(match, axis=1)
    which = jnp.sum(jnp.where(match, block_ids[None, :], 0), axis=1)
    row_start = which // col_tiles * tile
    col_start = which % col_tiles * tile
    partial_grad = lax.dot_general(
        features, kv_cotangent, (((0,), (0,)), ((), ())), preferred_element_type=jnp.float32
    )
    grad = lax.psum(partial_grad, ("dp", "inner"))
    fetched = [
        lax.dynamic_slice(grad, (row_start[slot_index], col_start[slot_index]), (tile, tile))
        for slot_index in range(capacity)
    ]
    grads = jnp.stack(fetched)
    basis_left = left_basis[0].astype(jnp.float32)
    basis_right = right_basis[0].astype(jnp.float32)
    direction, left_iter, right_iter = soap_tiles(
        grads,
        first_moment[0],
        second_moment[0],
        left_stat[0],
        right_stat[0],
        basis_left,
        basis_right,
    )
    direction_low = direction.astype(jnp.bfloat16)
    everyone = lax.all_gather(direction_low[None], "dp", axis=0, tiled=True)
    tiles = everyone[owner_of_block, slot]
    update = (
        tiles.reshape(row_tiles, col_tiles, tile, tile).transpose(0, 2, 1, 3).reshape(d_win, width)
    )
    keep = live[:, None, None]
    new_left = jnp.where(keep, left_iter.astype(jnp.bfloat16), left_basis[0])
    new_right = jnp.where(keep, right_iter.astype(jnp.bfloat16), right_basis[0])
    return (update, new_left[None], new_right[None])


MM = ((1,), (0,))
MT = ((1,), (1,))
TM = ((0,), (0,))


def swap_along(values, axis, size, bit):
    return lax.ppermute(values, axis, [(i, i ^ bit) for i in range(size)])


def dot(left, right, dims):
    return lax.dot_general(left, right, (dims, ((), ())), preferred_element_type=jnp.float32)


def halves(x):
    high = x.astype(jnp.bfloat16)
    return high, (x - high.astype(jnp.float32)).astype(jnp.bfloat16)


def beside(a, b):
    return jnp.concatenate([a, b], axis=1)


def above(a, b):
    return jnp.concatenate([a, b], axis=0)


def folded(both):
    n = both.shape[1] // 2
    return both[:, :n] + both[:, n:]


def pair_product(left, right, dims):
    if dims == TM:
        rows = above(*left)
    else:
        rows = beside(*left)
    if dims == MT:
        return folded(dot(rows, above(beside(right[0], right[0]), beside(right[1], right[1])), MT))
    return folded(dot(rows, above(beside(*right), beside(*right)), dims))


def low_times(low, x, dims):
    high, rest = halves(x)
    if dims == MT:
        return dot(beside(low, low), beside(high, rest), MT)
    return dot(beside(low, low), above(high, rest), MM)


def times_low(x, low):
    high, rest = halves(x)
    return dot(beside(high, rest), above(low, low), MM)


def stream_offsets(owners):
    bits = owners.bit_length() - 1
    orders = ([0, 1] + list(range(2, bits)), [1, 0] + list(range(2, bits)))
    offsets = [
        [sum(((p >> (bits - 1 - i)) & 1) << bit for i, bit in enumerate(order)) for p in range(owners)]
        for order in orders
    ]
    return orders, offsets


def table_kernel(owners, capacity, place_ref, owner_ref, kv_ref, *rest):
    table_ref, own_rows, count, held = rest
    own_rows[...] = kv_ref[...].T

    for o in range(owners):
        count[o] = 0

    def enter(b, carry):
        o = owner_ref[b]
        s = count[o]
        count[o] = s + 1
        held[o * capacity + s] = b
        return carry

    lax.fori_loop(0, owners * capacity, enter, 0, unroll=8)
    here, core = place_ref[0], place_ref[1]
    offsets = stream_offsets(owners)[1]
    for side in range(2):
        first_slot = 2 * (core ^ side)
        for stream in range(2):
            for p in range(owners):
                entry = (side * 2 + stream) * owners + p
                table_ref[entry] = held[(here ^ offsets[stream][p]) * capacity + first_slot + stream]


def tiles_kernel(owners, first, table_ref, f_own, f_sib, own_rows, kv_sib, *rest):
    out_a, out_b, sib_rows = rest
    tile = out_a.shape[-1]
    col_tiles = own_rows.shape[0] // tile
    sib_rows[...] = kv_sib[...].T
    for stream, out in enumerate((out_a, out_b)):

        def one(i, carry, stream=stream, out=out):
            block = table_ref[stream * owners + first + i]
            at = pl.ds(pl.multiple_of(block // col_tiles * tile, tile), tile)
            cots = pl.ds(pl.multiple_of(block % col_tiles * tile, tile), tile)
            out[i] = dot(own_rows[cots, :], f_own[:, at], MM) + dot(
                sib_rows[cots, :], f_sib[:, at], MM
            )
            return carry

        lax.fori_loop(0, owners // 2, one, 0, unroll=8)


SMEM = pl.BlockSpec(memory_space=pltpu.SMEM)
HBM = pl.BlockSpec(memory_space=pltpu.HBM)
VMEM = pl.BlockSpec(memory_space=pltpu.VMEM)


def whole(shape):
    return pl.BlockSpec(shape, lambda *g: (0,) * len(shape))


def wholes(arrays):
    return [whole(a.shape) for a in arrays]


BIG = pltpu.CompilerParams(vmem_limit_bytes=24 * 2**20)
SMALL = pltpu.CompilerParams(vmem_limit_bytes=12 * 2**20)


def rotated_kernel(side_ref, m_ref, v_ref, l_ref, r_ref, ql_ref, qr_ref, *outs):
    rot_ref, second_ref, power_ref = outs
    for k in range(2):
        left = ql_ref[0, k]
        right = qr_ref[0, k]
        half = times_low(m_ref[0, k].T, left)
        rot_ref[k] = 0.95 * low_times(right.T, half, MM)
        second_ref[k] = 0.95 * v_ref[0, k].T
        power_ref[2 * k] = 0.95 * times_low(l_ref[0, k], left)
        power_ref[2 * k + 1] = 0.95 * times_low(r_ref[0, k], right)


def direction_kernel(side_ref, a_ref, b_ref, m_ref, v_ref, ql_ref, qr_ref, dir_ref, grad_ref):
    pair = range(2)
    lefts = [ql_ref[0, k] for k in pair]
    rights = [qr_ref[0, k] for k in pair]
    turned = [right.T for right in rights]
    grads = [a_ref[k] + b_ref[k] for k in pair]
    rots = [times_low(grads[k], lefts[k]) for k in pair]
    rots = [low_times(turned[k], rots[k], MM) for k in pair]
    scaled = []
    for k in pair:
        moment_rot = m_ref[k] + 0.05 * rots[k]
        second = v_ref[k] + 0.05 * rots[k] * rots[k]
        scaled.append(moment_rot / (jnp.sqrt(second) + 1e-08))
    outs = [low_times(rights[k], scaled[k], MM) for k in pair]
    outs = [low_times(lefts[k], outs[k], MT) for k in pair]
    for k in pair:
        dir_ref[k] = outs[k].astype(dir_ref.dtype)
        grad_ref[k] = grads[k]


def slots_of(*arrays):
    tile = arrays[0].shape[-1]
    return [pl.BlockSpec((1, 2, tile, tile), lambda i, s: (0, s[0], 0, 0)) for _ in arrays]


def on_slots(kernel, side, plain, slotted, outs, flops):
    return pl.pallas_call(
        kernel,
        out_shape=tuple(outs),
        grid_spec=pltpu.PrefetchScalarGridSpec(
            num_scalar_prefetch=1,
            grid=(1,),
            in_specs=wholes(plain) + slots_of(*slotted),
            out_specs=tuple(wholes(outs)),
        ),
        compiler_params=SMALL,
        cost_estimate=pl.CostEstimate(flops=flops, bytes_accessed=800_000, transcendentals=0),
        name=kernel.__name__.removesuffix("_kernel"),
    )(side, *plain, *slotted)


def sweep(values):
    pairs = [halves(y) for y in values]
    grams = [halves(pair_product(p, p, MT)) for p in pairs]
    return tuple(
        1.5 * y - 0.5 * pair_product(g, p, MM) for y, g, p in zip(values, grams, pairs)
    )


def sweeps(values, count):
    return lax.fori_loop(0, count, lambda i, v: sweep(v), tuple(values), unroll=2)


STAGES = (5, NS_STEPS - 5)


def refresh_kernel(side_ref, g_ref, power_ref, ql_ref, qr_ref, iter_ref):
    values = []
    for k in range(2):
        turned = g_ref[k]
        grad = turned.T
        for i, rows, columns, basis in ((0, grad, turned, ql_ref), (1, turned, grad, qr_ref)):
            half = times_low(columns, basis[0, k])
            power = power_ref[2 * k + i] + 0.05 * pair_product(halves(rows), halves(half), MM)
            values.append((power / jnp.sqrt(jnp.sum(power * power) + 1e-06)).T)
    for i, y in enumerate(sweeps(values, STAGES[0])):
        iter_ref[i] = y


def finish_kernel(iter_ref, out_ref):
    for i, y in enumerate(sweeps([iter_ref[i] for i in range(4)], STAGES[1])):
        out_ref[i] = y.T.astype(out_ref.dtype)


def sweeping(kernel, values, dtype, count):
    tile = values.shape[-1]
    return pl.pallas_call(
        kernel,
        out_shape=jax.ShapeDtypeStruct(values.shape, dtype),
        compiler_params=SMALL,
        cost_estimate=pl.CostEstimate(
            flops=4 * 2 * count * 4 * 2 * tile**3, bytes_accessed=400_000, transcendentals=0
        ),
        name=kernel.__name__.removesuffix("_kernel"),
    )(values)


def far_order(high):
    return [0] + sorted(range(1, high), key=lambda p: (p % 2, -(p // 2)))


def place_tiles(col_tiles, high, entries, table_ref, sources, out, sems):
    tile = sources[0].shape[-1]
    copies = []
    for entry, source in zip(entries, sources):
        for i in range(source.shape[0]):
            block = table_ref[entry + i - i % high + far_order(high)[i % high]]
            rows = pl.ds(pl.multiple_of(block // col_tiles * tile, tile), tile)
            columns = pl.ds(pl.multiple_of(block % col_tiles * tile, tile), tile)
            copies.append(
                pltpu.make_async_copy(source.at[i], out.at[rows, columns], sems.at[len(copies)])
            )
            copies[-1].start()
    return copies


def begin_kernel(col_tiles, high, entries, table_ref, place_ref, own_ref, sib_ref, *refs):
    sources = refs[:-4]
    out, left, right, sems = refs[-4:]
    copies = place_tiles(col_tiles, high, entries, table_ref, sources, out, sems)
    core = place_ref[1]
    for source, first in ((own_ref, 2 * core), (sib_ref, 2 - 2 * core)):
        for k in range(2):
            for i, target in enumerate((left, right)):
                copies.append(
                    pltpu.make_async_copy(
                        source.at[2 * k + i], target.at[0, first + k], sems.at[len(copies)]
                    )
                )
                copies[-1].start()
    for copy in copies:
        copy.wait()


def more_kernel(col_tiles, high, entries, table_ref, *refs):
    out, sems = refs[-2:]
    for copy in place_tiles(col_tiles, high, entries, table_ref, refs[:-3], out, sems):
        copy.wait()


def place_more(update, table, col_tiles, high, entries, sources):
    count = sum(x.shape[0] for x in sources)
    return pl.pallas_call(
        functools.partial(more_kernel, col_tiles, high, entries),
        out_shape=jax.ShapeDtypeStruct(update.shape, update.dtype),
        in_specs=[SMEM] + [VMEM] * len(sources) + [HBM],
        out_specs=HBM,
        scratch_shapes=[pltpu.SemaphoreType.DMA((count,))],
        input_output_aliases={1 + len(sources): 0},
        compiler_params=SMALL,
        cost_estimate=pl.CostEstimate(flops=0, bytes_accessed=1_000_000, transcendentals=0),
        name="more",
    )(table, *sources, update)


def per_device_dealt(
    owners,
    features,
    kv_cotangent,
    owner_of_block,
    first_moment,
    second_moment,
    left_stat,
    right_stat,
    left_basis,
    right_basis,
):
    tile = left_basis.shape[-1]
    capacity = left_basis.shape[1]
    rows, d_win = features.shape
    width = kv_cotangent.shape[1]
    col_tiles = width // tile
    here = lax.axis_index("dp")
    core = lax.axis_index("inner")
    place = jnp.stack([here, core]).astype(jnp.int32)
    side = core.reshape(1).astype(jnp.int32)
    orders = stream_offsets(owners)[0]
    near = owners // 2

    f_sib = swap_along(features, "inner", 2, 1)
    kv_sib = swap_along(kv_cotangent, "inner", 2, 1)
    flipped = pltpu.VMEM((width, rows), jnp.bfloat16)
    part = jax.ShapeDtypeStruct((near, tile, tile), jnp.float32)
    f32_pair = jax.ShapeDtypeStruct((2, tile, tile), jnp.float32)
    table, own_rows = pl.pallas_call(
        functools.partial(table_kernel, owners, capacity),
        out_shape=(
            jax.ShapeDtypeStruct((4 * owners,), jnp.int32),
            jax.ShapeDtypeStruct((width, rows), jnp.bfloat16),
        ),
        in_specs=[SMEM, SMEM, VMEM],
        out_specs=(SMEM, VMEM),
        compiler_params=SMALL,
        scratch_shapes=[
            pltpu.SMEM((owners,), jnp.int32),
            pltpu.SMEM((owners * capacity,), jnp.int32),
        ],
        cost_estimate=pl.CostEstimate(flops=0, bytes_accessed=1_000_000, transcendentals=0),
        name="table",
    )(place, owner_of_block, kv_cotangent)

    def tiles_from(first):
        inputs = (features, f_sib, own_rows, kv_sib)
        return pl.pallas_call(
            functools.partial(tiles_kernel, owners, first),
            out_shape=(part, part),
            grid=(1,),
            in_specs=[SMEM] + wholes(inputs),
            out_specs=(whole(part.shape), whole(part.shape)),
            scratch_shapes=[flipped],
            compiler_params=BIG,
            cost_estimate=pl.CostEstimate(
                flops=2 * owners * 2 * tile * tile * 2 * rows,
                bytes_accessed=3_500_000,
                transcendentals=0,
            ),
            name="tiles",
        )(table, *inputs)

    sent_a, sent_b = tiles_from(near)
    got_a = swap_along(sent_a, "dp", owners, 1 << orders[0][0])
    got_b = swap_along(sent_b, "dp", owners, 1 << orders[1][0])
    kept_a, kept_b = tiles_from(0)
    quad = jax.ShapeDtypeStruct((4, tile, tile), jnp.float32)
    moment_rot, second, power = on_slots(
        rotated_kernel,
        side,
        (),
        (first_moment, second_moment, left_stat, right_stat, left_basis, right_basis),
        (f32_pair, f32_pair, quad),
        16 * 2 * tile**3,
    )

    half = near // 2
    next_a = swap_along(kept_a[half:] + got_a[half:], "dp", owners, 1 << orders[0][1])
    next_b = swap_along(kept_b[half:] + got_b[half:], "dp", owners, 1 << orders[1][1])
    kept = jnp.stack([kept_a[:half] + got_a[:half], kept_b[:half] + got_b[:half]], axis=1)
    got = jnp.stack([next_a, next_b], axis=1)
    for bit in orders[0][2:]:
        half = kept.shape[0] // 2
        sent = kept[half:] + got[half:]
        kept = kept[:half] + got[:half]
        if half == 1:
            sent, kept = sent[0], kept[0]
        got = swap_along(sent, "dp", owners, 1 << bit)
    direction, grads = on_slots(
        direction_kernel,
        side,
        (kept, got, moment_rot, second),
        (left_basis, right_basis),
        (jax.ShapeDtypeStruct(f32_pair.shape, jnp.bfloat16), f32_pair),
        16 * 2 * tile**3,
    )

    bits = len(orders[0])
    high = owners // 4
    tiles = []
    for p in far_order(high):
        offset = sum(((p >> (bits - 3 - i)) & 1) << bit for i, bit in enumerate(orders[0][2:]))
        tiles.append(swap_along(direction, "dp", owners, offset) if offset else direction)
    values = on_slots(
        refresh_kernel,
        side,
        (grads, power),
        (left_basis, right_basis),
        (quad,),
        4 * (4 + 2 * STAGES[0]) * 4 * 2 * tile**3,
    )[0]
    mine = [jnp.stack([t[stream] for t in tiles]) for stream in range(2)]
    mine, values = lax.optimization_barrier((mine, values))
    other = [swap_along(m, "dp", owners, 1 << order[1]) for m, order in zip(mine, orders)]
    fresh = sweeping(finish_kernel, values, jnp.bfloat16, STAGES[1])
    mine = [jnp.concatenate(both, axis=0) for both in zip(mine, other)]
    mine, fresh = lax.optimization_barrier((mine, fresh))
    other = [swap_along(m, "dp", owners, 1 << order[0]) for m, order in zip(mine, orders)]
    fresh_sib = swap_along(fresh, "inner", 2, 1)
    basis = jax.ShapeDtypeStruct(left_basis.shape, left_basis.dtype)
    update, new_left, new_right = pl.pallas_call(
        functools.partial(begin_kernel, col_tiles, high, (0, owners)),
        out_shape=(jax.ShapeDtypeStruct((d_win, width), jnp.bfloat16), basis, basis),
        in_specs=[SMEM, SMEM] + [VMEM] * 4,
        out_specs=(HBM, HBM, HBM),
        scratch_shapes=[pltpu.SemaphoreType.DMA((2 * near + 8,))],
        compiler_params=SMALL,
        cost_estimate=pl.CostEstimate(flops=0, bytes_accessed=800_000, transcendentals=0),
        name="begin",
    )(table, place, fresh, fresh_sib, *mine)
    update, other = lax.optimization_barrier((update, other))
    mine_sib = [swap_along(m, "inner", 2, 1) for m in mine]
    other_sib = [swap_along(o, "inner", 2, 1) for o in other]
    update = place_more(
        update,
        table,
        col_tiles,
        high,
        (2 * owners, 3 * owners, near, owners + near),
        mine_sib + other,
    )
    update = place_more(
        update, table, col_tiles, high, (2 * owners + near, 3 * owners + near), other_sib
    )
    return update, new_left, new_right


def solution(mesh):
    owners = mesh.shape["dp"]
    inner = mesh.shape["inner"]

    def per_device(*args):
        capacity = args[-1].shape[1]
        full = args[2].shape[0] == owners * capacity
        if full and inner == 2 and capacity == 4 and owners >= 8 and owners & (owners - 1) == 0:
            return per_device_dealt(owners, *args)
        return per_device_plain(*args)

    return jax.shard_map(
        per_device,
        mesh=mesh,
        in_specs=(
            P(("dp", "inner"), None),
            P(("dp", "inner"), None),
            P(),
            P("dp", None, None, None),
            P("dp", None, None, None),
            P("dp", None, None, None),
            P("dp", None, None, None),
            P("dp", None, None, None),
            P("dp", None, None, None),
        ),
        out_specs=(P(), P("dp", None, None, None), P("dp", None, None, None)),
        check_vma=False,
    )
```

```python
import functools

import jax
import jax.numpy as jnp
from jax import lax
from jax.experimental import pallas as pl
from jax.experimental.pallas import tpu as pltpu
from jax.sharding import PartitionSpec as P

NS_STEPS = 12


highest = lax.Precision.HIGHEST


def rotate_in(basis_left, matrix, basis_right):
    half = jnp.einsum("sji,sjk->sik", basis_left, matrix, precision=highest)
    return jnp.einsum("sij,sjk->sik", half, basis_right, precision=highest)


def rotate_out(basis_left, matrix, basis_right):
    half = jnp.einsum("sij,sjk->sik", basis_left, matrix, precision=highest)
    return jnp.einsum("sij,skj->sik", half, basis_right, precision=highest)


def orthogonalize(stat, basis):
    power = jnp.einsum("sij,sjk->sik", stat, basis, precision=highest)
    scale = jnp.sqrt(jnp.sum(power * power, axis=(1, 2), keepdims=True) + 1e-06)
    iterate = power / scale
    for sweep in range(NS_STEPS):
        gram = jnp.einsum("sji,sjk->sik", iterate, iterate, precision=highest)
        iterate = 1.5 * iterate - 0.5 * jnp.einsum("sij,sjk->sik", iterate, gram, precision=highest)
    return iterate


def soap_tiles(grads, first, second, stat_left, stat_right, basis_left, basis_right):
    rotated = rotate_in(basis_left, grads, basis_right)
    moment = 0.95 * first + 0.05 * grads
    moment_rot = rotate_in(basis_left, moment, basis_right)
    second_new = 0.95 * second + 0.05 * rotated * rotated
    direction = rotate_out(basis_left, moment_rot / (jnp.sqrt(second_new) + 1e-08), basis_right)
    left_new = 0.95 * stat_left + 0.05 * jnp.einsum("sij,skj->sik", grads, grads, precision=highest)
    right_new = 0.95 * stat_right + 0.05 * jnp.einsum(
        "sji,sjk->sik", grads, grads, precision=highest
    )
    return (direction, orthogonalize(left_new, basis_left), orthogonalize(right_new, basis_right))


def per_device_plain(
    features,
    kv_cotangent,
    owner_of_block,
    first_moment,
    second_moment,
    left_stat,
    right_stat,
    left_basis,
    right_basis,
):
    tile = left_basis.shape[-1]
    capacity = left_basis.shape[1]
    d_win = features.shape[1]
    width = kv_cotangent.shape[1]
    row_tiles = d_win // tile
    col_tiles = width // tile
    nblocks = owner_of_block.shape[0]
    owner_here = lax.axis_index("dp")
    block_ids = jnp.arange(nblocks, dtype=jnp.int32)
    same = owner_of_block[:, None] == owner_of_block[None, :]
    earlier = block_ids[None, :] < block_ids[:, None]
    slot = jnp.sum((same & earlier).astype(jnp.int32), axis=1)
    slot_ids = jnp.arange(capacity, dtype=jnp.int32)
    match = (owner_of_block[None, :] == owner_here) & (slot[None, :] == slot_ids[:, None])
    live = jnp.any(match, axis=1)
    which = jnp.sum(jnp.where(match, block_ids[None, :], 0), axis=1)
    row_start = which // col_tiles * tile
    col_start = which % col_tiles * tile
    partial_grad = lax.dot_general(
        features, kv_cotangent, (((0,), (0,)), ((), ())), preferred_element_type=jnp.float32
    )
    grad = lax.psum(partial_grad, ("dp", "inner"))
    fetched = [
        lax.dynamic_slice(grad, (row_start[slot_index], col_start[slot_index]), (tile, tile))
        for slot_index in range(capacity)
    ]
    grads = jnp.stack(fetched)
    basis_left = left_basis[0].astype(jnp.float32)
    basis_right = right_basis[0].astype(jnp.float32)
    direction, left_iter, right_iter = soap_tiles(
        grads,
        first_moment[0],
        second_moment[0],
        left_stat[0],
        right_stat[0],
        basis_left,
        basis_right,
    )
    direction_low = direction.astype(jnp.bfloat16)
    everyone = lax.all_gather(direction_low[None], "dp", axis=0, tiled=True)
    tiles = everyone[owner_of_block, slot]
    update = (
        tiles.reshape(row_tiles, col_tiles, tile, tile).transpose(0, 2, 1, 3).reshape(d_win, width)
    )
    keep = live[:, None, None]
    new_left = jnp.where(keep, left_iter.astype(jnp.bfloat16), left_basis[0])
    new_right = jnp.where(keep, right_iter.astype(jnp.bfloat16), right_basis[0])
    return (update, new_left[None], new_right[None])


MM = ((1,), (0,))
MT = ((1,), (1,))
TM = ((0,), (0,))


def swap_along(values, axis, size, bit):
    return lax.ppermute(values, axis, [(i, i ^ bit) for i in range(size)])


def dot(left, right, dims):
    return lax.dot_general(left, right, (dims, ((), ())), preferred_element_type=jnp.float32)


def halves(x):
    high = x.astype(jnp.bfloat16)
    return high, (x - high.astype(jnp.float32)).astype(jnp.bfloat16)


def beside(a, b):
    return jnp.concatenate([a, b], axis=1)


def above(a, b):
    return jnp.concatenate([a, b], axis=0)


def folded(both):
    n = both.shape[1] // 2
    return both[:, :n] + both[:, n:]


def pair_product(left, right, dims):
    if dims == TM:
        rows = above(*left)
    else:
        rows = beside(*left)
    if dims == MT:
        return folded(dot(rows, above(beside(right[0], right[0]), beside(right[1], right[1])), MT))
    return folded(dot(rows, above(beside(*right), beside(*right)), dims))


def low_times(low, x, dims):
    high, rest = halves(x)
    if dims == MT:
        return dot(beside(low, low), beside(high, rest), MT)
    return dot(beside(low, low), above(high, rest), MM)


def times_low(x, low):
    high, rest = halves(x)
    return dot(beside(high, rest), above(low, low), MM)


def stream_offsets(owners):
    bits = owners.bit_length() - 1
    highs = list(range(2, bits))
    orders = ([0, 1] + highs, [1, 0] + highs, highs + [0, 1])
    offsets = [
        [sum(((p >> (bits - 1 - i)) & 1) << bit for i, bit in enumerate(order)) for p in range(owners)]
        for order in orders
    ]
    return orders, offsets


def table_kernel(owners, capacity, place_ref, owner_ref, kv_ref, *rest):
    table_ref, own_rows, count, held = rest
    own_rows[...] = kv_ref[...].T

    for o in range(owners):
        count[o] = 0

    def enter(b, carry):
        o = owner_ref[b]
        s = count[o]
        count[o] = s + 1
        held[o * capacity + s] = b
        return carry

    lax.fori_loop(0, owners * capacity, enter, 0, unroll=8)
    here, core = place_ref[0], place_ref[1]
    offsets = stream_offsets(owners)[1]
    for side in range(2):
        first_slot = 2 * (core ^ side)
        for stream in range(2):
            for p in range(owners):
                entry = (side * 2 + stream) * owners + p
                table_ref[entry] = held[(here ^ offsets[stream][p]) * capacity + first_slot + stream]


EDGE = 16


def tiles_kernel(owners, first, table_ref, f_own, f_sib, own_rows, kv_sib, *rest):
    sib_rows = rest[-1]
    out_a, out_b = rest[-5:-3] if first == 0 else rest[:2]
    tile = out_a.shape[-1]
    body = tile - EDGE
    near = owners // 2
    col_tiles = own_rows.shape[0] // tile
    offsets = stream_offsets(owners)[1]
    sib_rows[...] = kv_sib[...].T
    for stream, out in enumerate((out_a, out_b)):
        for i in range(near):
            block = table_ref[stream * owners + first + i]
            at = pl.ds(pl.multiple_of(block // col_tiles * tile, tile), tile)
            cots = pl.ds(pl.multiple_of(block % col_tiles * tile, tile), tile)
            total = dot(own_rows[cots, :], f_own[:, at], MM) + dot(
                sib_rows[cots, :], f_sib[:, at], MM
            )
            out[i] = total[:body]
            place = 2 * offsets[2].index(offsets[stream][first + i]) + stream
            if first:
                rest[2][place] = total[body:]
            elif place < owners:
                rest[-3][place] = total[body:]
            else:
                rest[-2][place - owners] = total[body:]
            if first == 0:
                place = 2 * offsets[2].index(offsets[stream][near + i]) + stream
                if place < owners:
                    rest[-3][place] = rest[0][place]
                else:
                    rest[-2][place - owners] = rest[0][place]


SMEM = pl.BlockSpec(memory_space=pltpu.SMEM)
HBM = pl.BlockSpec(memory_space=pltpu.HBM)
VMEM = pl.BlockSpec(memory_space=pltpu.VMEM)


def whole(shape):
    return pl.BlockSpec(shape, lambda *g: (0,) * len(shape))


def wholes(arrays):
    return [whole(a.shape) for a in arrays]


BIG = pltpu.CompilerParams(vmem_limit_bytes=24 * 2**20)
SMALL = pltpu.CompilerParams(vmem_limit_bytes=12 * 2**20)


def rotated_kernel(side_ref, m_ref, v_ref, l_ref, r_ref, ql_ref, qr_ref, *outs):
    rot_ref, second_ref, power_ref = outs
    for k in range(2):
        left = ql_ref[0, k]
        right = qr_ref[0, k]
        half = times_low(m_ref[0, k].T, left)
        rot_ref[k] = 0.95 * low_times(right.T, half, MM)
        second_ref[k] = 0.95 * v_ref[0, k].T
        power_ref[2 * k] = 0.95 * times_low(l_ref[0, k], left)
        power_ref[2 * k + 1] = 0.95 * times_low(r_ref[0, k], right)


def direction_kernel(side_ref, a_ref, b_ref, c_ref, d_ref, m_ref, v_ref, *rest):
    ql_ref, qr_ref, dir_ref, grad_ref = rest
    pair = range(2)
    lefts = [ql_ref[0, k] for k in pair]
    rights = [qr_ref[0, k] for k in pair]
    turned = [right.T for right in rights]
    grads = [above(a_ref[k] + b_ref[k], c_ref[k] + d_ref[k]) for k in pair]
    rots = [times_low(grads[k], lefts[k]) for k in pair]
    rots = [low_times(turned[k], rots[k], MM) for k in pair]
    scaled = []
    for k in pair:
        moment_rot = m_ref[k] + 0.05 * rots[k]
        second = v_ref[k] + 0.05 * rots[k] * rots[k]
        scaled.append(moment_rot / (jnp.sqrt(second) + 1e-08))
    outs = [low_times(rights[k], scaled[k], MM) for k in pair]
    outs = [low_times(lefts[k], outs[k], MT) for k in pair]
    for k in pair:
        dir_ref[k] = outs[k].astype(dir_ref.dtype)
        grad_ref[k] = grads[k]


def slots_of(*arrays):
    tile = arrays[0].shape[-1]
    return [pl.BlockSpec((1, 2, tile, tile), lambda i, s: (0, s[0], 0, 0)) for _ in arrays]


def on_slots(kernel, side, plain, slotted, outs, flops):
    return pl.pallas_call(
        kernel,
        out_shape=tuple(outs),
        grid_spec=pltpu.PrefetchScalarGridSpec(
            num_scalar_prefetch=1,
            grid=(1,),
            in_specs=wholes(plain) + slots_of(*slotted),
            out_specs=tuple(wholes(outs)),
        ),
        compiler_params=SMALL,
        cost_estimate=pl.CostEstimate(flops=flops, bytes_accessed=800_000, transcendentals=0),
        name=kernel.__name__.removesuffix("_kernel"),
    )(side, *plain, *slotted)


def sweep(values):
    pairs = [halves(y) for y in values]
    grams = [halves(pair_product(p, p, MT)) for p in pairs]
    return tuple(
        1.5 * y - 0.5 * pair_product(g, p, MM) for y, g, p in zip(values, grams, pairs)
    )


def sweeps(values, count):
    return lax.fori_loop(0, count, lambda i, v: sweep(v), tuple(values), unroll=2)


STAGES = (5, NS_STEPS - 5)


def refresh_kernel(side_ref, g_ref, power_ref, ql_ref, qr_ref, iter_ref):
    values = []
    for k in range(2):
        turned = g_ref[k]
        grad = turned.T
        for i, rows, columns, basis in ((0, grad, turned, ql_ref), (1, turned, grad, qr_ref)):
            half = times_low(columns, basis[0, k])
            power = power_ref[2 * k + i] + 0.05 * pair_product(halves(rows), halves(half), MM)
            values.append((power / jnp.sqrt(jnp.sum(power * power) + 1e-06)).T)
    for i, y in enumerate(sweeps(values, STAGES[0])):
        iter_ref[i] = y


def finish_kernel(iter_ref, out_ref):
    for i, y in enumerate(sweeps([iter_ref[i] for i in range(4)], STAGES[1])):
        out_ref[i] = y.T.astype(out_ref.dtype)


def sweeping(kernel, values, dtype, count):
    tile = values.shape[-1]
    return pl.pallas_call(
        kernel,
        out_shape=jax.ShapeDtypeStruct(values.shape, dtype),
        compiler_params=SMALL,
        cost_estimate=pl.CostEstimate(
            flops=4 * 2 * count * 4 * 2 * tile**3, bytes_accessed=400_000, transcendentals=0
        ),
        name=kernel.__name__.removesuffix("_kernel"),
    )(values)


def place_tiles(col_tiles, entries, table_ref, sources, out, sems):
    tile = sources[0].shape[-1]
    copies = []
    for entry, source in zip(entries, sources):
        for i in range(source.shape[0]):
            block = table_ref[entry + i]
            rows = pl.ds(pl.multiple_of(block // col_tiles * tile, tile), tile)
            columns = pl.ds(pl.multiple_of(block % col_tiles * tile, tile), tile)
            copies.append(
                pltpu.make_async_copy(source.at[i], out.at[rows, columns], sems.at[len(copies)])
            )
            copies[-1].start()
    return copies


def begin_kernel(col_tiles, entries, table_ref, place_ref, own_ref, sib_ref, *refs):
    sources = refs[:-4]
    out, left, right, sems = refs[-4:]
    copies = place_tiles(col_tiles, entries, table_ref, sources, out, sems)
    core = place_ref[1]
    for source, first in ((own_ref, 2 * core), (sib_ref, 2 - 2 * core)):
        for k in range(2):
            for i, target in enumerate((left, right)):
                copies.append(
                    pltpu.make_async_copy(
                        source.at[2 * k + i], target.at[0, first + k], sems.at[len(copies)]
                    )
                )
                copies[-1].start()
    for copy in copies:
        copy.wait()


def more_kernel(col_tiles, entries, table_ref, *refs):
    out, sems = refs[-2:]
    for copy in place_tiles(col_tiles, entries, table_ref, refs[:-3], out, sems):
        copy.wait()


def place_more(update, table, col_tiles, entries, sources):
    count = sum(x.shape[0] for x in sources)
    return pl.pallas_call(
        functools.partial(more_kernel, col_tiles, entries),
        out_shape=jax.ShapeDtypeStruct(update.shape, update.dtype),
        in_specs=[SMEM] + [VMEM] * len(sources) + [HBM],
        out_specs=HBM,
        scratch_shapes=[pltpu.SemaphoreType.DMA((count,))],
        input_output_aliases={1 + len(sources): 0},
        compiler_params=SMALL,
        cost_estimate=pl.CostEstimate(flops=0, bytes_accessed=1_000_000, transcendentals=0),
        name="more",
    )(table, *sources, update)


def per_device_dealt(
    owners,
    features,
    kv_cotangent,
    owner_of_block,
    first_moment,
    second_moment,
    left_stat,
    right_stat,
    left_basis,
    right_basis,
):
    tile = left_basis.shape[-1]
    capacity = left_basis.shape[1]
    rows, d_win = features.shape
    width = kv_cotangent.shape[1]
    col_tiles = width // tile
    here = lax.axis_index("dp")
    core = lax.axis_index("inner")
    place = jnp.stack([here, core]).astype(jnp.int32)
    side = core.reshape(1).astype(jnp.int32)
    orders = stream_offsets(owners)[0]
    near = owners // 2
    bits = len(orders[0])

    f_sib = swap_along(features, "inner", 2, 1)
    kv_sib = swap_along(kv_cotangent, "inner", 2, 1)
    flipped = pltpu.VMEM((width, rows), jnp.bfloat16)
    part = jax.ShapeDtypeStruct((near, tile - EDGE, tile), jnp.float32)
    edge = jax.ShapeDtypeStruct((owners, EDGE, tile), jnp.float32)
    edges = jax.ShapeDtypeStruct((2 * owners, EDGE, tile), jnp.float32)
    f32_pair = jax.ShapeDtypeStruct((2, tile, tile), jnp.float32)
    table, own_rows = pl.pallas_call(
        functools.partial(table_kernel, owners, capacity),
        out_shape=(
            jax.ShapeDtypeStruct((4 * owners,), jnp.int32),
            jax.ShapeDtypeStruct((width, rows), jnp.bfloat16),
        ),
        in_specs=[SMEM, SMEM, VMEM],
        out_specs=(SMEM, VMEM),
        compiler_params=SMALL,
        scratch_shapes=[
            pltpu.SMEM((owners,), jnp.int32),
            pltpu.SMEM((owners * capacity,), jnp.int32),
        ],
        cost_estimate=pl.CostEstimate(flops=0, bytes_accessed=1_000_000, transcendentals=0),
        name="table",
    )(place, owner_of_block, kv_cotangent)

    def tiles_from(first, outs, *more):
        inputs = (features, f_sib, own_rows, kv_sib, *more)
        return pl.pallas_call(
            functools.partial(tiles_kernel, owners, first),
            out_shape=outs,
            grid=(1,),
            in_specs=[SMEM] + wholes(inputs),
            out_specs=tuple(wholes(outs)),
            scratch_shapes=[flipped],
            compiler_params=BIG,
            cost_estimate=pl.CostEstimate(
                flops=2 * owners * 2 * tile * tile * 2 * rows,
                bytes_accessed=3_500_000,
                transcendentals=0,
            ),
            name="tiles",
        )(table, *inputs)

    sent_a, sent_b, early = tiles_from(near, (part, part, edges))
    got_a = swap_along(sent_a, "dp", owners, 1 << orders[0][0])
    got_b = swap_along(sent_b, "dp", owners, 1 << orders[1][0])
    kept_a, kept_b, kept_c, sent_c = tiles_from(0, (part, part, edge, edge), early)
    got_c = swap_along(sent_c, "dp", owners, 1 << orders[2][0])
    quad = jax.ShapeDtypeStruct((4, tile, tile), jnp.float32)
    moment_rot, second, power = on_slots(
        rotated_kernel,
        side,
        (),
        (first_moment, second_moment, left_stat, right_stat, left_basis, right_basis),
        (f32_pair, f32_pair, quad),
        16 * 2 * tile**3,
    )

    def halved(kept, got):
        half = kept.shape[0] // 2
        return kept[:half] + got[:half], kept[half:] + got[half:]

    def after(values, *needed):
        return lax.optimization_barrier((values, *needed))[0]

    def edges_on(step, kept, got):
        kept, sent = halved(kept, got)
        return kept, sent, swap_along(sent, "dp", owners, 1 << orders[2][step])

    kept_c, sent_c, got_c = edges_on(1, kept_c, got_c)
    kept_a, sent_a = halved(kept_a, got_a)
    kept_b, sent_b = halved(kept_b, got_b)
    got_a = swap_along(sent_a, "dp", owners, 1 << orders[0][1])
    got_b = swap_along(sent_b, "dp", owners, 1 << orders[1][1])
    kept = jnp.stack([kept_a, kept_b], axis=1)
    got = jnp.stack([got_a, got_b], axis=1)
    for step in range(2, bits):
        due = got_c
        kept_c, sent_c, got_c = edges_on(step, kept_c, got_c)
        kept, sent = halved(kept, got)
        sent = after(sent, due)
        if step == bits - 1:
            sent, kept = sent[0], kept[0]
        got = swap_along(sent, "dp", owners, 1 << orders[0][step])
    direction, grads = on_slots(
        direction_kernel,
        side,
        (kept, got, kept_c, got_c, moment_rot, second),
        (left_basis, right_basis),
        (jax.ShapeDtypeStruct(f32_pair.shape, jnp.bfloat16), f32_pair),
        16 * 2 * tile**3,
    )

    high = owners // 4
    tiles = []
    for p in range(high):
        offset = sum(((p >> (bits - 3 - i)) & 1) << bit for i, bit in enumerate(orders[0][2:]))
        tiles.append(swap_along(direction, "dp", owners, offset) if offset else direction)
    values = on_slots(
        refresh_kernel,
        side,
        (grads, power),
        (left_basis, right_basis),
        (quad,),
        4 * (4 + 2 * STAGES[0]) * 4 * 2 * tile**3,
    )[0]
    mine = [jnp.stack([t[stream] for t in tiles]) for stream in range(2)]
    mine, values = lax.optimization_barrier((mine, values))
    other = [swap_along(m, "dp", owners, 1 << order[1]) for m, order in zip(mine, orders)]
    fresh = sweeping(finish_kernel, values, jnp.bfloat16, STAGES[1])
    mine = [jnp.concatenate(both, axis=0) for both in zip(mine, other)]
    mine, fresh = lax.optimization_barrier((mine, fresh))
    other = [swap_along(m, "dp", owners, 1 << order[0]) for m, order in zip(mine, orders)]
    fresh_sib = swap_along(fresh, "inner", 2, 1)
    basis = jax.ShapeDtypeStruct(left_basis.shape, left_basis.dtype)
    update, new_left, new_right = pl.pallas_call(
        functools.partial(begin_kernel, col_tiles, (0, owners)),
        out_shape=(jax.ShapeDtypeStruct((d_win, width), jnp.bfloat16), basis, basis),
        in_specs=[SMEM, SMEM] + [VMEM] * 4,
        out_specs=(HBM, HBM, HBM),
        scratch_shapes=[pltpu.SemaphoreType.DMA((2 * near + 8,))],
        compiler_params=SMALL,
        cost_estimate=pl.CostEstimate(flops=0, bytes_accessed=800_000, transcendentals=0),
        name="begin",
    )(table, place, fresh, fresh_sib, *mine)
    update, other = lax.optimization_barrier((update, other))
    mine_sib = [swap_along(m, "inner", 2, 1) for m in mine]
    other_sib = [swap_along(o, "inner", 2, 1) for o in other]
    update = place_more(
        update,
        table,
        col_tiles,
        (2 * owners, 3 * owners, near, owners + near),
        mine_sib + other,
    )
    update = place_more(
        update, table, col_tiles, (2 * owners + near, 3 * owners + near), other_sib
    )
    return update, new_left, new_right


def solution(mesh):
    owners = mesh.shape["dp"]
    inner = mesh.shape["inner"]

    def per_device(*args):
        capacity = args[-1].shape[1]
        full = args[2].shape[0] == owners * capacity
        if full and inner == 2 and capacity == 4 and owners >= 8 and owners & (owners - 1) == 0:
            return per_device_dealt(owners, *args)
        return per_device_plain(*args)

    return jax.shard_map(
        per_device,
        mesh=mesh,
        in_specs=(
            P(("dp", "inner"), None),
            P(("dp", "inner"), None),
            P(),
            P("dp", None, None, None),
            P("dp", None, None, None),
            P("dp", None, None, None),
            P("dp", None, None, None),
            P("dp", None, None, None),
            P("dp", None, None, None),
        ),
        out_specs=(P(), P("dp", None, None, None), P("dp", None, None, None)),
        check_vma=False,
    )
```

```python
import functools

import jax
import jax.numpy as jnp
from jax import lax
from jax.experimental import pallas as pl
from jax.experimental.pallas import tpu as pltpu
from jax.sharding import PartitionSpec as P

NS_STEPS = 12


highest = lax.Precision.HIGHEST


def rotate_in(basis_left, matrix, basis_right):
    half = jnp.einsum("sji,sjk->sik", basis_left, matrix, precision=highest)
    return jnp.einsum("sij,sjk->sik", half, basis_right, precision=highest)


def rotate_out(basis_left, matrix, basis_right):
    half = jnp.einsum("sij,sjk->sik", basis_left, matrix, precision=highest)
    return jnp.einsum("sij,skj->sik", half, basis_right, precision=highest)


def orthogonalize(stat, basis):
    power = jnp.einsum("sij,sjk->sik", stat, basis, precision=highest)
    scale = jnp.sqrt(jnp.sum(power * power, axis=(1, 2), keepdims=True) + 1e-06)
    iterate = power / scale
    for sweep in range(NS_STEPS):
        gram = jnp.einsum("sji,sjk->sik", iterate, iterate, precision=highest)
        iterate = 1.5 * iterate - 0.5 * jnp.einsum("sij,sjk->sik", iterate, gram, precision=highest)
    return iterate


def soap_tiles(grads, first, second, stat_left, stat_right, basis_left, basis_right):
    rotated = rotate_in(basis_left, grads, basis_right)
    moment = 0.95 * first + 0.05 * grads
    moment_rot = rotate_in(basis_left, moment, basis_right)
    second_new = 0.95 * second + 0.05 * rotated * rotated
    direction = rotate_out(basis_left, moment_rot / (jnp.sqrt(second_new) + 1e-08), basis_right)
    left_new = 0.95 * stat_left + 0.05 * jnp.einsum("sij,skj->sik", grads, grads, precision=highest)
    right_new = 0.95 * stat_right + 0.05 * jnp.einsum(
        "sji,sjk->sik", grads, grads, precision=highest
    )
    return (direction, orthogonalize(left_new, basis_left), orthogonalize(right_new, basis_right))


def per_device_plain(
    features,
    kv_cotangent,
    owner_of_block,
    first_moment,
    second_moment,
    left_stat,
    right_stat,
    left_basis,
    right_basis,
):
    tile = left_basis.shape[-1]
    capacity = left_basis.shape[1]
    d_win = features.shape[1]
    width = kv_cotangent.shape[1]
    row_tiles = d_win // tile
    col_tiles = width // tile
    nblocks = owner_of_block.shape[0]
    owner_here = lax.axis_index("dp")
    block_ids = jnp.arange(nblocks, dtype=jnp.int32)
    same = owner_of_block[:, None] == owner_of_block[None, :]
    earlier = block_ids[None, :] < block_ids[:, None]
    slot = jnp.sum((same & earlier).astype(jnp.int32), axis=1)
    slot_ids = jnp.arange(capacity, dtype=jnp.int32)
    match = (owner_of_block[None, :] == owner_here) & (slot[None, :] == slot_ids[:, None])
    live = jnp.any(match, axis=1)
    which = jnp.sum(jnp.where(match, block_ids[None, :], 0), axis=1)
    row_start = which // col_tiles * tile
    col_start = which % col_tiles * tile
    partial_grad = lax.dot_general(
        features, kv_cotangent, (((0,), (0,)), ((), ())), preferred_element_type=jnp.float32
    )
    grad = lax.psum(partial_grad, ("dp", "inner"))
    fetched = [
        lax.dynamic_slice(grad, (row_start[slot_index], col_start[slot_index]), (tile, tile))
        for slot_index in range(capacity)
    ]
    grads = jnp.stack(fetched)
    basis_left = left_basis[0].astype(jnp.float32)
    basis_right = right_basis[0].astype(jnp.float32)
    direction, left_iter, right_iter = soap_tiles(
        grads,
        first_moment[0],
        second_moment[0],
        left_stat[0],
        right_stat[0],
        basis_left,
        basis_right,
    )
    direction_low = direction.astype(jnp.bfloat16)
    everyone = lax.all_gather(direction_low[None], "dp", axis=0, tiled=True)
    tiles = everyone[owner_of_block, slot]
    update = (
        tiles.reshape(row_tiles, col_tiles, tile, tile).transpose(0, 2, 1, 3).reshape(d_win, width)
    )
    keep = live[:, None, None]
    new_left = jnp.where(keep, left_iter.astype(jnp.bfloat16), left_basis[0])
    new_right = jnp.where(keep, right_iter.astype(jnp.bfloat16), right_basis[0])
    return (update, new_left[None], new_right[None])


MM = ((1,), (0,))
MT = ((1,), (1,))
TM = ((0,), (0,))


def swap_along(values, axis, size, bit):
    return lax.ppermute(values, axis, [(i, i ^ bit) for i in range(size)])


def dot(left, right, dims):
    return lax.dot_general(left, right, (dims, ((), ())), preferred_element_type=jnp.float32)


def halves(x):
    high = x.astype(jnp.bfloat16)
    return high, (x - high.astype(jnp.float32)).astype(jnp.bfloat16)


def beside(a, b):
    return jnp.concatenate([a, b], axis=1)


def above(a, b):
    return jnp.concatenate([a, b], axis=0)


def folded(both):
    n = both.shape[1] // 2
    return both[:, :n] + both[:, n:]


def pair_product(left, right, dims):
    if dims == TM:
        rows = above(*left)
    else:
        rows = beside(*left)
    if dims == MT:
        return folded(dot(rows, above(beside(right[0], right[0]), beside(right[1], right[1])), MT))
    return folded(dot(rows, above(beside(*right), beside(*right)), dims))


def low_times(low, x, dims):
    high, rest = halves(x)
    if dims == MT:
        return dot(beside(low, low), beside(high, rest), MT)
    return dot(beside(low, low), above(high, rest), MM)


def times_low(x, low):
    high, rest = halves(x)
    return dot(beside(high, rest), above(low, low), MM)


def stream_offsets(owners):
    bits = owners.bit_length() - 1
    highs = list(range(2, bits))
    orders = ([0, 1] + highs, [1, 0] + highs, highs + [0, 1])
    offsets = [
        [sum(((p >> (bits - 1 - i)) & 1) << bit for i, bit in enumerate(order)) for p in range(owners)]
        for order in orders
    ]
    return orders, offsets


def table_kernel(owners, capacity, place_ref, owner_ref, kv_ref, *rest):
    table_ref, own_rows, count, held = rest
    own_rows[...] = kv_ref[...].T

    for o in range(owners):
        count[o] = 0

    def enter(b, carry):
        o = owner_ref[b]
        s = count[o]
        count[o] = s + 1
        held[o * capacity + s] = b
        return carry

    lax.fori_loop(0, owners * capacity, enter, 0, unroll=8)
    here, core = place_ref[0], place_ref[1]
    offsets = stream_offsets(owners)[1]
    for side in range(2):
        first_slot = 2 * (core ^ side)
        for stream in range(2):
            for p in range(owners):
                entry = (side * 2 + stream) * owners + p
                table_ref[entry] = held[(here ^ offsets[stream][p]) * capacity + first_slot + stream]


EDGE = 24


def tiles_kernel(owners, first, table_ref, f_own, f_sib, own_rows, kv_sib, *rest):
    sib_rows = rest[-1]
    out_a, out_b = rest[-5:-3] if first == 0 else rest[:2]
    tile = out_a.shape[-1]
    body = tile - EDGE
    near = owners // 2
    col_tiles = own_rows.shape[0] // tile
    offsets = stream_offsets(owners)[1]
    sib_rows[...] = kv_sib[...].T
    for stream, out in enumerate((out_a, out_b)):
        for i in range(near):
            block = table_ref[stream * owners + first + i]
            at = pl.ds(pl.multiple_of(block // col_tiles * tile, tile), tile)
            cots = pl.ds(pl.multiple_of(block % col_tiles * tile, tile), tile)
            total = dot(own_rows[cots, :], f_own[:, at], MM) + dot(
                sib_rows[cots, :], f_sib[:, at], MM
            )
            out[i] = total[:body]
            place = 2 * offsets[2].index(offsets[stream][first + i]) + stream
            if first:
                rest[2][place] = total[body:]
            elif place < owners:
                rest[-3][place] = total[body:]
            else:
                rest[-2][place - owners] = total[body:]
            if first == 0:
                place = 2 * offsets[2].index(offsets[stream][near + i]) + stream
                if place < owners:
                    rest[-3][place] = rest[0][place]
                else:
                    rest[-2][place - owners] = rest[0][place]


SMEM = pl.BlockSpec(memory_space=pltpu.SMEM)
HBM = pl.BlockSpec(memory_space=pltpu.HBM)
VMEM = pl.BlockSpec(memory_space=pltpu.VMEM)


def whole(shape):
    return pl.BlockSpec(shape, lambda *g: (0,) * len(shape))


def wholes(arrays):
    return [whole(a.shape) for a in arrays]


BIG = pltpu.CompilerParams(vmem_limit_bytes=24 * 2**20)
SMALL = pltpu.CompilerParams(vmem_limit_bytes=12 * 2**20)


def rotated_kernel(side_ref, m_ref, v_ref, l_ref, r_ref, ql_ref, qr_ref, *outs):
    rot_ref, second_ref, power_ref = outs
    for k in range(2):
        left = ql_ref[0, k]
        right = qr_ref[0, k]
        half = times_low(m_ref[0, k].T, left)
        rot_ref[k] = 0.95 * low_times(right.T, half, MM)
        second_ref[k] = 0.95 * v_ref[0, k].T
        power_ref[2 * k] = 0.95 * times_low(l_ref[0, k], left)
        power_ref[2 * k + 1] = 0.95 * times_low(r_ref[0, k], right)


def direction_kernel(side_ref, a_ref, b_ref, c_ref, d_ref, m_ref, v_ref, *rest):
    ql_ref, qr_ref, dir_ref, grad_ref = rest
    pair = range(2)
    lefts = [ql_ref[0, k] for k in pair]
    rights = [qr_ref[0, k] for k in pair]
    turned = [right.T for right in rights]
    grads = [above(a_ref[k] + b_ref[k], c_ref[k] + d_ref[k]) for k in pair]
    rots = [times_low(grads[k], lefts[k]) for k in pair]
    rots = [low_times(turned[k], rots[k], MM) for k in pair]
    scaled = []
    for k in pair:
        moment_rot = m_ref[k] + 0.05 * rots[k]
        second = v_ref[k] + 0.05 * rots[k] * rots[k]
        scaled.append(moment_rot / (jnp.sqrt(second) + 1e-08))
    outs = [low_times(rights[k], scaled[k], MM) for k in pair]
    outs = [low_times(lefts[k], outs[k], MT) for k in pair]
    for k in pair:
        dir_ref[k] = outs[k].astype(dir_ref.dtype)
        grad_ref[k] = grads[k]


def slots_of(*arrays):
    tile = arrays[0].shape[-1]
    return [pl.BlockSpec((1, 2, tile, tile), lambda i, s: (0, s[0], 0, 0)) for _ in arrays]


def on_slots(kernel, side, plain, slotted, outs, flops):
    return pl.pallas_call(
        kernel,
        out_shape=tuple(outs),
        grid_spec=pltpu.PrefetchScalarGridSpec(
            num_scalar_prefetch=1,
            grid=(1,),
            in_specs=wholes(plain) + slots_of(*slotted),
            out_specs=tuple(wholes(outs)),
        ),
        compiler_params=SMALL,
        cost_estimate=pl.CostEstimate(flops=flops, bytes_accessed=800_000, transcendentals=0),
        name=kernel.__name__.removesuffix("_kernel"),
    )(side, *plain, *slotted)


def sweep(values):
    pairs = [halves(y) for y in values]
    grams = [halves(pair_product(p, p, MT)) for p in pairs]
    return tuple(
        1.5 * y - 0.5 * pair_product(g, p, MM) for y, g, p in zip(values, grams, pairs)
    )


def sweeps(values, count):
    return lax.fori_loop(0, count, lambda i, v: sweep(v), tuple(values), unroll=2)


STAGES = (5, NS_STEPS - 5)


def refresh_kernel(side_ref, g_ref, power_ref, ql_ref, qr_ref, iter_ref):
    values = []
    for k in range(2):
        turned = g_ref[k]
        grad = turned.T
        for i, rows, columns, basis in ((0, grad, turned, ql_ref), (1, turned, grad, qr_ref)):
            half = times_low(columns, basis[0, k])
            power = power_ref[2 * k + i] + 0.05 * pair_product(halves(rows), halves(half), MM)
            values.append((power / jnp.sqrt(jnp.sum(power * power) + 1e-06)).T)
    for i, y in enumerate(sweeps(values, STAGES[0])):
        iter_ref[i] = y


def finish_kernel(iter_ref, out_ref):
    for i, y in enumerate(sweeps([iter_ref[i] for i in range(4)], STAGES[1])):
        out_ref[i] = y.T.astype(out_ref.dtype)


def sweeping(kernel, values, dtype, count):
    tile = values.shape[-1]
    return pl.pallas_call(
        kernel,
        out_shape=jax.ShapeDtypeStruct(values.shape, dtype),
        compiler_params=SMALL,
        cost_estimate=pl.CostEstimate(
            flops=4 * 2 * count * 4 * 2 * tile**3, bytes_accessed=400_000, transcendentals=0
        ),
        name=kernel.__name__.removesuffix("_kernel"),
    )(values)


def place_tiles(col_tiles, entries, table_ref, sources, out, sems):
    tile = sources[0].shape[-1]
    copies = []
    for entry, source in zip(entries, sources):
        for i in range(source.shape[0]):
            block = table_ref[entry + i]
            rows = pl.ds(pl.multiple_of(block // col_tiles * tile, tile), tile)
            columns = pl.ds(pl.multiple_of(block % col_tiles * tile, tile), tile)
            copies.append(
                pltpu.make_async_copy(source.at[i], out.at[rows, columns], sems.at[len(copies)])
            )
            copies[-1].start()
    return copies


def begin_kernel(col_tiles, entries, table_ref, place_ref, own_ref, sib_ref, *refs):
    sources = refs[:-4]
    out, left, right, sems = refs[-4:]
    copies = place_tiles(col_tiles, entries, table_ref, sources, out, sems)
    core = place_ref[1]
    for source, first in ((own_ref, 2 * core), (sib_ref, 2 - 2 * core)):
        for k in range(2):
            for i, target in enumerate((left, right)):
                copies.append(
                    pltpu.make_async_copy(
                        source.at[2 * k + i], target.at[0, first + k], sems.at[len(copies)]
                    )
                )
                copies[-1].start()
    for copy in copies:
        copy.wait()


def more_kernel(col_tiles, entries, table_ref, *refs):
    out, sems = refs[-2:]
    for copy in place_tiles(col_tiles, entries, table_ref, refs[:-3], out, sems):
        copy.wait()


def place_more(update, table, col_tiles, entries, sources):
    count = sum(x.shape[0] for x in sources)
    return pl.pallas_call(
        functools.partial(more_kernel, col_tiles, entries),
        out_shape=jax.ShapeDtypeStruct(update.shape, update.dtype),
        in_specs=[SMEM] + [VMEM] * len(sources) + [HBM],
        out_specs=HBM,
        scratch_shapes=[pltpu.SemaphoreType.DMA((count,))],
        input_output_aliases={1 + len(sources): 0},
        compiler_params=SMALL,
        cost_estimate=pl.CostEstimate(flops=0, bytes_accessed=1_000_000, transcendentals=0),
        name="more",
    )(table, *sources, update)


def per_device_dealt(
    owners,
    features,
    kv_cotangent,
    owner_of_block,
    first_moment,
    second_moment,
    left_stat,
    right_stat,
    left_basis,
    right_basis,
):
    tile = left_basis.shape[-1]
    capacity = left_basis.shape[1]
    rows, d_win = features.shape
    width = kv_cotangent.shape[1]
    col_tiles = width // tile
    here = lax.axis_index("dp")
    core = lax.axis_index("inner")
    place = jnp.stack([here, core]).astype(jnp.int32)
    side = core.reshape(1).astype(jnp.int32)
    orders = stream_offsets(owners)[0]
    near = owners // 2
    bits = len(orders[0])

    f_sib = swap_along(features, "inner", 2, 1)
    kv_sib = swap_along(kv_cotangent, "inner", 2, 1)
    flipped = pltpu.VMEM((width, rows), jnp.bfloat16)
    part = jax.ShapeDtypeStruct((near, tile - EDGE, tile), jnp.float32)
    edge = jax.ShapeDtypeStruct((owners, EDGE, tile), jnp.float32)
    edges = jax.ShapeDtypeStruct((2 * owners, EDGE, tile), jnp.float32)
    f32_pair = jax.ShapeDtypeStruct((2, tile, tile), jnp.float32)
    table, own_rows = pl.pallas_call(
        functools.partial(table_kernel, owners, capacity),
        out_shape=(
            jax.ShapeDtypeStruct((4 * owners,), jnp.int32),
            jax.ShapeDtypeStruct((width, rows), jnp.bfloat16),
        ),
        in_specs=[SMEM, SMEM, VMEM],
        out_specs=(SMEM, VMEM),
        compiler_params=SMALL,
        scratch_shapes=[
            pltpu.SMEM((owners,), jnp.int32),
            pltpu.SMEM((owners * capacity,), jnp.int32),
        ],
        cost_estimate=pl.CostEstimate(flops=0, bytes_accessed=1_000_000, transcendentals=0),
        name="table",
    )(place, owner_of_block, kv_cotangent)

    def tiles_from(first, outs, *more):
        inputs = (features, f_sib, own_rows, kv_sib, *more)
        return pl.pallas_call(
            functools.partial(tiles_kernel, owners, first),
            out_shape=outs,
            grid=(1,),
            in_specs=[SMEM] + wholes(inputs),
            out_specs=tuple(wholes(outs)),
            scratch_shapes=[flipped],
            compiler_params=BIG,
            cost_estimate=pl.CostEstimate(
                flops=2 * owners * 2 * tile * tile * 2 * rows,
                bytes_accessed=3_500_000,
                transcendentals=0,
            ),
            name="tiles",
        )(table, *inputs)

    sent_a, sent_b, early = tiles_from(near, (part, part, edges))
    got_a = swap_along(sent_a, "dp", owners, 1 << orders[0][0])
    got_b = swap_along(sent_b, "dp", owners, 1 << orders[1][0])
    kept_a, kept_b, kept_c, sent_c = tiles_from(0, (part, part, edge, edge), early)
    got_c = swap_along(sent_c, "dp", owners, 1 << orders[2][0])
    quad = jax.ShapeDtypeStruct((4, tile, tile), jnp.float32)
    moment_rot, second, power = on_slots(
        rotated_kernel,
        side,
        (),
        (first_moment, second_moment, left_stat, right_stat, left_basis, right_basis),
        (f32_pair, f32_pair, quad),
        16 * 2 * tile**3,
    )

    def halved(kept, got):
        half = kept.shape[0] // 2
        return kept[:half] + got[:half], kept[half:] + got[half:]

    def after(values, *needed):
        return lax.optimization_barrier((values, *needed))[0]

    def edges_on(step, kept, got):
        kept, sent = halved(kept, got)
        return kept, sent, swap_along(sent, "dp", owners, 1 << orders[2][step])

    kept_c, sent_c, got_c = edges_on(1, kept_c, got_c)
    kept_a, sent_a = halved(kept_a, got_a)
    kept_b, sent_b = halved(kept_b, got_b)
    got_a = swap_along(sent_a, "dp", owners, 1 << orders[0][1])
    got_b = swap_along(sent_b, "dp", owners, 1 << orders[1][1])
    kept = jnp.stack([kept_a, kept_b], axis=1)
    got = jnp.stack([got_a, got_b], axis=1)
    for step in range(2, bits):
        kept, sent = halved(kept, got)
        if step > 2:
            sent = after(sent, got_c)
            kept_c, sent_c, got_c = edges_on(step - 1, kept_c, got_c)
        if step == bits - 1:
            sent, kept = sent[0], kept[0]
        got = swap_along(sent, "dp", owners, 1 << orders[0][step])
    kept_c, sent_c, got_c = edges_on(bits - 1, kept_c, got_c)
    direction, grads = on_slots(
        direction_kernel,
        side,
        (kept, got, kept_c, got_c, moment_rot, second),
        (left_basis, right_basis),
        (jax.ShapeDtypeStruct(f32_pair.shape, jnp.bfloat16), f32_pair),
        16 * 2 * tile**3,
    )

    high = owners // 4
    tiles = []
    for p in range(high):
        offset = sum(((p >> (bits - 3 - i)) & 1) << bit for i, bit in enumerate(orders[0][2:]))
        tiles.append(swap_along(direction, "dp", owners, offset) if offset else direction)
    values = on_slots(
        refresh_kernel,
        side,
        (grads, power),
        (left_basis, right_basis),
        (quad,),
        4 * (4 + 2 * STAGES[0]) * 4 * 2 * tile**3,
    )[0]
    mine = [jnp.stack([t[stream] for t in tiles]) for stream in range(2)]
    mine, values = lax.optimization_barrier((mine, values))
    other = [swap_along(m, "dp", owners, 1 << order[1]) for m, order in zip(mine, orders)]
    fresh = sweeping(finish_kernel, values, jnp.bfloat16, STAGES[1])
    mine = [jnp.concatenate(both, axis=0) for both in zip(mine, other)]
    mine, fresh = lax.optimization_barrier((mine, fresh))
    other = [swap_along(m, "dp", owners, 1 << order[0]) for m, order in zip(mine, orders)]
    fresh_sib = swap_along(fresh, "inner", 2, 1)
    basis = jax.ShapeDtypeStruct(left_basis.shape, left_basis.dtype)
    update, new_left, new_right = pl.pallas_call(
        functools.partial(begin_kernel, col_tiles, (0, owners)),
        out_shape=(jax.ShapeDtypeStruct((d_win, width), jnp.bfloat16), basis, basis),
        in_specs=[SMEM, SMEM] + [VMEM] * 4,
        out_specs=(HBM, HBM, HBM),
        scratch_shapes=[pltpu.SemaphoreType.DMA((2 * near + 8,))],
        compiler_params=SMALL,
        cost_estimate=pl.CostEstimate(flops=0, bytes_accessed=800_000, transcendentals=0),
        name="begin",
    )(table, place, fresh, fresh_sib, *mine)
    update, other = lax.optimization_barrier((update, other))
    mine_sib = [swap_along(m, "inner", 2, 1) for m in mine]
    other_sib = [swap_along(o, "inner", 2, 1) for o in other]
    update = place_more(
        update,
        table,
        col_tiles,
        (2 * owners, 3 * owners, near, owners + near),
        mine_sib + other,
    )
    update = place_more(
        update, table, col_tiles, (2 * owners + near, 3 * owners + near), other_sib
    )
    return update, new_left, new_right


def solution(mesh):
    owners = mesh.shape["dp"]
    inner = mesh.shape["inner"]

    def per_device(*args):
        capacity = args[-1].shape[1]
        full = args[2].shape[0] == owners * capacity
        if full and inner == 2 and capacity == 4 and owners >= 8 and owners & (owners - 1) == 0:
            return per_device_dealt(owners, *args)
        return per_device_plain(*args)

    return jax.shard_map(
        per_device,
        mesh=mesh,
        in_specs=(
            P(("dp", "inner"), None),
            P(("dp", "inner"), None),
            P(),
            P("dp", None, None, None),
            P("dp", None, None, None),
            P("dp", None, None, None),
            P("dp", None, None, None),
            P("dp", None, None, None),
            P("dp", None, None, None),
        ),
        out_specs=(P(), P("dp", None, None, None), P("dp", None, None, None)),
        check_vma=False,
    )
```

```python
import functools

import jax
import jax.numpy as jnp
from jax import lax
from jax.experimental import pallas as pl
from jax.experimental.pallas import tpu as pltpu
from jax.sharding import PartitionSpec as P

NS_STEPS = 12


highest = lax.Precision.HIGHEST


def rotate_in(basis_left, matrix, basis_right):
    half = jnp.einsum("sji,sjk->sik", basis_left, matrix, precision=highest)
    return jnp.einsum("sij,sjk->sik", half, basis_right, precision=highest)


def rotate_out(basis_left, matrix, basis_right):
    half = jnp.einsum("sij,sjk->sik", basis_left, matrix, precision=highest)
    return jnp.einsum("sij,skj->sik", half, basis_right, precision=highest)


def orthogonalize(stat, basis):
    power = jnp.einsum("sij,sjk->sik", stat, basis, precision=highest)
    scale = jnp.sqrt(jnp.sum(power * power, axis=(1, 2), keepdims=True) + 1e-06)
    iterate = power / scale
    for sweep in range(NS_STEPS):
        gram = jnp.einsum("sji,sjk->sik", iterate, iterate, precision=highest)
        iterate = 1.5 * iterate - 0.5 * jnp.einsum("sij,sjk->sik", iterate, gram, precision=highest)
    return iterate


def soap_tiles(grads, first, second, stat_left, stat_right, basis_left, basis_right):
    rotated = rotate_in(basis_left, grads, basis_right)
    moment = 0.95 * first + 0.05 * grads
    moment_rot = rotate_in(basis_left, moment, basis_right)
    second_new = 0.95 * second + 0.05 * rotated * rotated
    direction = rotate_out(basis_left, moment_rot / (jnp.sqrt(second_new) + 1e-08), basis_right)
    left_new = 0.95 * stat_left + 0.05 * jnp.einsum("sij,skj->sik", grads, grads, precision=highest)
    right_new = 0.95 * stat_right + 0.05 * jnp.einsum(
        "sji,sjk->sik", grads, grads, precision=highest
    )
    return (direction, orthogonalize(left_new, basis_left), orthogonalize(right_new, basis_right))


def per_device_plain(
    features,
    kv_cotangent,
    owner_of_block,
    first_moment,
    second_moment,
    left_stat,
    right_stat,
    left_basis,
    right_basis,
):
    tile = left_basis.shape[-1]
    capacity = left_basis.shape[1]
    d_win = features.shape[1]
    width = kv_cotangent.shape[1]
    row_tiles = d_win // tile
    col_tiles = width // tile
    nblocks = owner_of_block.shape[0]
    owner_here = lax.axis_index("dp")
    block_ids = jnp.arange(nblocks, dtype=jnp.int32)
    same = owner_of_block[:, None] == owner_of_block[None, :]
    earlier = block_ids[None, :] < block_ids[:, None]
    slot = jnp.sum((same & earlier).astype(jnp.int32), axis=1)
    slot_ids = jnp.arange(capacity, dtype=jnp.int32)
    match = (owner_of_block[None, :] == owner_here) & (slot[None, :] == slot_ids[:, None])
    live = jnp.any(match, axis=1)
    which = jnp.sum(jnp.where(match, block_ids[None, :], 0), axis=1)
    row_start = which // col_tiles * tile
    col_start = which % col_tiles * tile
    partial_grad = lax.dot_general(
        features, kv_cotangent, (((0,), (0,)), ((), ())), preferred_element_type=jnp.float32
    )
    grad = lax.psum(partial_grad, ("dp", "inner"))
    fetched = [
        lax.dynamic_slice(grad, (row_start[slot_index], col_start[slot_index]), (tile, tile))
        for slot_index in range(capacity)
    ]
    grads = jnp.stack(fetched)
    basis_left = left_basis[0].astype(jnp.float32)
    basis_right = right_basis[0].astype(jnp.float32)
    direction, left_iter, right_iter = soap_tiles(
        grads,
        first_moment[0],
        second_moment[0],
        left_stat[0],
        right_stat[0],
        basis_left,
        basis_right,
    )
    direction_low = direction.astype(jnp.bfloat16)
    everyone = lax.all_gather(direction_low[None], "dp", axis=0, tiled=True)
    tiles = everyone[owner_of_block, slot]
    update = (
        tiles.reshape(row_tiles, col_tiles, tile, tile).transpose(0, 2, 1, 3).reshape(d_win, width)
    )
    keep = live[:, None, None]
    new_left = jnp.where(keep, left_iter.astype(jnp.bfloat16), left_basis[0])
    new_right = jnp.where(keep, right_iter.astype(jnp.bfloat16), right_basis[0])
    return (update, new_left[None], new_right[None])


MM = ((1,), (0,))
MT = ((1,), (1,))
TM = ((0,), (0,))


def swap_along(values, axis, size, bit):
    return lax.ppermute(values, axis, [(i, i ^ bit) for i in range(size)])


def dot(left, right, dims):
    return lax.dot_general(left, right, (dims, ((), ())), preferred_element_type=jnp.float32)


def halves(x):
    high = x.astype(jnp.bfloat16)
    return high, (x - high.astype(jnp.float32)).astype(jnp.bfloat16)


def beside(a, b):
    return jnp.concatenate([a, b], axis=1)


def above(a, b):
    return jnp.concatenate([a, b], axis=0)


def folded(both):
    n = both.shape[1] // 2
    return both[:, :n] + both[:, n:]


def pair_product(left, right, dims):
    if dims == TM:
        rows = above(*left)
    else:
        rows = beside(*left)
    if dims == MT:
        return folded(dot(rows, above(beside(right[0], right[0]), beside(right[1], right[1])), MT))
    return folded(dot(rows, above(beside(*right), beside(*right)), dims))


def low_times(low, x, dims):
    high, rest = halves(x)
    if dims == MT:
        return dot(beside(low, low), beside(high, rest), MT)
    return dot(beside(low, low), above(high, rest), MM)


def times_low(x, low):
    high, rest = halves(x)
    return dot(beside(high, rest), above(low, low), MM)


def stream_offsets(owners):
    bits = owners.bit_length() - 1
    highs = list(range(2, bits))
    orders = ([0, 1] + highs, [1, 0] + highs, highs + [0, 1])
    offsets = [
        [sum(((p >> (bits - 1 - i)) & 1) << bit for i, bit in enumerate(order)) for p in range(owners)]
        for order in orders
    ]
    return orders, offsets


def table_kernel(owners, capacity, place_ref, owner_ref, kv_ref, *rest):
    table_ref, own_rows, count, held = rest
    own_rows[...] = kv_ref[...].T

    for o in range(owners):
        count[o] = 0

    def enter(b, carry):
        o = owner_ref[b]
        s = count[o]
        count[o] = s + 1
        held[o * capacity + s] = b
        return carry

    lax.fori_loop(0, owners * capacity, enter, 0, unroll=8)
    here, core = place_ref[0], place_ref[1]
    offsets = stream_offsets(owners)[1]
    for side in range(2):
        first_slot = 2 * (core ^ side)
        for stream in range(2):
            for p in range(owners):
                entry = (side * 2 + stream) * owners + p
                table_ref[entry] = held[(here ^ offsets[stream][p]) * capacity + first_slot + stream]


EDGE = 32


def tile_of(block, f_own, f_sib, own_rows, sib_rows, tile):
    col_tiles = own_rows.shape[0] // tile
    at = pl.ds(pl.multiple_of(block // col_tiles * tile, tile), tile)
    cots = pl.ds(pl.multiple_of(block % col_tiles * tile, tile), tile)
    return dot(own_rows[cots, :], f_own[:, at], MM) + dot(sib_rows[cots, :], f_sib[:, at], MM)


def sent_kernel(owners, stream, table_ref, f_own, f_sib, own_rows, cots_sib, out, edge, *flipped):
    sib_rows = cots_sib
    if flipped:
        sib_rows = flipped[0]
        sib_rows[...] = cots_sib[...].T
    near = owners // 2
    body, tile = out.shape[1:]
    for i in range(near):
        block = table_ref[stream * owners + near + i]
        total = tile_of(block, f_own, f_sib, own_rows, sib_rows, tile)
        out[i] = total[:body]
        edge[i] = total[body:]


def kept_kernel(owners, table_ref, f_own, f_sib, own_rows, sib_rows, *rest):
    early, outs, edges = rest[:2], rest[2:4], rest[4:]
    near = owners // 2
    body, tile = outs[0].shape[1:]
    offsets = stream_offsets(owners)[1]
    for stream, out in enumerate(outs):
        for p in range(owners):
            place = 2 * offsets[2].index(offsets[stream][p]) + stream
            target, at = edges[place // owners], place % owners
            if p < near:
                block = table_ref[stream * owners + p]
                total = tile_of(block, f_own, f_sib, own_rows, sib_rows, tile)
                out[p] = total[:body]
                target[at] = total[body:]
            else:
                target[at] = early[stream][p - near]


SMEM = pl.BlockSpec(memory_space=pltpu.SMEM)
HBM = pl.BlockSpec(memory_space=pltpu.HBM)
VMEM = pl.BlockSpec(memory_space=pltpu.VMEM)


def whole(shape):
    return pl.BlockSpec(shape, lambda *g: (0,) * len(shape))


def wholes(arrays):
    return [whole(a.shape) for a in arrays]


BIG = pltpu.CompilerParams(vmem_limit_bytes=24 * 2**20)
SMALL = pltpu.CompilerParams(vmem_limit_bytes=12 * 2**20)


def rotated_kernel(side_ref, m_ref, v_ref, l_ref, r_ref, ql_ref, qr_ref, *outs):
    rot_ref, second_ref, power_ref = outs
    for k in range(2):
        left = ql_ref[0, k]
        right = qr_ref[0, k]
        half = times_low(m_ref[0, k].T, left)
        rot_ref[k] = 0.95 * low_times(right.T, half, MM)
        second_ref[k] = 0.95 * v_ref[0, k].T
        power_ref[2 * k] = 0.95 * times_low(l_ref[0, k], left)
        power_ref[2 * k + 1] = 0.95 * times_low(r_ref[0, k], right)


def direction_kernel(side_ref, a_ref, b_ref, c_ref, d_ref, m_ref, v_ref, *rest):
    ql_ref, qr_ref, dir_ref, grad_ref = rest
    pair = range(2)
    lefts = [ql_ref[0, k] for k in pair]
    rights = [qr_ref[0, k] for k in pair]
    turned = [right.T for right in rights]
    grads = [above(a_ref[k] + b_ref[k], c_ref[k] + d_ref[k]) for k in pair]
    rots = [times_low(grads[k], lefts[k]) for k in pair]
    rots = [low_times(turned[k], rots[k], MM) for k in pair]
    scaled = []
    for k in pair:
        moment_rot = m_ref[k] + 0.05 * rots[k]
        second = v_ref[k] + 0.05 * rots[k] * rots[k]
        scaled.append(moment_rot / (jnp.sqrt(second) + 1e-08))
    outs = [low_times(rights[k], scaled[k], MM) for k in pair]
    outs = [low_times(lefts[k], outs[k], MT) for k in pair]
    for k in pair:
        dir_ref[k] = outs[k].astype(dir_ref.dtype)
        grad_ref[k] = grads[k]


def slots_of(*arrays):
    tile = arrays[0].shape[-1]
    return [pl.BlockSpec((1, 2, tile, tile), lambda i, s: (0, s[0], 0, 0)) for _ in arrays]


def on_slots(kernel, side, plain, slotted, outs, flops):
    return pl.pallas_call(
        kernel,
        out_shape=tuple(outs),
        grid_spec=pltpu.PrefetchScalarGridSpec(
            num_scalar_prefetch=1,
            grid=(1,),
            in_specs=wholes(plain) + slots_of(*slotted),
            out_specs=tuple(wholes(outs)),
        ),
        compiler_params=SMALL,
        cost_estimate=pl.CostEstimate(flops=flops, bytes_accessed=800_000, transcendentals=0),
        name=kernel.__name__.removesuffix("_kernel"),
    )(side, *plain, *slotted)


def sweep(values):
    pairs = [halves(y) for y in values]
    grams = [halves(pair_product(p, p, MT)) for p in pairs]
    return tuple(
        1.5 * y - 0.5 * pair_product(g, p, MM) for y, g, p in zip(values, grams, pairs)
    )


def sweeps(values, count):
    return lax.fori_loop(0, count, lambda i, v: sweep(v), tuple(values), unroll=2)


STAGES = (5, NS_STEPS - 5)


def refresh_kernel(side_ref, g_ref, power_ref, ql_ref, qr_ref, iter_ref):
    values = []
    for k in range(2):
        turned = g_ref[k]
        grad = turned.T
        for i, rows, columns, basis in ((0, grad, turned, ql_ref), (1, turned, grad, qr_ref)):
            half = times_low(columns, basis[0, k])
            power = power_ref[2 * k + i] + 0.05 * pair_product(halves(rows), halves(half), MM)
            values.append((power / jnp.sqrt(jnp.sum(power * power) + 1e-06)).T)
    for i, y in enumerate(sweeps(values, STAGES[0])):
        iter_ref[i] = y


def finish_kernel(iter_ref, out_ref):
    for i, y in enumerate(sweeps([iter_ref[i] for i in range(4)], STAGES[1])):
        out_ref[i] = y.T.astype(out_ref.dtype)


def sweeping(kernel, values, dtype, count):
    tile = values.shape[-1]
    return pl.pallas_call(
        kernel,
        out_shape=jax.ShapeDtypeStruct(values.shape, dtype),
        compiler_params=SMALL,
        cost_estimate=pl.CostEstimate(
            flops=4 * 2 * count * 4 * 2 * tile**3, bytes_accessed=400_000, transcendentals=0
        ),
        name=kernel.__name__.removesuffix("_kernel"),
    )(values)


def place_tiles(col_tiles, entries, table_ref, sources, out, sems):
    tile = sources[0].shape[-1]
    copies = []
    for entry, source in zip(entries, sources):
        for i in range(source.shape[0]):
            block = table_ref[entry + i]
            rows = pl.ds(pl.multiple_of(block // col_tiles * tile, tile), tile)
            columns = pl.ds(pl.multiple_of(block % col_tiles * tile, tile), tile)
            copies.append(
                pltpu.make_async_copy(source.at[i], out.at[rows, columns], sems.at[len(copies)])
            )
            copies[-1].start()
    return copies


def begin_kernel(col_tiles, entries, table_ref, place_ref, own_ref, sib_ref, *refs):
    sources = refs[:-4]
    out, left, right, sems = refs[-4:]
    copies = place_tiles(col_tiles, entries, table_ref, sources, out, sems)
    core = place_ref[1]
    for source, first in ((own_ref, 2 * core), (sib_ref, 2 - 2 * core)):
        for k in range(2):
            for i, target in enumerate((left, right)):
                copies.append(
                    pltpu.make_async_copy(
                        source.at[2 * k + i], target.at[0, first + k], sems.at[len(copies)]
                    )
                )
                copies[-1].start()
    for copy in copies:
        copy.wait()


def more_kernel(col_tiles, entries, table_ref, *refs):
    out, sems = refs[-2:]
    for copy in place_tiles(col_tiles, entries, table_ref, refs[:-3], out, sems):
        copy.wait()


def place_more(update, table, col_tiles, entries, sources):
    count = sum(x.shape[0] for x in sources)
    return pl.pallas_call(
        functools.partial(more_kernel, col_tiles, entries),
        out_shape=jax.ShapeDtypeStruct(update.shape, update.dtype),
        in_specs=[SMEM] + [VMEM] * len(sources) + [HBM],
        out_specs=HBM,
        scratch_shapes=[pltpu.SemaphoreType.DMA((count,))],
        input_output_aliases={1 + len(sources): 0},
        compiler_params=SMALL,
        cost_estimate=pl.CostEstimate(flops=0, bytes_accessed=1_000_000, transcendentals=0),
        name="more",
    )(table, *sources, update)


def per_device_dealt(
    owners,
    features,
    kv_cotangent,
    owner_of_block,
    first_moment,
    second_moment,
    left_stat,
    right_stat,
    left_basis,
    right_basis,
):
    tile = left_basis.shape[-1]
    capacity = left_basis.shape[1]
    rows, d_win = features.shape
    width = kv_cotangent.shape[1]
    col_tiles = width // tile
    here = lax.axis_index("dp")
    core = lax.axis_index("inner")
    place = jnp.stack([here, core]).astype(jnp.int32)
    side = core.reshape(1).astype(jnp.int32)
    orders = stream_offsets(owners)[0]
    near = owners // 2
    bits = len(orders[0])

    f_sib = swap_along(features, "inner", 2, 1)
    kv_sib = swap_along(kv_cotangent, "inner", 2, 1)
    part = jax.ShapeDtypeStruct((near, tile - EDGE, tile), jnp.float32)
    edge = jax.ShapeDtypeStruct((owners, EDGE, tile), jnp.float32)
    early = jax.ShapeDtypeStruct((near, EDGE, tile), jnp.float32)
    f32_pair = jax.ShapeDtypeStruct((2, tile, tile), jnp.float32)
    table, own_rows = pl.pallas_call(
        functools.partial(table_kernel, owners, capacity),
        out_shape=(
            jax.ShapeDtypeStruct((4 * owners,), jnp.int32),
            jax.ShapeDtypeStruct((width, rows), jnp.bfloat16),
        ),
        in_specs=[SMEM, SMEM, VMEM],
        out_specs=(SMEM, VMEM),
        compiler_params=SMALL,
        scratch_shapes=[
            pltpu.SMEM((owners,), jnp.int32),
            pltpu.SMEM((owners * capacity,), jnp.int32),
        ],
        cost_estimate=pl.CostEstimate(flops=0, bytes_accessed=1_000_000, transcendentals=0),
        name="table",
    )(place, owner_of_block, kv_cotangent)

    def tiles(kernel, outs, inputs, share):
        return pl.pallas_call(
            kernel,
            out_shape=outs,
            grid=(1,),
            in_specs=[SMEM] + wholes(inputs),
            out_specs=tuple(wholes(outs)),
            compiler_params=BIG,
            cost_estimate=pl.CostEstimate(
                flops=share * owners * 2 * tile * tile * 2 * rows,
                bytes_accessed=share * 1_700_000,
                transcendentals=0,
            ),
            name="tiles",
        )(table, *inputs)

    sent_a, early_a, sib_rows = tiles(
        functools.partial(sent_kernel, owners, 0),
        (part, early, jax.ShapeDtypeStruct((width, rows), jnp.bfloat16)),
        (features, f_sib, own_rows, kv_sib),
        1,
    )
    got_a = swap_along(sent_a, "dp", owners, 1 << orders[0][0])
    sent_b, early_b = tiles(
        functools.partial(sent_kernel, owners, 1),
        (part, early),
        (features, f_sib, own_rows, sib_rows),
        1,
    )
    got_b = swap_along(sent_b, "dp", owners, 1 << orders[1][0])
    kept_a, kept_b, kept_c, sent_c = tiles(
        functools.partial(kept_kernel, owners),
        (part, part, edge, edge),
        (features, f_sib, own_rows, sib_rows, early_a, early_b),
        2,
    )
    got_c = swap_along(sent_c, "dp", owners, 1 << orders[2][0])
    quad = jax.ShapeDtypeStruct((4, tile, tile), jnp.float32)
    moment_rot, second, power = on_slots(
        rotated_kernel,
        side,
        (),
        (first_moment, second_moment, left_stat, right_stat, left_basis, right_basis),
        (f32_pair, f32_pair, quad),
        16 * 2 * tile**3,
    )

    def halved(kept, got):
        half = kept.shape[0] // 2
        return kept[:half] + got[:half], kept[half:] + got[half:]

    def after(values, *needed):
        return lax.optimization_barrier((values, *needed))[0]

    def edges_on(step, kept, got):
        kept, sent = halved(kept, got)
        return kept, sent, swap_along(sent, "dp", owners, 1 << orders[2][step])

    kept_c, sent_c, got_c = edges_on(1, kept_c, got_c)
    kept_a, sent_a = halved(kept_a, got_a)
    kept_b, sent_b = halved(kept_b, got_b)
    got_a = swap_along(sent_a, "dp", owners, 1 << orders[0][1])
    got_b = swap_along(sent_b, "dp", owners, 1 << orders[1][1])
    kept = jnp.stack([kept_a, kept_b], axis=1)
    got = jnp.stack([got_a, got_b], axis=1)
    for step in range(2, bits):
        kept, sent = halved(kept, got)
        if step > 2:
            sent = after(sent, got_c)
            kept_c, sent_c, got_c = edges_on(step - 1, kept_c, got_c)
        if step == bits - 1:
            sent, kept = sent[0], kept[0]
        got = swap_along(sent, "dp", owners, 1 << orders[0][step])
    kept_c, sent_c, got_c = edges_on(bits - 1, kept_c, got_c)
    direction, grads = on_slots(
        direction_kernel,
        side,
        (kept, got, kept_c, got_c, moment_rot, second),
        (left_basis, right_basis),
        (jax.ShapeDtypeStruct(f32_pair.shape, jnp.bfloat16), f32_pair),
        16 * 2 * tile**3,
    )

    high = owners // 4
    tiles = []
    for p in range(high):
        offset = sum(((p >> (bits - 3 - i)) & 1) << bit for i, bit in enumerate(orders[0][2:]))
        tiles.append(swap_along(direction, "dp", owners, offset) if offset else direction)
    values = on_slots(
        refresh_kernel,
        side,
        (grads, power),
        (left_basis, right_basis),
        (quad,),
        4 * (4 + 2 * STAGES[0]) * 4 * 2 * tile**3,
    )[0]
    mine = [jnp.stack([t[stream] for t in tiles]) for stream in range(2)]
    mine, values = lax.optimization_barrier((mine, values))
    other = [swap_along(m, "dp", owners, 1 << order[1]) for m, order in zip(mine, orders)]
    fresh = sweeping(finish_kernel, values, jnp.bfloat16, STAGES[1])
    mine = [jnp.concatenate(both, axis=0) for both in zip(mine, other)]
    mine, fresh = lax.optimization_barrier((mine, fresh))
    other = [swap_along(m, "dp", owners, 1 << order[0]) for m, order in zip(mine, orders)]
    fresh_sib = swap_along(fresh, "inner", 2, 1)
    basis = jax.ShapeDtypeStruct(left_basis.shape, left_basis.dtype)
    update, new_left, new_right = pl.pallas_call(
        functools.partial(begin_kernel, col_tiles, (0, owners)),
        out_shape=(jax.ShapeDtypeStruct((d_win, width), jnp.bfloat16), basis, basis),
        in_specs=[SMEM, SMEM] + [VMEM] * 4,
        out_specs=(HBM, HBM, HBM),
        scratch_shapes=[pltpu.SemaphoreType.DMA((2 * near + 8,))],
        compiler_params=SMALL,
        cost_estimate=pl.CostEstimate(flops=0, bytes_accessed=800_000, transcendentals=0),
        name="begin",
    )(table, place, fresh, fresh_sib, *mine)
    update, other = lax.optimization_barrier((update, other))
    mine_sib = [swap_along(m, "inner", 2, 1) for m in mine]
    other_sib = [swap_along(o, "inner", 2, 1) for o in other]
    update = place_more(
        update,
        table,
        col_tiles,
        (2 * owners, 3 * owners, near, owners + near),
        mine_sib + other,
    )
    update = place_more(
        update, table, col_tiles, (2 * owners + near, 3 * owners + near), other_sib
    )
    return update, new_left, new_right


def solution(mesh):
    owners = mesh.shape["dp"]
    inner = mesh.shape["inner"]

    def per_device(*args):
        capacity = args[-1].shape[1]
        full = args[2].shape[0] == owners * capacity
        if full and inner == 2 and capacity == 4 and owners >= 8 and owners & (owners - 1) == 0:
            return per_device_dealt(owners, *args)
        return per_device_plain(*args)

    return jax.shard_map(
        per_device,
        mesh=mesh,
        in_specs=(
            P(("dp", "inner"), None),
            P(("dp", "inner"), None),
            P(),
            P("dp", None, None, None),
            P("dp", None, None, None),
            P("dp", None, None, None),
            P("dp", None, None, None),
            P("dp", None, None, None),
            P("dp", None, None, None),
        ),
        out_specs=(P(), P("dp", None, None, None), P("dp", None, None, None)),
        check_vma=False,
    )
```

```python
import functools

import jax
import jax.numpy as jnp
from jax import lax
from jax.experimental import pallas as pl
from jax.experimental.pallas import tpu as pltpu
from jax.sharding import PartitionSpec as P

NS_STEPS = 12


highest = lax.Precision.HIGHEST


def rotate_in(basis_left, matrix, basis_right):
    half = jnp.einsum("sji,sjk->sik", basis_left, matrix, precision=highest)
    return jnp.einsum("sij,sjk->sik", half, basis_right, precision=highest)


def rotate_out(basis_left, matrix, basis_right):
    half = jnp.einsum("sij,sjk->sik", basis_left, matrix, precision=highest)
    return jnp.einsum("sij,skj->sik", half, basis_right, precision=highest)


def orthogonalize(stat, basis):
    power = jnp.einsum("sij,sjk->sik", stat, basis, precision=highest)
    scale = jnp.sqrt(jnp.sum(power * power, axis=(1, 2), keepdims=True) + 1e-06)
    iterate = power / scale
    for sweep in range(NS_STEPS):
        gram = jnp.einsum("sji,sjk->sik", iterate, iterate, precision=highest)
        iterate = 1.5 * iterate - 0.5 * jnp.einsum("sij,sjk->sik", iterate, gram, precision=highest)
    return iterate


def soap_tiles(grads, first, second, stat_left, stat_right, basis_left, basis_right):
    rotated = rotate_in(basis_left, grads, basis_right)
    moment = 0.95 * first + 0.05 * grads
    moment_rot = rotate_in(basis_left, moment, basis_right)
    second_new = 0.95 * second + 0.05 * rotated * rotated
    direction = rotate_out(basis_left, moment_rot / (jnp.sqrt(second_new) + 1e-08), basis_right)
    left_new = 0.95 * stat_left + 0.05 * jnp.einsum("sij,skj->sik", grads, grads, precision=highest)
    right_new = 0.95 * stat_right + 0.05 * jnp.einsum(
        "sji,sjk->sik", grads, grads, precision=highest
    )
    return (direction, orthogonalize(left_new, basis_left), orthogonalize(right_new, basis_right))


def per_device_plain(
    features,
    kv_cotangent,
    owner_of_block,
    first_moment,
    second_moment,
    left_stat,
    right_stat,
    left_basis,
    right_basis,
):
    tile = left_basis.shape[-1]
    capacity = left_basis.shape[1]
    d_win = features.shape[1]
    width = kv_cotangent.shape[1]
    row_tiles = d_win // tile
    col_tiles = width // tile
    nblocks = owner_of_block.shape[0]
    owner_here = lax.axis_index("dp")
    block_ids = jnp.arange(nblocks, dtype=jnp.int32)
    same = owner_of_block[:, None] == owner_of_block[None, :]
    earlier = block_ids[None, :] < block_ids[:, None]
    slot = jnp.sum((same & earlier).astype(jnp.int32), axis=1)
    slot_ids = jnp.arange(capacity, dtype=jnp.int32)
    match = (owner_of_block[None, :] == owner_here) & (slot[None, :] == slot_ids[:, None])
    live = jnp.any(match, axis=1)
    which = jnp.sum(jnp.where(match, block_ids[None, :], 0), axis=1)
    row_start = which // col_tiles * tile
    col_start = which % col_tiles * tile
    partial_grad = lax.dot_general(
        features, kv_cotangent, (((0,), (0,)), ((), ())), preferred_element_type=jnp.float32
    )
    grad = lax.psum(partial_grad, ("dp", "inner"))
    fetched = [
        lax.dynamic_slice(grad, (row_start[slot_index], col_start[slot_index]), (tile, tile))
        for slot_index in range(capacity)
    ]
    grads = jnp.stack(fetched)
    basis_left = left_basis[0].astype(jnp.float32)
    basis_right = right_basis[0].astype(jnp.float32)
    direction, left_iter, right_iter = soap_tiles(
        grads,
        first_moment[0],
        second_moment[0],
        left_stat[0],
        right_stat[0],
        basis_left,
        basis_right,
    )
    direction_low = direction.astype(jnp.bfloat16)
    everyone = lax.all_gather(direction_low[None], "dp", axis=0, tiled=True)
    tiles = everyone[owner_of_block, slot]
    update = (
        tiles.reshape(row_tiles, col_tiles, tile, tile).transpose(0, 2, 1, 3).reshape(d_win, width)
    )
    keep = live[:, None, None]
    new_left = jnp.where(keep, left_iter.astype(jnp.bfloat16), left_basis[0])
    new_right = jnp.where(keep, right_iter.astype(jnp.bfloat16), right_basis[0])
    return (update, new_left[None], new_right[None])


MM = ((1,), (0,))
MT = ((1,), (1,))
TM = ((0,), (0,))


def swap_along(values, axis, size, bit):
    return lax.ppermute(values, axis, [(i, i ^ bit) for i in range(size)])


def dot(left, right, dims):
    return lax.dot_general(left, right, (dims, ((), ())), preferred_element_type=jnp.float32)


def halves(x):
    high = x.astype(jnp.bfloat16)
    return high, (x - high.astype(jnp.float32)).astype(jnp.bfloat16)


def beside(a, b):
    return jnp.concatenate([a, b], axis=1)


def above(a, b):
    return jnp.concatenate([a, b], axis=0)


def folded(both):
    n = both.shape[1] // 2
    return both[:, :n] + both[:, n:]


def pair_product(left, right, dims):
    if dims == TM:
        rows = above(*left)
    else:
        rows = beside(*left)
    if dims == MT:
        return folded(dot(rows, above(beside(right[0], right[0]), beside(right[1], right[1])), MT))
    return folded(dot(rows, above(beside(*right), beside(*right)), dims))


def low_times(low, x, dims):
    high, rest = halves(x)
    if dims == MT:
        return dot(beside(low, low), beside(high, rest), MT)
    return dot(beside(low, low), above(high, rest), MM)


def times_low(x, low):
    high, rest = halves(x)
    return dot(beside(high, rest), above(low, low), MM)


def stream_offsets(owners):
    bits = owners.bit_length() - 1
    highs = list(range(2, bits))
    orders = ([0, 1] + highs, [1, 0] + highs, highs + [0, 1])
    offsets = [
        [sum(((p >> (bits - 1 - i)) & 1) << bit for i, bit in enumerate(order)) for p in range(owners)]
        for order in orders
    ]
    return orders, offsets


def table_kernel(owners, capacity, place_ref, owner_ref, kv_ref, *rest):
    table_ref, own_rows, count, held = rest
    own_rows[...] = kv_ref[...].T

    for o in range(owners):
        count[o] = 0

    def enter(b, carry):
        o = owner_ref[b]
        s = count[o]
        count[o] = s + 1
        held[o * capacity + s] = b
        return carry

    lax.fori_loop(0, owners * capacity, enter, 0, unroll=8)
    here, core = place_ref[0], place_ref[1]
    offsets = stream_offsets(owners)[1]
    for side in range(2):
        first_slot = 2 * (core ^ side)
        for stream in range(2):
            for p in range(owners):
                entry = (side * 2 + stream) * owners + p
                table_ref[entry] = held[(here ^ offsets[stream][p]) * capacity + first_slot + stream]


EDGE = 32


def tiles_kernel(owners, first, table_ref, f_own, f_sib, own_rows, kv_sib, *rest):
    sib_rows = rest[-1]
    out_a, out_b = rest[-5:-3] if first == 0 else rest[:2]
    tile = out_a.shape[-1]
    body = tile - EDGE
    near = owners // 2
    col_tiles = own_rows.shape[0] // tile
    offsets = stream_offsets(owners)[1]
    sib_rows[...] = kv_sib[...].T
    for stream, out in enumerate((out_a, out_b)):
        for i in range(near):
            block = table_ref[stream * owners + first + i]
            at = pl.ds(pl.multiple_of(block // col_tiles * tile, tile), tile)
            cots = pl.ds(pl.multiple_of(block % col_tiles * tile, tile), tile)
            total = dot(own_rows[cots, :], f_own[:, at], MM) + dot(
                sib_rows[cots, :], f_sib[:, at], MM
            )
            out[i] = total[:body]
            place = 2 * offsets[2].index(offsets[stream][first + i]) + stream
            if first:
                rest[2][place] = total[body:]
            elif place < owners:
                rest[-3][place] = total[body:]
            else:
                rest[-2][place - owners] = total[body:]
            if first == 0:
                place = 2 * offsets[2].index(offsets[stream][near + i]) + stream
                if place < owners:
                    rest[-3][place] = rest[0][place]
                else:
                    rest[-2][place - owners] = rest[0][place]


SMEM = pl.BlockSpec(memory_space=pltpu.SMEM)
HBM = pl.BlockSpec(memory_space=pltpu.HBM)
VMEM = pl.BlockSpec(memory_space=pltpu.VMEM)


def whole(shape):
    return pl.BlockSpec(shape, lambda *g: (0,) * len(shape))


def wholes(arrays):
    return [whole(a.shape) for a in arrays]


BIG = pltpu.CompilerParams(vmem_limit_bytes=24 * 2**20)
SMALL = pltpu.CompilerParams(vmem_limit_bytes=12 * 2**20)


def rotated_kernel(side_ref, m_ref, v_ref, l_ref, r_ref, ql_ref, qr_ref, *outs):
    rot_ref, second_ref, power_ref = outs
    for k in range(2):
        left = ql_ref[0, k]
        right = qr_ref[0, k]
        half = times_low(m_ref[0, k].T, left)
        rot_ref[k] = 0.95 * low_times(right.T, half, MM)
        second_ref[k] = 0.95 * v_ref[0, k].T
        power_ref[2 * k] = 0.95 * times_low(l_ref[0, k], left)
        power_ref[2 * k + 1] = 0.95 * times_low(r_ref[0, k], right)


def direction_kernel(side_ref, a_ref, b_ref, c_ref, d_ref, m_ref, v_ref, *rest):
    ql_ref, qr_ref, dir_ref, grad_ref = rest
    pair = range(2)
    lefts = [ql_ref[0, k] for k in pair]
    rights = [qr_ref[0, k] for k in pair]
    turned = [right.T for right in rights]
    grads = [above(a_ref[k] + b_ref[k], c_ref[k] + d_ref[k]) for k in pair]
    rots = [times_low(grads[k], lefts[k]) for k in pair]
    rots = [low_times(turned[k], rots[k], MM) for k in pair]
    scaled = []
    for k in pair:
        moment_rot = m_ref[k] + 0.05 * rots[k]
        second = v_ref[k] + 0.05 * rots[k] * rots[k]
        scaled.append(moment_rot / (jnp.sqrt(second) + 1e-08))
    outs = [low_times(rights[k], scaled[k], MM) for k in pair]
    outs = [low_times(lefts[k], outs[k], MT) for k in pair]
    for k in pair:
        dir_ref[k] = outs[k].astype(dir_ref.dtype)
        grad_ref[k] = grads[k]


def slots_of(*arrays):
    tile = arrays[0].shape[-1]
    return [pl.BlockSpec((1, 2, tile, tile), lambda i, s: (0, s[0], 0, 0)) for _ in arrays]


def on_slots(kernel, side, plain, slotted, outs, flops):
    return pl.pallas_call(
        kernel,
        out_shape=tuple(outs),
        grid_spec=pltpu.PrefetchScalarGridSpec(
            num_scalar_prefetch=1,
            grid=(1,),
            in_specs=wholes(plain) + slots_of(*slotted),
            out_specs=tuple(wholes(outs)),
        ),
        compiler_params=SMALL,
        cost_estimate=pl.CostEstimate(flops=flops, bytes_accessed=800_000, transcendentals=0),
        name=kernel.__name__.removesuffix("_kernel"),
    )(side, *plain, *slotted)


def sweep(values):
    pairs = [halves(y) for y in values]
    grams = [halves(pair_product(p, p, MT)) for p in pairs]
    return tuple(
        1.5 * y - 0.5 * pair_product(g, p, MM) for y, g, p in zip(values, grams, pairs)
    )


def sweeps(values, count):
    return lax.fori_loop(0, count, lambda i, v: sweep(v), tuple(values), unroll=2)


STAGES = (5, NS_STEPS - 5)


def refresh_kernel(side_ref, g_ref, power_ref, ql_ref, qr_ref, iter_ref):
    values = []
    for k in range(2):
        turned = g_ref[k]
        grad = turned.T
        for i, rows, columns, basis in ((0, grad, turned, ql_ref), (1, turned, grad, qr_ref)):
            half = times_low(columns, basis[0, k])
            power = power_ref[2 * k + i] + 0.05 * pair_product(halves(rows), halves(half), MM)
            values.append((power / jnp.sqrt(jnp.sum(power * power) + 1e-06)).T)
    for i, y in enumerate(sweeps(values, STAGES[0])):
        iter_ref[i] = y


def finish_kernel(iter_ref, out_ref):
    for i, y in enumerate(sweeps([iter_ref[i] for i in range(4)], STAGES[1])):
        out_ref[i] = y.T.astype(out_ref.dtype)


def sweeping(kernel, values, dtype, count):
    tile = values.shape[-1]
    return pl.pallas_call(
        kernel,
        out_shape=jax.ShapeDtypeStruct(values.shape, dtype),
        compiler_params=SMALL,
        cost_estimate=pl.CostEstimate(
            flops=4 * 2 * count * 4 * 2 * tile**3, bytes_accessed=400_000, transcendentals=0
        ),
        name=kernel.__name__.removesuffix("_kernel"),
    )(values)


def place_tiles(col_tiles, entries, table_ref, sources, out, sems):
    tile = sources[0].shape[-1]
    copies = []
    for entry, source in zip(entries, sources):
        for i in range(source.shape[0]):
            block = table_ref[entry + i]
            rows = pl.ds(pl.multiple_of(block // col_tiles * tile, tile), tile)
            columns = pl.ds(pl.multiple_of(block % col_tiles * tile, tile), tile)
            copies.append(
                pltpu.make_async_copy(source.at[i], out.at[rows, columns], sems.at[len(copies)])
            )
            copies[-1].start()
    return copies


def begin_kernel(col_tiles, entries, table_ref, place_ref, own_ref, sib_ref, *refs):
    sources = refs[:-4]
    out, left, right, sems = refs[-4:]
    copies = place_tiles(col_tiles, entries, table_ref, sources, out, sems)
    core = place_ref[1]
    for source, first in ((own_ref, 2 * core), (sib_ref, 2 - 2 * core)):
        for k in range(2):
            for i, target in enumerate((left, right)):
                copies.append(
                    pltpu.make_async_copy(
                        source.at[2 * k + i], target.at[0, first + k], sems.at[len(copies)]
                    )
                )
                copies[-1].start()
    for copy in copies:
        copy.wait()


def more_kernel(col_tiles, entries, table_ref, *refs):
    out, sems = refs[-2:]
    for copy in place_tiles(col_tiles, entries, table_ref, refs[:-3], out, sems):
        copy.wait()


def place_more(update, table, col_tiles, entries, sources):
    count = sum(x.shape[0] for x in sources)
    return pl.pallas_call(
        functools.partial(more_kernel, col_tiles, entries),
        out_shape=jax.ShapeDtypeStruct(update.shape, update.dtype),
        in_specs=[SMEM] + [VMEM] * len(sources) + [HBM],
        out_specs=HBM,
        scratch_shapes=[pltpu.SemaphoreType.DMA((count,))],
        input_output_aliases={1 + len(sources): 0},
        compiler_params=SMALL,
        cost_estimate=pl.CostEstimate(flops=0, bytes_accessed=1_000_000, transcendentals=0),
        name="more",
    )(table, *sources, update)


def per_device_dealt(
    owners,
    features,
    kv_cotangent,
    owner_of_block,
    first_moment,
    second_moment,
    left_stat,
    right_stat,
    left_basis,
    right_basis,
):
    tile = left_basis.shape[-1]
    capacity = left_basis.shape[1]
    rows, d_win = features.shape
    width = kv_cotangent.shape[1]
    col_tiles = width // tile
    here = lax.axis_index("dp")
    core = lax.axis_index("inner")
    place = jnp.stack([here, core]).astype(jnp.int32)
    side = core.reshape(1).astype(jnp.int32)
    orders = stream_offsets(owners)[0]
    near = owners // 2
    bits = len(orders[0])

    f_sib = swap_along(features, "inner", 2, 1)
    kv_sib = swap_along(kv_cotangent, "inner", 2, 1)
    flipped = pltpu.VMEM((width, rows), jnp.bfloat16)
    part = jax.ShapeDtypeStruct((near, tile - EDGE, tile), jnp.float32)
    edge = jax.ShapeDtypeStruct((owners, EDGE, tile), jnp.float32)
    edges = jax.ShapeDtypeStruct((2 * owners, EDGE, tile), jnp.float32)
    f32_pair = jax.ShapeDtypeStruct((2, tile, tile), jnp.float32)
    table, own_rows = pl.pallas_call(
        functools.partial(table_kernel, owners, capacity),
        out_shape=(
            jax.ShapeDtypeStruct((4 * owners,), jnp.int32),
            jax.ShapeDtypeStruct((width, rows), jnp.bfloat16),
        ),
        in_specs=[SMEM, SMEM, VMEM],
        out_specs=(SMEM, VMEM),
        compiler_params=SMALL,
        scratch_shapes=[
            pltpu.SMEM((owners,), jnp.int32),
            pltpu.SMEM((owners * capacity,), jnp.int32),
        ],
        cost_estimate=pl.CostEstimate(flops=0, bytes_accessed=1_000_000, transcendentals=0),
        name="table",
    )(place, owner_of_block, kv_cotangent)

    def tiles_from(first, outs, *more):
        inputs = (features, f_sib, own_rows, kv_sib, *more)
        return pl.pallas_call(
            functools.partial(tiles_kernel, owners, first),
            out_shape=outs,
            grid=(1,),
            in_specs=[SMEM] + wholes(inputs),
            out_specs=tuple(wholes(outs)),
            scratch_shapes=[flipped],
            compiler_params=BIG,
            cost_estimate=pl.CostEstimate(
                flops=2 * owners * 2 * tile * tile * 2 * rows,
                bytes_accessed=3_500_000,
                transcendentals=0,
            ),
            name="tiles",
        )(table, *inputs)

    sent_a, sent_b, early = tiles_from(near, (part, part, edges))
    got_a = swap_along(sent_a, "dp", owners, 1 << orders[0][0])
    got_b = swap_along(sent_b, "dp", owners, 1 << orders[1][0])
    kept_a, kept_b, kept_c, sent_c = tiles_from(0, (part, part, edge, edge), early)
    got_c = swap_along(sent_c, "dp", owners, 1 << orders[2][0])
    quad = jax.ShapeDtypeStruct((4, tile, tile), jnp.float32)
    moment_rot, second, power = on_slots(
        rotated_kernel,
        side,
        (),
        (first_moment, second_moment, left_stat, right_stat, left_basis, right_basis),
        (f32_pair, f32_pair, quad),
        16 * 2 * tile**3,
    )

    def halved(kept, got):
        half = kept.shape[0] // 2
        return kept[:half] + got[:half], kept[half:] + got[half:]

    def after(values, *needed):
        return lax.optimization_barrier((values, *needed))[0]

    def edges_on(step, kept, got):
        kept, sent = halved(kept, got)
        return kept, sent, swap_along(sent, "dp", owners, 1 << orders[2][step])

    kept_c, sent_c, got_c = edges_on(1, kept_c, got_c)
    kept_a, sent_a = halved(kept_a, got_a)
    kept_b, sent_b = halved(kept_b, got_b)
    got_a = swap_along(sent_a, "dp", owners, 1 << orders[0][1])
    got_b = swap_along(sent_b, "dp", owners, 1 << orders[1][1])
    kept = jnp.stack([kept_a, kept_b], axis=1)
    got = jnp.stack([got_a, got_b], axis=1)
    for step in range(2, bits):
        kept, sent = halved(kept, got)
        if step > 2:
            sent = after(sent, got_c)
            kept_c, sent_c, got_c = edges_on(step - 1, kept_c, got_c)
        if step == bits - 1:
            sent, kept = sent[0], kept[0]
        got = swap_along(sent, "dp", owners, 1 << orders[0][step])
    kept_c, sent_c, got_c = edges_on(bits - 1, kept_c, got_c)
    direction, grads = on_slots(
        direction_kernel,
        side,
        (kept, got, kept_c, got_c, moment_rot, second),
        (left_basis, right_basis),
        (jax.ShapeDtypeStruct(f32_pair.shape, jnp.bfloat16), f32_pair),
        16 * 2 * tile**3,
    )

    high = owners // 4
    tiles = []
    for p in range(high):
        offset = sum(((p >> (bits - 3 - i)) & 1) << bit for i, bit in enumerate(orders[0][2:]))
        tiles.append(swap_along(direction, "dp", owners, offset) if offset else direction)
    values = on_slots(
        refresh_kernel,
        side,
        (grads, power),
        (left_basis, right_basis),
        (quad,),
        4 * (4 + 2 * STAGES[0]) * 4 * 2 * tile**3,
    )[0]
    mine = [jnp.stack([t[stream] for t in tiles]) for stream in range(2)]
    mine, values = lax.optimization_barrier((mine, values))
    other = [swap_along(m, "dp", owners, 1 << order[1]) for m, order in zip(mine, orders)]
    fresh = sweeping(finish_kernel, values, jnp.bfloat16, STAGES[1])
    mine = [jnp.concatenate(both, axis=0) for both in zip(mine, other)]
    mine, fresh = lax.optimization_barrier((mine, fresh))
    other = [swap_along(m, "dp", owners, 1 << order[0]) for m, order in zip(mine, orders)]
    fresh_sib = swap_along(fresh, "inner", 2, 1)
    basis = jax.ShapeDtypeStruct(left_basis.shape, left_basis.dtype)
    update, new_left, new_right = pl.pallas_call(
        functools.partial(begin_kernel, col_tiles, (0, owners)),
        out_shape=(jax.ShapeDtypeStruct((d_win, width), jnp.bfloat16), basis, basis),
        in_specs=[SMEM, SMEM] + [VMEM] * 4,
        out_specs=(HBM, HBM, HBM),
        scratch_shapes=[pltpu.SemaphoreType.DMA((2 * near + 8,))],
        compiler_params=SMALL,
        cost_estimate=pl.CostEstimate(flops=0, bytes_accessed=800_000, transcendentals=0),
        name="begin",
    )(table, place, fresh, fresh_sib, *mine)
    update, other = lax.optimization_barrier((update, other))
    mine_sib = [swap_along(m, "inner", 2, 1) for m in mine]
    other_sib = [swap_along(o, "inner", 2, 1) for o in other]
    update = place_more(
        update,
        table,
        col_tiles,
        (2 * owners, 3 * owners, near, owners + near),
        mine_sib + other,
    )
    update = place_more(
        update, table, col_tiles, (2 * owners + near, 3 * owners + near), other_sib
    )
    return update, new_left, new_right


def solution(mesh):
    owners = mesh.shape["dp"]
    inner = mesh.shape["inner"]

    def per_device(*args):
        capacity = args[-1].shape[1]
        full = args[2].shape[0] == owners * capacity
        if full and inner == 2 and capacity == 4 and owners >= 8 and owners & (owners - 1) == 0:
            return per_device_dealt(owners, *args)
        return per_device_plain(*args)

    return jax.shard_map(
        per_device,
        mesh=mesh,
        in_specs=(
            P(("dp", "inner"), None),
            P(("dp", "inner"), None),
            P(),
            P("dp", None, None, None),
            P("dp", None, None, None),
            P("dp", None, None, None),
            P("dp", None, None, None),
            P("dp", None, None, None),
            P("dp", None, None, None),
        ),
        out_specs=(P(), P("dp", None, None, None), P("dp", None, None, None)),
        check_vma=False,
    )
```

```python
import functools

import jax
import jax.numpy as jnp
from jax import lax
from jax.experimental import pallas as pl
from jax.experimental.pallas import tpu as pltpu
from jax.sharding import PartitionSpec as P

NS_STEPS = 12


highest = lax.Precision.HIGHEST


def rotate_in(basis_left, matrix, basis_right):
    half = jnp.einsum("sji,sjk->sik", basis_left, matrix, precision=highest)
    return jnp.einsum("sij,sjk->sik", half, basis_right, precision=highest)


def rotate_out(basis_left, matrix, basis_right):
    half = jnp.einsum("sij,sjk->sik", basis_left, matrix, precision=highest)
    return jnp.einsum("sij,skj->sik", half, basis_right, precision=highest)


def orthogonalize(stat, basis):
    power = jnp.einsum("sij,sjk->sik", stat, basis, precision=highest)
    scale = jnp.sqrt(jnp.sum(power * power, axis=(1, 2), keepdims=True) + 1e-06)
    iterate = power / scale
    for sweep in range(NS_STEPS):
        gram = jnp.einsum("sji,sjk->sik", iterate, iterate, precision=highest)
        iterate = 1.5 * iterate - 0.5 * jnp.einsum("sij,sjk->sik", iterate, gram, precision=highest)
    return iterate


def soap_tiles(grads, first, second, stat_left, stat_right, basis_left, basis_right):
    rotated = rotate_in(basis_left, grads, basis_right)
    moment = 0.95 * first + 0.05 * grads
    moment_rot = rotate_in(basis_left, moment, basis_right)
    second_new = 0.95 * second + 0.05 * rotated * rotated
    direction = rotate_out(basis_left, moment_rot / (jnp.sqrt(second_new) + 1e-08), basis_right)
    left_new = 0.95 * stat_left + 0.05 * jnp.einsum("sij,skj->sik", grads, grads, precision=highest)
    right_new = 0.95 * stat_right + 0.05 * jnp.einsum(
        "sji,sjk->sik", grads, grads, precision=highest
    )
    return (direction, orthogonalize(left_new, basis_left), orthogonalize(right_new, basis_right))


def per_device_plain(
    features,
    kv_cotangent,
    owner_of_block,
    first_moment,
    second_moment,
    left_stat,
    right_stat,
    left_basis,
    right_basis,
):
    tile = left_basis.shape[-1]
    capacity = left_basis.shape[1]
    d_win = features.shape[1]
    width = kv_cotangent.shape[1]
    row_tiles = d_win // tile
    col_tiles = width // tile
    nblocks = owner_of_block.shape[0]
    owner_here = lax.axis_index("dp")
    block_ids = jnp.arange(nblocks, dtype=jnp.int32)
    same = owner_of_block[:, None] == owner_of_block[None, :]
    earlier = block_ids[None, :] < block_ids[:, None]
    slot = jnp.sum((same & earlier).astype(jnp.int32), axis=1)
    slot_ids = jnp.arange(capacity, dtype=jnp.int32)
    match = (owner_of_block[None, :] == owner_here) & (slot[None, :] == slot_ids[:, None])
    live = jnp.any(match, axis=1)
    which = jnp.sum(jnp.where(match, block_ids[None, :], 0), axis=1)
    row_start = which // col_tiles * tile
    col_start = which % col_tiles * tile
    partial_grad = lax.dot_general(
        features, kv_cotangent, (((0,), (0,)), ((), ())), preferred_element_type=jnp.float32
    )
    grad = lax.psum(partial_grad, ("dp", "inner"))
    fetched = [
        lax.dynamic_slice(grad, (row_start[slot_index], col_start[slot_index]), (tile, tile))
        for slot_index in range(capacity)
    ]
    grads = jnp.stack(fetched)
    basis_left = left_basis[0].astype(jnp.float32)
    basis_right = right_basis[0].astype(jnp.float32)
    direction, left_iter, right_iter = soap_tiles(
        grads,
        first_moment[0],
        second_moment[0],
        left_stat[0],
        right_stat[0],
        basis_left,
        basis_right,
    )
    direction_low = direction.astype(jnp.bfloat16)
    everyone = lax.all_gather(direction_low[None], "dp", axis=0, tiled=True)
    tiles = everyone[owner_of_block, slot]
    update = (
        tiles.reshape(row_tiles, col_tiles, tile, tile).transpose(0, 2, 1, 3).reshape(d_win, width)
    )
    keep = live[:, None, None]
    new_left = jnp.where(keep, left_iter.astype(jnp.bfloat16), left_basis[0])
    new_right = jnp.where(keep, right_iter.astype(jnp.bfloat16), right_basis[0])
    return (update, new_left[None], new_right[None])


MM = ((1,), (0,))
MT = ((1,), (1,))
TM = ((0,), (0,))


def swap_along(values, axis, size, bit):
    return lax.ppermute(values, axis, [(i, i ^ bit) for i in range(size)])


def dot(left, right, dims):
    return lax.dot_general(left, right, (dims, ((), ())), preferred_element_type=jnp.float32)


def halves(x):
    high = x.astype(jnp.bfloat16)
    return high, (x - high.astype(jnp.float32)).astype(jnp.bfloat16)


def beside(a, b):
    return jnp.concatenate([a, b], axis=1)


def above(a, b):
    return jnp.concatenate([a, b], axis=0)


def folded(both):
    n = both.shape[1] // 2
    return both[:, :n] + both[:, n:]


def pair_product(left, right, dims):
    if dims == TM:
        rows = above(*left)
    else:
        rows = beside(*left)
    if dims == MT:
        return folded(dot(rows, above(beside(right[0], right[0]), beside(right[1], right[1])), MT))
    return folded(dot(rows, above(beside(*right), beside(*right)), dims))


def low_times(low, x, dims):
    high, rest = halves(x)
    if dims == MT:
        return dot(beside(low, low), beside(high, rest), MT)
    return dot(beside(low, low), above(high, rest), MM)


def times_low(x, low):
    high, rest = halves(x)
    return dot(beside(high, rest), above(low, low), MM)


def stream_offsets(owners):
    bits = owners.bit_length() - 1
    highs = list(range(2, bits))
    orders = ([0, 1] + highs, [1, 0] + highs, highs + [0, 1])
    offsets = [
        [sum(((p >> (bits - 1 - i)) & 1) << bit for i, bit in enumerate(order)) for p in range(owners)]
        for order in orders
    ]
    return orders, offsets


def table_kernel(owners, capacity, place_ref, owner_ref, kv_ref, *rest):
    table_ref, own_rows, held = rest
    own_rows[...] = kv_ref[...].T


    def enter(b, counts):
        o = owner_ref[b]
        shift = 4 * (o & 7)
        low = o < 8
        s = (jnp.where(low, counts[0], counts[1]) >> shift) & 15
        held[o * capacity + s] = b
        one = jnp.int32(1) << shift
        return (
            counts[0] + jnp.where(low, one, 0),
            counts[1] + jnp.where(low, 0, one),
        )

    lax.fori_loop(0, owners * capacity, enter, (jnp.int32(0), jnp.int32(0)), unroll=16)
    here, core = place_ref[0], place_ref[1]
    offsets = stream_offsets(owners)[1]
    for side in range(2):
        first_slot = 2 * (core ^ side)
        for stream in range(2):
            for p in range(owners):
                entry = (side * 2 + stream) * owners + p
                table_ref[entry] = held[(here ^ offsets[stream][p]) * capacity + first_slot + stream]


EDGE = 32


def tiles_kernel(owners, first, table_ref, f_own, f_sib, own_rows, kv_sib, *rest):
    sib_rows = rest[-1]
    out_a, out_b = rest[-5:-3] if first == 0 else rest[:2]
    tile = out_a.shape[-1]
    body = tile - EDGE
    near = owners // 2
    col_tiles = own_rows.shape[0] // tile
    offsets = stream_offsets(owners)[1]
    sib_rows[...] = kv_sib[...].T
    for stream, out in enumerate((out_a, out_b)):
        for i in range(near):
            block = table_ref[stream * owners + first + i]
            at = pl.ds(pl.multiple_of(block // col_tiles * tile, tile), tile)
            cots = pl.ds(pl.multiple_of(block % col_tiles * tile, tile), tile)
            total = dot(own_rows[cots, :], f_own[:, at], MM) + dot(
                sib_rows[cots, :], f_sib[:, at], MM
            )
            out[i] = total[:body]
            place = 2 * offsets[2].index(offsets[stream][first + i]) + stream
            if first:
                rest[2][place] = total[body:]
            elif place < owners:
                rest[-3][place] = total[body:]
            else:
                rest[-2][place - owners] = total[body:]
            if first == 0:
                place = 2 * offsets[2].index(offsets[stream][near + i]) + stream
                if place < owners:
                    rest[-3][place] = rest[0][place]
                else:
                    rest[-2][place - owners] = rest[0][place]


SMEM = pl.BlockSpec(memory_space=pltpu.SMEM)
HBM = pl.BlockSpec(memory_space=pltpu.HBM)
VMEM = pl.BlockSpec(memory_space=pltpu.VMEM)


def whole(shape):
    return pl.BlockSpec(shape, lambda *g: (0,) * len(shape))


def wholes(arrays):
    return [whole(a.shape) for a in arrays]


BIG = pltpu.CompilerParams(vmem_limit_bytes=24 * 2**20)
SMALL = pltpu.CompilerParams(vmem_limit_bytes=12 * 2**20)


def rotated_kernel(side_ref, m_ref, v_ref, l_ref, r_ref, ql_ref, qr_ref, *outs):
    rot_ref, second_ref, power_ref = outs
    for k in range(2):
        left = ql_ref[0, k]
        right = qr_ref[0, k]
        half = times_low(m_ref[0, k].T, left)
        rot_ref[k] = 0.95 * low_times(right.T, half, MM)
        second_ref[k] = 0.95 * v_ref[0, k].T
        power_ref[2 * k] = 0.95 * times_low(l_ref[0, k], left)
        power_ref[2 * k + 1] = 0.95 * times_low(r_ref[0, k], right)


def direction_kernel(side_ref, a_ref, b_ref, c_ref, d_ref, m_ref, v_ref, *rest):
    ql_ref, qr_ref, dir_ref, grad_ref = rest
    pair = range(2)
    lefts = [ql_ref[0, k] for k in pair]
    rights = [qr_ref[0, k] for k in pair]
    turned = [right.T for right in rights]
    grads = [above(a_ref[k] + b_ref[k], c_ref[k] + d_ref[k]) for k in pair]
    rots = [times_low(grads[k], lefts[k]) for k in pair]
    rots = [low_times(turned[k], rots[k], MM) for k in pair]
    scaled = []
    for k in pair:
        moment_rot = m_ref[k] + 0.05 * rots[k]
        second = v_ref[k] + 0.05 * rots[k] * rots[k]
        scaled.append(moment_rot / (jnp.sqrt(second) + 1e-08))
    outs = [low_times(rights[k], scaled[k], MM) for k in pair]
    outs = [low_times(lefts[k], outs[k], MT) for k in pair]
    for k in pair:
        dir_ref[k] = outs[k].astype(dir_ref.dtype)
        grad_ref[k] = grads[k]


def slots_of(*arrays):
    tile = arrays[0].shape[-1]
    return [pl.BlockSpec((1, 2, tile, tile), lambda i, s: (0, s[0], 0, 0)) for _ in arrays]


def on_slots(kernel, side, plain, slotted, outs, flops):
    return pl.pallas_call(
        kernel,
        out_shape=tuple(outs),
        grid_spec=pltpu.PrefetchScalarGridSpec(
            num_scalar_prefetch=1,
            grid=(1,),
            in_specs=wholes(plain) + slots_of(*slotted),
            out_specs=tuple(wholes(outs)),
        ),
        compiler_params=SMALL,
        cost_estimate=pl.CostEstimate(flops=flops, bytes_accessed=800_000, transcendentals=0),
        name=kernel.__name__.removesuffix("_kernel"),
    )(side, *plain, *slotted)


def sweep(values):
    pairs = [halves(y) for y in values]
    grams = [halves(pair_product(p, p, MT)) for p in pairs]
    return tuple(
        1.5 * y - 0.5 * pair_product(g, p, MM) for y, g, p in zip(values, grams, pairs)
    )


def sweeps(values, count):
    return lax.fori_loop(0, count, lambda i, v: sweep(v), tuple(values), unroll=2)


STAGES = (5, NS_STEPS - 5)


def refresh_kernel(side_ref, g_ref, power_ref, ql_ref, qr_ref, iter_ref):
    values = []
    for k in range(2):
        turned = g_ref[k]
        grad = turned.T
        for i, rows, columns, basis in ((0, grad, turned, ql_ref), (1, turned, grad, qr_ref)):
            half = times_low(columns, basis[0, k])
            power = power_ref[2 * k + i] + 0.05 * pair_product(halves(rows), halves(half), MM)
            values.append((power / jnp.sqrt(jnp.sum(power * power) + 1e-06)).T)
    for i, y in enumerate(sweeps(values, STAGES[0])):
        iter_ref[i] = y


def finish_kernel(iter_ref, out_ref):
    for i, y in enumerate(sweeps([iter_ref[i] for i in range(4)], STAGES[1])):
        out_ref[i] = y.T.astype(out_ref.dtype)


def sweeping(kernel, values, dtype, count):
    tile = values.shape[-1]
    return pl.pallas_call(
        kernel,
        out_shape=jax.ShapeDtypeStruct(values.shape, dtype),
        compiler_params=SMALL,
        cost_estimate=pl.CostEstimate(
            flops=4 * 2 * count * 4 * 2 * tile**3, bytes_accessed=400_000, transcendentals=0
        ),
        name=kernel.__name__.removesuffix("_kernel"),
    )(values)


def place_tiles(col_tiles, entries, table_ref, sources, out, sems):
    tile = sources[0].shape[-1]
    copies = []
    for entry, source in zip(entries, sources):
        for i in range(source.shape[0]):
            block = table_ref[entry + i]
            rows = pl.ds(pl.multiple_of(block // col_tiles * tile, tile), tile)
            columns = pl.ds(pl.multiple_of(block % col_tiles * tile, tile), tile)
            copies.append(
                pltpu.make_async_copy(source.at[i], out.at[rows, columns], sems.at[len(copies)])
            )
            copies[-1].start()
    return copies


def begin_kernel(col_tiles, entries, table_ref, place_ref, own_ref, sib_ref, *refs):
    sources = refs[:-4]
    out, left, right, sems = refs[-4:]
    copies = place_tiles(col_tiles, entries, table_ref, sources, out, sems)
    core = place_ref[1]
    for source, first in ((own_ref, 2 * core), (sib_ref, 2 - 2 * core)):
        for k in range(2):
            for i, target in enumerate((left, right)):
                copies.append(
                    pltpu.make_async_copy(
                        source.at[2 * k + i], target.at[0, first + k], sems.at[len(copies)]
                    )
                )
                copies[-1].start()
    for copy in copies:
        copy.wait()


def more_kernel(col_tiles, entries, table_ref, *refs):
    out, sems = refs[-2:]
    for copy in place_tiles(col_tiles, entries, table_ref, refs[:-3], out, sems):
        copy.wait()


def place_more(update, table, col_tiles, entries, sources):
    count = sum(x.shape[0] for x in sources)
    return pl.pallas_call(
        functools.partial(more_kernel, col_tiles, entries),
        out_shape=jax.ShapeDtypeStruct(update.shape, update.dtype),
        in_specs=[SMEM] + [VMEM] * len(sources) + [HBM],
        out_specs=HBM,
        scratch_shapes=[pltpu.SemaphoreType.DMA((count,))],
        input_output_aliases={1 + len(sources): 0},
        compiler_params=SMALL,
        cost_estimate=pl.CostEstimate(flops=0, bytes_accessed=1_000_000, transcendentals=0),
        name="more",
    )(table, *sources, update)


def per_device_dealt(
    owners,
    features,
    kv_cotangent,
    owner_of_block,
    first_moment,
    second_moment,
    left_stat,
    right_stat,
    left_basis,
    right_basis,
):
    tile = left_basis.shape[-1]
    capacity = left_basis.shape[1]
    rows, d_win = features.shape
    width = kv_cotangent.shape[1]
    col_tiles = width // tile
    here = lax.axis_index("dp")
    core = lax.axis_index("inner")
    place = jnp.stack([here, core]).astype(jnp.int32)
    side = core.reshape(1).astype(jnp.int32)
    orders = stream_offsets(owners)[0]
    near = owners // 2
    bits = len(orders[0])

    f_sib = swap_along(features, "inner", 2, 1)
    kv_sib = swap_along(kv_cotangent, "inner", 2, 1)
    flipped = pltpu.VMEM((width, rows), jnp.bfloat16)
    part = jax.ShapeDtypeStruct((near, tile - EDGE, tile), jnp.float32)
    edge = jax.ShapeDtypeStruct((owners, EDGE, tile), jnp.float32)
    edges = jax.ShapeDtypeStruct((2 * owners, EDGE, tile), jnp.float32)
    f32_pair = jax.ShapeDtypeStruct((2, tile, tile), jnp.float32)
    table, own_rows = pl.pallas_call(
        functools.partial(table_kernel, owners, capacity),
        out_shape=(
            jax.ShapeDtypeStruct((4 * owners,), jnp.int32),
            jax.ShapeDtypeStruct((width, rows), jnp.bfloat16),
        ),
        in_specs=[SMEM, SMEM, VMEM],
        out_specs=(SMEM, VMEM),
        compiler_params=SMALL,
        scratch_shapes=[
            pltpu.SMEM((owners * capacity,), jnp.int32),
        ],
        cost_estimate=pl.CostEstimate(flops=0, bytes_accessed=1_000_000, transcendentals=0),
        name="table",
    )(place, owner_of_block, kv_cotangent)

    def tiles_from(first, outs, *more):
        inputs = (features, f_sib, own_rows, kv_sib, *more)
        return pl.pallas_call(
            functools.partial(tiles_kernel, owners, first),
            out_shape=outs,
            grid=(1,),
            in_specs=[SMEM] + wholes(inputs),
            out_specs=tuple(wholes(outs)),
            scratch_shapes=[flipped],
            compiler_params=BIG,
            cost_estimate=pl.CostEstimate(
                flops=2 * owners * 2 * tile * tile * 2 * rows,
                bytes_accessed=3_500_000,
                transcendentals=0,
            ),
            name="tiles",
        )(table, *inputs)

    sent_a, sent_b, early = tiles_from(near, (part, part, edges))
    got_a = swap_along(sent_a, "dp", owners, 1 << orders[0][0])
    got_b = swap_along(sent_b, "dp", owners, 1 << orders[1][0])
    kept_a, kept_b, kept_c, sent_c = tiles_from(0, (part, part, edge, edge), early)
    got_c = swap_along(sent_c, "dp", owners, 1 << orders[2][0])
    quad = jax.ShapeDtypeStruct((4, tile, tile), jnp.float32)
    moment_rot, second, power = on_slots(
        rotated_kernel,
        side,
        (),
        (first_moment, second_moment, left_stat, right_stat, left_basis, right_basis),
        (f32_pair, f32_pair, quad),
        16 * 2 * tile**3,
    )

    def halved(kept, got):
        half = kept.shape[0] // 2
        return kept[:half] + got[:half], kept[half:] + got[half:]

    def after(values, *needed):
        return lax.optimization_barrier((values, *needed))[0]

    def edges_on(step, kept, got):
        kept, sent = halved(kept, got)
        return kept, sent, swap_along(sent, "dp", owners, 1 << orders[2][step])

    kept_c, sent_c, got_c = edges_on(1, kept_c, got_c)
    kept_a, sent_a = halved(kept_a, got_a)
    kept_b, sent_b = halved(kept_b, got_b)
    got_a = swap_along(sent_a, "dp", owners, 1 << orders[0][1])
    got_b = swap_along(sent_b, "dp", owners, 1 << orders[1][1])
    kept = jnp.stack([kept_a, kept_b], axis=1)
    got = jnp.stack([got_a, got_b], axis=1)
    for step in range(2, bits):
        kept, sent = halved(kept, got)
        if step > 2:
            sent = after(sent, got_c)
            kept_c, sent_c, got_c = edges_on(step - 1, kept_c, got_c)
        if step == bits - 1:
            sent, kept = sent[0], kept[0]
        got = swap_along(sent, "dp", owners, 1 << orders[0][step])
    kept_c, sent_c, got_c = edges_on(bits - 1, kept_c, got_c)
    direction, grads = on_slots(
        direction_kernel,
        side,
        (kept, got, kept_c, got_c, moment_rot, second),
        (left_basis, right_basis),
        (jax.ShapeDtypeStruct(f32_pair.shape, jnp.bfloat16), f32_pair),
        16 * 2 * tile**3,
    )

    high = owners // 4
    tiles = []
    for p in range(high):
        offset = sum(((p >> (bits - 3 - i)) & 1) << bit for i, bit in enumerate(orders[0][2:]))
        tiles.append(swap_along(direction, "dp", owners, offset) if offset else direction)
    values = on_slots(
        refresh_kernel,
        side,
        (grads, power),
        (left_basis, right_basis),
        (quad,),
        4 * (4 + 2 * STAGES[0]) * 4 * 2 * tile**3,
    )[0]
    mine = [jnp.stack([t[stream] for t in tiles]) for stream in range(2)]
    mine, values = lax.optimization_barrier((mine, values))
    other = [swap_along(m, "dp", owners, 1 << order[1]) for m, order in zip(mine, orders)]
    fresh = sweeping(finish_kernel, values, jnp.bfloat16, STAGES[1])
    mine = [jnp.concatenate(both, axis=0) for both in zip(mine, other)]
    mine, fresh = lax.optimization_barrier((mine, fresh))
    other = [swap_along(m, "dp", owners, 1 << order[0]) for m, order in zip(mine, orders)]
    fresh_sib = swap_along(fresh, "inner", 2, 1)
    basis = jax.ShapeDtypeStruct(left_basis.shape, left_basis.dtype)
    update, new_left, new_right = pl.pallas_call(
        functools.partial(begin_kernel, col_tiles, (0, owners)),
        out_shape=(jax.ShapeDtypeStruct((d_win, width), jnp.bfloat16), basis, basis),
        in_specs=[SMEM, SMEM] + [VMEM] * 4,
        out_specs=(HBM, HBM, HBM),
        scratch_shapes=[pltpu.SemaphoreType.DMA((2 * near + 8,))],
        compiler_params=SMALL,
        cost_estimate=pl.CostEstimate(flops=0, bytes_accessed=800_000, transcendentals=0),
        name="begin",
    )(table, place, fresh, fresh_sib, *mine)
    update, other = lax.optimization_barrier((update, other))
    mine_sib = [swap_along(m, "inner", 2, 1) for m in mine]
    other_sib = [swap_along(o, "inner", 2, 1) for o in other]
    update = place_more(
        update,
        table,
        col_tiles,
        (2 * owners, 3 * owners, near, owners + near),
        mine_sib + other,
    )
    update = place_more(
        update, table, col_tiles, (2 * owners + near, 3 * owners + near), other_sib
    )
    return update, new_left, new_right


def solution(mesh):
    owners = mesh.shape["dp"]
    inner = mesh.shape["inner"]

    def per_device(*args):
        capacity = args[-1].shape[1]
        full = args[2].shape[0] == owners * capacity
        if full and inner == 2 and capacity == 4 and 8 <= owners <= 16 and owners & (owners - 1) == 0:
            return per_device_dealt(owners, *args)
        return per_device_plain(*args)

    return jax.shard_map(
        per_device,
        mesh=mesh,
        in_specs=(
            P(("dp", "inner"), None),
            P(("dp", "inner"), None),
            P(),
            P("dp", None, None, None),
            P("dp", None, None, None),
            P("dp", None, None, None),
            P("dp", None, None, None),
            P("dp", None, None, None),
            P("dp", None, None, None),
        ),
        out_specs=(P(), P("dp", None, None, None), P("dp", None, None, None)),
        check_vma=False,
    )
```

```python
import functools

import jax
import jax.numpy as jnp
from jax import lax
from jax.experimental import pallas as pl
from jax.experimental.pallas import tpu as pltpu
from jax.sharding import PartitionSpec as P

NS_STEPS = 12


highest = lax.Precision.HIGHEST


def rotate_in(basis_left, matrix, basis_right):
    half = jnp.einsum("sji,sjk->sik", basis_left, matrix, precision=highest)
    return jnp.einsum("sij,sjk->sik", half, basis_right, precision=highest)


def rotate_out(basis_left, matrix, basis_right):
    half = jnp.einsum("sij,sjk->sik", basis_left, matrix, precision=highest)
    return jnp.einsum("sij,skj->sik", half, basis_right, precision=highest)


def orthogonalize(stat, basis):
    power = jnp.einsum("sij,sjk->sik", stat, basis, precision=highest)
    scale = jnp.sqrt(jnp.sum(power * power, axis=(1, 2), keepdims=True) + 1e-06)
    iterate = power / scale
    for sweep in range(NS_STEPS):
        gram = jnp.einsum("sji,sjk->sik", iterate, iterate, precision=highest)
        iterate = 1.5 * iterate - 0.5 * jnp.einsum("sij,sjk->sik", iterate, gram, precision=highest)
    return iterate


def soap_tiles(grads, first, second, stat_left, stat_right, basis_left, basis_right):
    rotated = rotate_in(basis_left, grads, basis_right)
    moment = 0.95 * first + 0.05 * grads
    moment_rot = rotate_in(basis_left, moment, basis_right)
    second_new = 0.95 * second + 0.05 * rotated * rotated
    direction = rotate_out(basis_left, moment_rot / (jnp.sqrt(second_new) + 1e-08), basis_right)
    left_new = 0.95 * stat_left + 0.05 * jnp.einsum("sij,skj->sik", grads, grads, precision=highest)
    right_new = 0.95 * stat_right + 0.05 * jnp.einsum(
        "sji,sjk->sik", grads, grads, precision=highest
    )
    return (direction, orthogonalize(left_new, basis_left), orthogonalize(right_new, basis_right))


def per_device_plain(
    features,
    kv_cotangent,
    owner_of_block,
    first_moment,
    second_moment,
    left_stat,
    right_stat,
    left_basis,
    right_basis,
):
    tile = left_basis.shape[-1]
    capacity = left_basis.shape[1]
    d_win = features.shape[1]
    width = kv_cotangent.shape[1]
    row_tiles = d_win // tile
    col_tiles = width // tile
    nblocks = owner_of_block.shape[0]
    owner_here = lax.axis_index("dp")
    block_ids = jnp.arange(nblocks, dtype=jnp.int32)
    same = owner_of_block[:, None] == owner_of_block[None, :]
    earlier = block_ids[None, :] < block_ids[:, None]
    slot = jnp.sum((same & earlier).astype(jnp.int32), axis=1)
    slot_ids = jnp.arange(capacity, dtype=jnp.int32)
    match = (owner_of_block[None, :] == owner_here) & (slot[None, :] == slot_ids[:, None])
    live = jnp.any(match, axis=1)
    which = jnp.sum(jnp.where(match, block_ids[None, :], 0), axis=1)
    row_start = which // col_tiles * tile
    col_start = which % col_tiles * tile
    partial_grad = lax.dot_general(
        features, kv_cotangent, (((0,), (0,)), ((), ())), preferred_element_type=jnp.float32
    )
    grad = lax.psum(partial_grad, ("dp", "inner"))
    fetched = [
        lax.dynamic_slice(grad, (row_start[slot_index], col_start[slot_index]), (tile, tile))
        for slot_index in range(capacity)
    ]
    grads = jnp.stack(fetched)
    basis_left = left_basis[0].astype(jnp.float32)
    basis_right = right_basis[0].astype(jnp.float32)
    direction, left_iter, right_iter = soap_tiles(
        grads,
        first_moment[0],
        second_moment[0],
        left_stat[0],
        right_stat[0],
        basis_left,
        basis_right,
    )
    direction_low = direction.astype(jnp.bfloat16)
    everyone = lax.all_gather(direction_low[None], "dp", axis=0, tiled=True)
    tiles = everyone[owner_of_block, slot]
    update = (
        tiles.reshape(row_tiles, col_tiles, tile, tile).transpose(0, 2, 1, 3).reshape(d_win, width)
    )
    keep = live[:, None, None]
    new_left = jnp.where(keep, left_iter.astype(jnp.bfloat16), left_basis[0])
    new_right = jnp.where(keep, right_iter.astype(jnp.bfloat16), right_basis[0])
    return (update, new_left[None], new_right[None])


MM = ((1,), (0,))
MT = ((1,), (1,))
TM = ((0,), (0,))


def swap_along(values, axis, size, bit):
    return lax.ppermute(values, axis, [(i, i ^ bit) for i in range(size)])


def dot(left, right, dims):
    return lax.dot_general(left, right, (dims, ((), ())), preferred_element_type=jnp.float32)


def halves(x):
    high = x.astype(jnp.bfloat16)
    return high, (x - high.astype(jnp.float32)).astype(jnp.bfloat16)


def beside(a, b):
    return jnp.concatenate([a, b], axis=1)


def above(a, b):
    return jnp.concatenate([a, b], axis=0)


def folded(both):
    n = both.shape[1] // 2
    return both[:, :n] + both[:, n:]


def pair_product(left, right, dims):
    if dims == TM:
        rows = above(*left)
    else:
        rows = beside(*left)
    if dims == MT:
        return folded(dot(rows, above(beside(right[0], right[0]), beside(right[1], right[1])), MT))
    return folded(dot(rows, above(beside(*right), beside(*right)), dims))


def low_times(low, x, dims):
    high, rest = halves(x)
    if dims == MT:
        return dot(beside(low, low), beside(high, rest), MT)
    return dot(beside(low, low), above(high, rest), MM)


def times_low(x, low):
    high, rest = halves(x)
    return dot(beside(high, rest), above(low, low), MM)


def stream_offsets(owners):
    bits = owners.bit_length() - 1
    highs = list(range(2, bits))
    orders = ([0, 1] + highs, [1, 0] + highs, highs + [0, 1])
    offsets = [
        [sum(((p >> (bits - 1 - i)) & 1) << bit for i, bit in enumerate(order)) for p in range(owners)]
        for order in orders
    ]
    return orders, offsets


def table_kernel(owners, capacity, place_ref, owner_ref, kv_ref, *rest):
    table_ref, own_rows, held = rest
    own_rows[...] = kv_ref[...].T


    def enter(b, counts):
        o = owner_ref[b]
        shift = 4 * (o & 7)
        low = o < 8
        s = (jnp.where(low, counts[0], counts[1]) >> shift) & 15
        held[o * capacity + s] = b
        one = jnp.int32(1) << shift
        return (
            counts[0] + jnp.where(low, one, 0),
            counts[1] + jnp.where(low, 0, one),
        )

    lax.fori_loop(0, owners * capacity, enter, (jnp.int32(0), jnp.int32(0)), unroll=16)
    here, core = place_ref[0], place_ref[1]
    offsets = stream_offsets(owners)[1]
    for side in range(2):
        first_slot = 2 * (core ^ side)
        for stream in range(2):
            for p in range(owners):
                entry = (side * 2 + stream) * owners + p
                table_ref[entry] = held[(here ^ offsets[stream][p]) * capacity + first_slot + stream]


EDGE = 32


def tiles_kernel(owners, first, table_ref, f_own, f_sib, own_rows, kv_sib, *rest):
    sib_rows = rest[-1]
    out_a, out_b = rest[-5:-3] if first == 0 else rest[:2]
    tile = out_a.shape[-1]
    body = tile - EDGE
    near = owners // 2
    col_tiles = own_rows.shape[0] // tile
    offsets = stream_offsets(owners)[1]
    sib_rows[...] = kv_sib[...].T
    for stream, out in enumerate((out_a, out_b)):
        for i in range(near):
            block = table_ref[stream * owners + first + i]
            at = pl.ds(pl.multiple_of(block // col_tiles * tile, tile), tile)
            cots = pl.ds(pl.multiple_of(block % col_tiles * tile, tile), tile)
            total = dot(own_rows[cots, :], f_own[:, at], MM) + dot(
                sib_rows[cots, :], f_sib[:, at], MM
            )
            out[i] = total[:body]
            place = 2 * offsets[2].index(offsets[stream][first + i]) + stream
            if first:
                rest[2][place] = total[body:]
            elif place < owners:
                rest[-3][place] = total[body:]
            else:
                rest[-2][place - owners] = total[body:]
            if first == 0:
                place = 2 * offsets[2].index(offsets[stream][near + i]) + stream
                if place < owners:
                    rest[-3][place] = rest[0][place]
                else:
                    rest[-2][place - owners] = rest[0][place]


SMEM = pl.BlockSpec(memory_space=pltpu.SMEM)
HBM = pl.BlockSpec(memory_space=pltpu.HBM)
VMEM = pl.BlockSpec(memory_space=pltpu.VMEM)


def whole(shape):
    return pl.BlockSpec(shape, lambda *g: (0,) * len(shape))


def wholes(arrays):
    return [whole(a.shape) for a in arrays]


BIG = pltpu.CompilerParams(vmem_limit_bytes=24 * 2**20)
SMALL = pltpu.CompilerParams(vmem_limit_bytes=12 * 2**20)


def rotated_kernel(side_ref, m_ref, v_ref, l_ref, r_ref, ql_ref, qr_ref, *outs):
    rot_ref, second_ref, power_ref = outs
    for k in range(2):
        left = ql_ref[0, k]
        right = qr_ref[0, k]
        half = times_low(m_ref[0, k].T, left)
        rot_ref[k] = 0.95 * low_times(right.T, half, MM)
        second_ref[k] = 0.95 * v_ref[0, k].T
        power_ref[2 * k] = 0.95 * times_low(l_ref[0, k], left)
        power_ref[2 * k + 1] = 0.95 * times_low(r_ref[0, k], right)


def direction_kernel(side_ref, a_ref, b_ref, c_ref, d_ref, m_ref, v_ref, *rest):
    ql_ref, qr_ref, dir_ref, grad_ref = rest
    pair = range(2)
    lefts = [ql_ref[0, k] for k in pair]
    rights = [qr_ref[0, k] for k in pair]
    turned = [right.T for right in rights]
    grads = [above(a_ref[k] + b_ref[k], c_ref[k] + d_ref[k]) for k in pair]
    rots = [times_low(grads[k], lefts[k]) for k in pair]
    rots = [low_times(turned[k], rots[k], MM) for k in pair]
    scaled = []
    for k in pair:
        moment_rot = m_ref[k] + 0.05 * rots[k]
        second = v_ref[k] + 0.05 * rots[k] * rots[k]
        scaled.append(moment_rot / (jnp.sqrt(second) + 1e-08))
    outs = [low_times(rights[k], scaled[k], MM) for k in pair]
    outs = [low_times(lefts[k], outs[k], MT) for k in pair]
    for k in pair:
        dir_ref[k] = outs[k].astype(dir_ref.dtype)
        grad_ref[k] = grads[k]


def slots_of(*arrays):
    tile = arrays[0].shape[-1]
    return [pl.BlockSpec((1, 2, tile, tile), lambda i, s: (0, s[0], 0, 0)) for _ in arrays]


def on_slots(kernel, side, plain, slotted, outs, flops):
    return pl.pallas_call(
        kernel,
        out_shape=tuple(outs),
        grid_spec=pltpu.PrefetchScalarGridSpec(
            num_scalar_prefetch=1,
            grid=(1,),
            in_specs=wholes(plain) + slots_of(*slotted),
            out_specs=tuple(wholes(outs)),
        ),
        compiler_params=SMALL,
        cost_estimate=pl.CostEstimate(flops=flops, bytes_accessed=800_000, transcendentals=0),
        name=kernel.__name__.removesuffix("_kernel"),
    )(side, *plain, *slotted)


def sweep(values):
    pairs = [halves(y) for y in values]
    grams = [halves(pair_product(p, p, MT)) for p in pairs]
    return tuple(
        1.5 * y - 0.5 * pair_product(g, p, MM) for y, g, p in zip(values, grams, pairs)
    )


def sweeps(values, count):
    return lax.fori_loop(0, count, lambda i, v: sweep(v), tuple(values), unroll=2)


STAGES = (5, NS_STEPS - 5)


def refresh_kernel(side_ref, g_ref, power_ref, ql_ref, qr_ref, iter_ref):
    values = []
    for k in range(2):
        turned = g_ref[k]
        grad = turned.T
        for i, rows, columns, basis in ((0, grad, turned, ql_ref), (1, turned, grad, qr_ref)):
            half = times_low(columns, basis[0, k])
            power = power_ref[2 * k + i] + 0.05 * pair_product(halves(rows), halves(half), MM)
            values.append((power / jnp.sqrt(jnp.sum(power * power) + 1e-06)).T)
    for i, y in enumerate(sweeps(values, STAGES[0])):
        iter_ref[i] = y


def finish_kernel(iter_ref, out_ref):
    for i, y in enumerate(sweeps([iter_ref[i] for i in range(4)], STAGES[1])):
        out_ref[i] = y.T.astype(out_ref.dtype)


def sweeping(kernel, values, dtype, count):
    tile = values.shape[-1]
    return pl.pallas_call(
        kernel,
        out_shape=jax.ShapeDtypeStruct(values.shape, dtype),
        compiler_params=SMALL,
        cost_estimate=pl.CostEstimate(
            flops=4 * 2 * count * 4 * 2 * tile**3, bytes_accessed=400_000, transcendentals=0
        ),
        name=kernel.__name__.removesuffix("_kernel"),
    )(values)


def place_tiles(col_tiles, entries, table_ref, sources, out, sems):
    tile = sources[0].shape[-1]
    copies = []
    for entry, source in zip(entries, sources):
        for i in range(source.shape[0]):
            block = table_ref[entry + i]
            rows = pl.ds(pl.multiple_of(block // col_tiles * tile, tile), tile)
            columns = pl.ds(pl.multiple_of(block % col_tiles * tile, tile), tile)
            copies.append(
                pltpu.make_async_copy(source.at[i], out.at[rows, columns], sems.at[len(copies)])
            )
            copies[-1].start()
    return copies


def begin_kernel(col_tiles, entries, table_ref, place_ref, own_ref, sib_ref, *refs):
    sources = refs[:-4]
    out, left, right, sems = refs[-4:]
    copies = place_tiles(col_tiles, entries, table_ref, sources, out, sems)
    core = place_ref[1]
    for source, first in ((own_ref, 2 * core), (sib_ref, 2 - 2 * core)):
        for k in range(2):
            for i, target in enumerate((left, right)):
                copies.append(
                    pltpu.make_async_copy(
                        source.at[2 * k + i], target.at[0, first + k], sems.at[len(copies)]
                    )
                )
                copies[-1].start()
    for copy in copies:
        copy.wait()


def more_kernel(col_tiles, entries, table_ref, *refs):
    out, sems = refs[-2:]
    for copy in place_tiles(col_tiles, entries, table_ref, refs[:-3], out, sems):
        copy.wait()


def place_more(update, table, col_tiles, entries, sources):
    count = sum(x.shape[0] for x in sources)
    return pl.pallas_call(
        functools.partial(more_kernel, col_tiles, entries),
        out_shape=jax.ShapeDtypeStruct(update.shape, update.dtype),
        in_specs=[SMEM] + [VMEM] * len(sources) + [HBM],
        out_specs=HBM,
        scratch_shapes=[pltpu.SemaphoreType.DMA((count,))],
        input_output_aliases={1 + len(sources): 0},
        compiler_params=SMALL,
        cost_estimate=pl.CostEstimate(flops=0, bytes_accessed=1_000_000, transcendentals=0),
        name="more",
    )(table, *sources, update)


def per_device_dealt(
    owners,
    features,
    kv_cotangent,
    owner_of_block,
    first_moment,
    second_moment,
    left_stat,
    right_stat,
    left_basis,
    right_basis,
):
    tile = left_basis.shape[-1]
    capacity = left_basis.shape[1]
    rows, d_win = features.shape
    width = kv_cotangent.shape[1]
    col_tiles = width // tile
    here = lax.axis_index("dp")
    core = lax.axis_index("inner")
    place = jnp.stack([here, core]).astype(jnp.int32)
    side = core.reshape(1).astype(jnp.int32)
    orders = stream_offsets(owners)[0]
    near = owners // 2
    bits = len(orders[0])

    f_sib = swap_along(features, "inner", 2, 1)
    kv_sib = swap_along(kv_cotangent, "inner", 2, 1)
    f_own, kv_own, owner_own = [
        lax.ppermute(x, "inner", [(0, 0), (1, 1)])
        for x in (features, kv_cotangent, owner_of_block)
    ]
    flipped = pltpu.VMEM((width, rows), jnp.bfloat16)
    part = jax.ShapeDtypeStruct((near, tile - EDGE, tile), jnp.float32)
    edge = jax.ShapeDtypeStruct((owners, EDGE, tile), jnp.float32)
    edges = jax.ShapeDtypeStruct((2 * owners, EDGE, tile), jnp.float32)
    f32_pair = jax.ShapeDtypeStruct((2, tile, tile), jnp.float32)
    table, own_rows = pl.pallas_call(
        functools.partial(table_kernel, owners, capacity),
        out_shape=(
            jax.ShapeDtypeStruct((4 * owners,), jnp.int32),
            jax.ShapeDtypeStruct((width, rows), jnp.bfloat16),
        ),
        in_specs=[SMEM, SMEM, VMEM],
        out_specs=(SMEM, VMEM),
        compiler_params=SMALL,
        scratch_shapes=[
            pltpu.SMEM((owners * capacity,), jnp.int32),
        ],
        cost_estimate=pl.CostEstimate(flops=0, bytes_accessed=1_000_000, transcendentals=0),
        name="table",
    )(place, owner_own, kv_own)

    def tiles_from(first, outs, *more):
        inputs = (f_own, f_sib, own_rows, kv_sib, *more)
        return pl.pallas_call(
            functools.partial(tiles_kernel, owners, first),
            out_shape=outs,
            grid=(1,),
            in_specs=[SMEM] + wholes(inputs),
            out_specs=tuple(wholes(outs)),
            scratch_shapes=[flipped],
            compiler_params=BIG,
            cost_estimate=pl.CostEstimate(
                flops=2 * owners * 2 * tile * tile * 2 * rows,
                bytes_accessed=3_500_000,
                transcendentals=0,
            ),
            name="tiles",
        )(table, *inputs)

    sent_a, sent_b, early = tiles_from(near, (part, part, edges))
    got_a = swap_along(sent_a, "dp", owners, 1 << orders[0][0])
    got_b = swap_along(sent_b, "dp", owners, 1 << orders[1][0])
    kept_a, kept_b, kept_c, sent_c = tiles_from(0, (part, part, edge, edge), early)
    got_c = swap_along(sent_c, "dp", owners, 1 << orders[2][0])
    quad = jax.ShapeDtypeStruct((4, tile, tile), jnp.float32)
    moment_rot, second, power = on_slots(
        rotated_kernel,
        side,
        (),
        (first_moment, second_moment, left_stat, right_stat, left_basis, right_basis),
        (f32_pair, f32_pair, quad),
        16 * 2 * tile**3,
    )

    def halved(kept, got):
        half = kept.shape[0] // 2
        return kept[:half] + got[:half], kept[half:] + got[half:]

    def after(values, *needed):
        return lax.optimization_barrier((values, *needed))[0]

    def edges_on(step, kept, got):
        kept, sent = halved(kept, got)
        return kept, sent, swap_along(sent, "dp", owners, 1 << orders[2][step])

    kept_c, sent_c, got_c = edges_on(1, kept_c, got_c)
    kept_a, sent_a = halved(kept_a, got_a)
    kept_b, sent_b = halved(kept_b, got_b)
    got_a = swap_along(sent_a, "dp", owners, 1 << orders[0][1])
    got_b = swap_along(sent_b, "dp", owners, 1 << orders[1][1])
    kept = jnp.stack([kept_a, kept_b], axis=1)
    got = jnp.stack([got_a, got_b], axis=1)
    for step in range(2, bits):
        kept, sent = halved(kept, got)
        if step > 2:
            sent = after(sent, got_c)
            kept_c, sent_c, got_c = edges_on(step - 1, kept_c, got_c)
        if step == bits - 1:
            sent, kept = sent[0], kept[0]
        got = swap_along(sent, "dp", owners, 1 << orders[0][step])
    kept_c, sent_c, got_c = edges_on(bits - 1, kept_c, got_c)
    direction, grads = on_slots(
        direction_kernel,
        side,
        (kept, got, kept_c, got_c, moment_rot, second),
        (left_basis, right_basis),
        (jax.ShapeDtypeStruct(f32_pair.shape, jnp.bfloat16), f32_pair),
        16 * 2 * tile**3,
    )

    high = owners // 4
    tiles = []
    for p in range(high):
        offset = sum(((p >> (bits - 3 - i)) & 1) << bit for i, bit in enumerate(orders[0][2:]))
        tiles.append(swap_along(direction, "dp", owners, offset) if offset else direction)
    values = on_slots(
        refresh_kernel,
        side,
        (grads, power),
        (left_basis, right_basis),
        (quad,),
        4 * (4 + 2 * STAGES[0]) * 4 * 2 * tile**3,
    )[0]
    mine = [jnp.stack([t[stream] for t in tiles]) for stream in range(2)]
    mine, values = lax.optimization_barrier((mine, values))
    other = [swap_along(m, "dp", owners, 1 << order[1]) for m, order in zip(mine, orders)]
    fresh = sweeping(finish_kernel, values, jnp.bfloat16, STAGES[1])
    mine = [jnp.concatenate(both, axis=0) for both in zip(mine, other)]
    mine, fresh = lax.optimization_barrier((mine, fresh))
    other = [swap_along(m, "dp", owners, 1 << order[0]) for m, order in zip(mine, orders)]
    fresh_sib = swap_along(fresh, "inner", 2, 1)
    basis = jax.ShapeDtypeStruct(left_basis.shape, left_basis.dtype)
    update, new_left, new_right = pl.pallas_call(
        functools.partial(begin_kernel, col_tiles, (0, owners)),
        out_shape=(jax.ShapeDtypeStruct((d_win, width), jnp.bfloat16), basis, basis),
        in_specs=[SMEM, SMEM] + [VMEM] * 4,
        out_specs=(HBM, HBM, HBM),
        scratch_shapes=[pltpu.SemaphoreType.DMA((2 * near + 8,))],
        compiler_params=SMALL,
        cost_estimate=pl.CostEstimate(flops=0, bytes_accessed=800_000, transcendentals=0),
        name="begin",
    )(table, place, fresh, fresh_sib, *mine)
    update, other = lax.optimization_barrier((update, other))
    mine_sib = [swap_along(m, "inner", 2, 1) for m in mine]
    other_sib = [swap_along(o, "inner", 2, 1) for o in other]
    update = place_more(
        update,
        table,
        col_tiles,
        (2 * owners, 3 * owners, near, owners + near),
        mine_sib + other,
    )
    update = place_more(
        update, table, col_tiles, (2 * owners + near, 3 * owners + near), other_sib
    )
    return update, new_left, new_right


def solution(mesh):
    owners = mesh.shape["dp"]
    inner = mesh.shape["inner"]

    def per_device(*args):
        capacity = args[-1].shape[1]
        full = args[2].shape[0] == owners * capacity
        if full and inner == 2 and capacity == 4 and 8 <= owners <= 16 and owners & (owners - 1) == 0:
            return per_device_dealt(owners, *args)
        return per_device_plain(*args)

    return jax.shard_map(
        per_device,
        mesh=mesh,
        in_specs=(
            P(("dp", "inner"), None),
            P(("dp", "inner"), None),
            P(),
            P("dp", None, None, None),
            P("dp", None, None, None),
            P("dp", None, None, None),
            P("dp", None, None, None),
            P("dp", None, None, None),
            P("dp", None, None, None),
        ),
        out_specs=(P(), P("dp", None, None, None), P("dp", None, None, None)),
        check_vma=False,
    )
```

```python
import functools

import jax
import jax.numpy as jnp
from jax import lax
from jax.experimental import pallas as pl
from jax.experimental.pallas import tpu as pltpu
from jax.sharding import PartitionSpec as P

NS_STEPS = 12


highest = lax.Precision.HIGHEST


def rotate_in(basis_left, matrix, basis_right):
    half = jnp.einsum("sji,sjk->sik", basis_left, matrix, precision=highest)
    return jnp.einsum("sij,sjk->sik", half, basis_right, precision=highest)


def rotate_out(basis_left, matrix, basis_right):
    half = jnp.einsum("sij,sjk->sik", basis_left, matrix, precision=highest)
    return jnp.einsum("sij,skj->sik", half, basis_right, precision=highest)


def orthogonalize(stat, basis):
    power = jnp.einsum("sij,sjk->sik", stat, basis, precision=highest)
    scale = jnp.sqrt(jnp.sum(power * power, axis=(1, 2), keepdims=True) + 1e-06)
    iterate = power / scale
    for sweep in range(NS_STEPS):
        gram = jnp.einsum("sji,sjk->sik", iterate, iterate, precision=highest)
        iterate = 1.5 * iterate - 0.5 * jnp.einsum("sij,sjk->sik", iterate, gram, precision=highest)
    return iterate


def soap_tiles(grads, first, second, stat_left, stat_right, basis_left, basis_right):
    rotated = rotate_in(basis_left, grads, basis_right)
    moment = 0.95 * first + 0.05 * grads
    moment_rot = rotate_in(basis_left, moment, basis_right)
    second_new = 0.95 * second + 0.05 * rotated * rotated
    direction = rotate_out(basis_left, moment_rot / (jnp.sqrt(second_new) + 1e-08), basis_right)
    left_new = 0.95 * stat_left + 0.05 * jnp.einsum("sij,skj->sik", grads, grads, precision=highest)
    right_new = 0.95 * stat_right + 0.05 * jnp.einsum(
        "sji,sjk->sik", grads, grads, precision=highest
    )
    return (direction, orthogonalize(left_new, basis_left), orthogonalize(right_new, basis_right))


def per_device_plain(
    features,
    kv_cotangent,
    owner_of_block,
    first_moment,
    second_moment,
    left_stat,
    right_stat,
    left_basis,
    right_basis,
):
    tile = left_basis.shape[-1]
    capacity = left_basis.shape[1]
    d_win = features.shape[1]
    width = kv_cotangent.shape[1]
    row_tiles = d_win // tile
    col_tiles = width // tile
    nblocks = owner_of_block.shape[0]
    owner_here = lax.axis_index("dp")
    block_ids = jnp.arange(nblocks, dtype=jnp.int32)
    same = owner_of_block[:, None] == owner_of_block[None, :]
    earlier = block_ids[None, :] < block_ids[:, None]
    slot = jnp.sum((same & earlier).astype(jnp.int32), axis=1)
    slot_ids = jnp.arange(capacity, dtype=jnp.int32)
    match = (owner_of_block[None, :] == owner_here) & (slot[None, :] == slot_ids[:, None])
    live = jnp.any(match, axis=1)
    which = jnp.sum(jnp.where(match, block_ids[None, :], 0), axis=1)
    row_start = which // col_tiles * tile
    col_start = which % col_tiles * tile
    partial_grad = lax.dot_general(
        features, kv_cotangent, (((0,), (0,)), ((), ())), preferred_element_type=jnp.float32
    )
    grad = lax.psum(partial_grad, ("dp", "inner"))
    fetched = [
        lax.dynamic_slice(grad, (row_start[slot_index], col_start[slot_index]), (tile, tile))
        for slot_index in range(capacity)
    ]
    grads = jnp.stack(fetched)
    basis_left = left_basis[0].astype(jnp.float32)
    basis_right = right_basis[0].astype(jnp.float32)
    direction, left_iter, right_iter = soap_tiles(
        grads,
        first_moment[0],
        second_moment[0],
        left_stat[0],
        right_stat[0],
        basis_left,
        basis_right,
    )
    direction_low = direction.astype(jnp.bfloat16)
    everyone = lax.all_gather(direction_low[None], "dp", axis=0, tiled=True)
    tiles = everyone[owner_of_block, slot]
    update = (
        tiles.reshape(row_tiles, col_tiles, tile, tile).transpose(0, 2, 1, 3).reshape(d_win, width)
    )
    keep = live[:, None, None]
    new_left = jnp.where(keep, left_iter.astype(jnp.bfloat16), left_basis[0])
    new_right = jnp.where(keep, right_iter.astype(jnp.bfloat16), right_basis[0])
    return (update, new_left[None], new_right[None])


MM = ((1,), (0,))
MT = ((1,), (1,))
TM = ((0,), (0,))


def turned(offset, core):
    if core == 0:
        return offset
    return (offset & ~12) | ((offset & 4) << 1) | ((offset & 8) >> 1)


def swap_along(values, axis, size, bit):
    if axis == "inner":
        return lax.ppermute(values, axis, [(i, i ^ bit) for i in range(size)])
    pairs = [(2 * i + c, 2 * (i ^ turned(bit, c)) + c) for i in range(size) for c in range(2)]
    return lax.ppermute(values, (axis, "inner"), pairs)


def dot(left, right, dims):
    return lax.dot_general(left, right, (dims, ((), ())), preferred_element_type=jnp.float32)


def halves(x):
    high = x.astype(jnp.bfloat16)
    return high, (x - high.astype(jnp.float32)).astype(jnp.bfloat16)


def beside(a, b):
    return jnp.concatenate([a, b], axis=1)


def above(a, b):
    return jnp.concatenate([a, b], axis=0)


def folded(both):
    n = both.shape[1] // 2
    return both[:, :n] + both[:, n:]


def pair_product(left, right, dims):
    if dims == TM:
        rows = above(*left)
    else:
        rows = beside(*left)
    if dims == MT:
        return folded(dot(rows, above(beside(right[0], right[0]), beside(right[1], right[1])), MT))
    return folded(dot(rows, above(beside(*right), beside(*right)), dims))


def low_times(low, x, dims):
    high, rest = halves(x)
    if dims == MT:
        return dot(beside(low, low), beside(high, rest), MT)
    return dot(beside(low, low), above(high, rest), MM)


def times_low(x, low):
    high, rest = halves(x)
    return dot(beside(high, rest), above(low, low), MM)


def stream_offsets(owners):
    bits = owners.bit_length() - 1
    highs = list(range(2, bits))
    orders = ([0, 1] + highs, [1, 0] + highs, highs + [0, 1])
    offsets = [
        [sum(((p >> (bits - 1 - i)) & 1) << bit for i, bit in enumerate(order)) for p in range(owners)]
        for order in orders
    ]
    return orders, offsets


def table_kernel(owners, capacity, place_ref, owner_ref, kv_ref, *rest):
    table_ref, own_rows, count, held = rest
    own_rows[...] = kv_ref[...].T

    for o in range(owners):
        count[o] = 0

    def enter(b, carry):
        o = owner_ref[b]
        s = count[o]
        count[o] = s + 1
        held[o * capacity + s] = b
        return carry

    lax.fori_loop(0, owners * capacity, enter, 0, unroll=8)
    here, core = place_ref[0], place_ref[1]
    offsets = stream_offsets(owners)[1]
    for side in range(2):
        at = core ^ side
        first_slot = 2 * at
        for stream in range(2):
            for p in range(owners):
                entry = (side * 2 + stream) * owners + p
                plain = offsets[stream][p]
                offset = plain + at * (turned(plain, 1) - plain)
                table_ref[entry] = held[(here ^ offset) * capacity + first_slot + stream]


EDGE = 32


def tiles_kernel(owners, first, table_ref, f_own, f_sib, own_rows, kv_sib, *rest):
    sib_rows = rest[-1]
    out_a, out_b = rest[-5:-3] if first == 0 else rest[:2]
    tile = out_a.shape[-1]
    body = tile - EDGE
    near = owners // 2
    col_tiles = own_rows.shape[0] // tile
    offsets = stream_offsets(owners)[1]
    sib_rows[...] = kv_sib[...].T
    for stream, out in enumerate((out_a, out_b)):
        for i in range(near):
            block = table_ref[stream * owners + first + i]
            at = pl.ds(pl.multiple_of(block // col_tiles * tile, tile), tile)
            cots = pl.ds(pl.multiple_of(block % col_tiles * tile, tile), tile)
            total = dot(own_rows[cots, :], f_own[:, at], MM) + dot(
                sib_rows[cots, :], f_sib[:, at], MM
            )
            out[i] = total[:body]
            place = 2 * offsets[2].index(offsets[stream][first + i]) + stream
            if first:
                rest[2][place] = total[body:]
            elif place < owners:
                rest[-3][place] = total[body:]
            else:
                rest[-2][place - owners] = total[body:]
            if first == 0:
                place = 2 * offsets[2].index(offsets[stream][near + i]) + stream
                if place < owners:
                    rest[-3][place] = rest[0][place]
                else:
                    rest[-2][place - owners] = rest[0][place]


SMEM = pl.BlockSpec(memory_space=pltpu.SMEM)
HBM = pl.BlockSpec(memory_space=pltpu.HBM)
VMEM = pl.BlockSpec(memory_space=pltpu.VMEM)


def whole(shape):
    return pl.BlockSpec(shape, lambda *g: (0,) * len(shape))


def wholes(arrays):
    return [whole(a.shape) for a in arrays]


BIG = pltpu.CompilerParams(vmem_limit_bytes=24 * 2**20)
SMALL = pltpu.CompilerParams(vmem_limit_bytes=12 * 2**20)


def rotated_kernel(side_ref, m_ref, v_ref, l_ref, r_ref, ql_ref, qr_ref, *outs):
    rot_ref, second_ref, power_ref = outs
    for k in range(2):
        left = ql_ref[0, k]
        right = qr_ref[0, k]
        half = times_low(m_ref[0, k].T, left)
        rot_ref[k] = 0.95 * low_times(right.T, half, MM)
        second_ref[k] = 0.95 * v_ref[0, k].T
        power_ref[2 * k] = 0.95 * times_low(l_ref[0, k], left)
        power_ref[2 * k + 1] = 0.95 * times_low(r_ref[0, k], right)


def direction_kernel(side_ref, a_ref, b_ref, c_ref, d_ref, m_ref, v_ref, *rest):
    ql_ref, qr_ref, dir_ref, grad_ref = rest
    pair = range(2)
    lefts = [ql_ref[0, k] for k in pair]
    rights = [qr_ref[0, k] for k in pair]
    turned = [right.T for right in rights]
    grads = [above(a_ref[k] + b_ref[k], c_ref[k] + d_ref[k]) for k in pair]
    rots = [times_low(grads[k], lefts[k]) for k in pair]
    rots = [low_times(turned[k], rots[k], MM) for k in pair]
    scaled = []
    for k in pair:
        moment_rot = m_ref[k] + 0.05 * rots[k]
        second = v_ref[k] + 0.05 * rots[k] * rots[k]
        scaled.append(moment_rot / (jnp.sqrt(second) + 1e-08))
    outs = [low_times(rights[k], scaled[k], MM) for k in pair]
    outs = [low_times(lefts[k], outs[k], MT) for k in pair]
    for k in pair:
        dir_ref[k] = outs[k].astype(dir_ref.dtype)
        grad_ref[k] = grads[k]


def slots_of(*arrays):
    tile = arrays[0].shape[-1]
    return [pl.BlockSpec((1, 2, tile, tile), lambda i, s: (0, s[0], 0, 0)) for _ in arrays]


def on_slots(kernel, side, plain, slotted, outs, flops):
    return pl.pallas_call(
        kernel,
        out_shape=tuple(outs),
        grid_spec=pltpu.PrefetchScalarGridSpec(
            num_scalar_prefetch=1,
            grid=(1,),
            in_specs=wholes(plain) + slots_of(*slotted),
            out_specs=tuple(wholes(outs)),
        ),
        compiler_params=SMALL,
        cost_estimate=pl.CostEstimate(flops=flops, bytes_accessed=800_000, transcendentals=0),
        name=kernel.__name__.removesuffix("_kernel"),
    )(side, *plain, *slotted)


def sweep(values):
    pairs = [halves(y) for y in values]
    grams = [halves(pair_product(p, p, MT)) for p in pairs]
    return tuple(
        1.5 * y - 0.5 * pair_product(g, p, MM) for y, g, p in zip(values, grams, pairs)
    )


def sweeps(values, count):
    return lax.fori_loop(0, count, lambda i, v: sweep(v), tuple(values), unroll=2)


STAGES = (5, NS_STEPS - 5)


def refresh_kernel(side_ref, g_ref, power_ref, ql_ref, qr_ref, iter_ref):
    values = []
    for k in range(2):
        turned = g_ref[k]
        grad = turned.T
        for i, rows, columns, basis in ((0, grad, turned, ql_ref), (1, turned, grad, qr_ref)):
            half = times_low(columns, basis[0, k])
            power = power_ref[2 * k + i] + 0.05 * pair_product(halves(rows), halves(half), MM)
            values.append((power / jnp.sqrt(jnp.sum(power * power) + 1e-06)).T)
    for i, y in enumerate(sweeps(values, STAGES[0])):
        iter_ref[i] = y


def finish_kernel(iter_ref, out_ref):
    for i, y in enumerate(sweeps([iter_ref[i] for i in range(4)], STAGES[1])):
        out_ref[i] = y.T.astype(out_ref.dtype)


def sweeping(kernel, values, dtype, count):
    tile = values.shape[-1]
    return pl.pallas_call(
        kernel,
        out_shape=jax.ShapeDtypeStruct(values.shape, dtype),
        compiler_params=SMALL,
        cost_estimate=pl.CostEstimate(
            flops=4 * 2 * count * 4 * 2 * tile**3, bytes_accessed=400_000, transcendentals=0
        ),
        name=kernel.__name__.removesuffix("_kernel"),
    )(values)


def place_tiles(col_tiles, entries, table_ref, sources, out, sems):
    tile = sources[0].shape[-1]
    copies = []
    for entry, source in zip(entries, sources):
        for i in range(source.shape[0]):
            block = table_ref[entry + i]
            rows = pl.ds(pl.multiple_of(block // col_tiles * tile, tile), tile)
            columns = pl.ds(pl.multiple_of(block % col_tiles * tile, tile), tile)
            copies.append(
                pltpu.make_async_copy(source.at[i], out.at[rows, columns], sems.at[len(copies)])
            )
            copies[-1].start()
    return copies


def begin_kernel(col_tiles, entries, table_ref, place_ref, own_ref, sib_ref, *refs):
    sources = refs[:-4]
    out, left, right, sems = refs[-4:]
    copies = place_tiles(col_tiles, entries, table_ref, sources, out, sems)
    core = place_ref[1]
    for source, first in ((own_ref, 2 * core), (sib_ref, 2 - 2 * core)):
        for k in range(2):
            for i, target in enumerate((left, right)):
                copies.append(
                    pltpu.make_async_copy(
                        source.at[2 * k + i], target.at[0, first + k], sems.at[len(copies)]
                    )
                )
                copies[-1].start()
    for copy in copies:
        copy.wait()


def more_kernel(col_tiles, entries, table_ref, *refs):
    out, sems = refs[-2:]
    for copy in place_tiles(col_tiles, entries, table_ref, refs[:-3], out, sems):
        copy.wait()


def place_more(update, table, col_tiles, entries, sources):
    count = sum(x.shape[0] for x in sources)
    return pl.pallas_call(
        functools.partial(more_kernel, col_tiles, entries),
        out_shape=jax.ShapeDtypeStruct(update.shape, update.dtype),
        in_specs=[SMEM] + [VMEM] * len(sources) + [HBM],
        out_specs=HBM,
        scratch_shapes=[pltpu.SemaphoreType.DMA((count,))],
        input_output_aliases={1 + len(sources): 0},
        compiler_params=SMALL,
        cost_estimate=pl.CostEstimate(flops=0, bytes_accessed=1_000_000, transcendentals=0),
        name="more",
    )(table, *sources, update)


def per_device_dealt(
    owners,
    features,
    kv_cotangent,
    owner_of_block,
    first_moment,
    second_moment,
    left_stat,
    right_stat,
    left_basis,
    right_basis,
):
    tile = left_basis.shape[-1]
    capacity = left_basis.shape[1]
    rows, d_win = features.shape
    width = kv_cotangent.shape[1]
    col_tiles = width // tile
    here = lax.axis_index("dp")
    core = lax.axis_index("inner")
    place = jnp.stack([here, core]).astype(jnp.int32)
    side = core.reshape(1).astype(jnp.int32)
    orders = stream_offsets(owners)[0]
    near = owners // 2
    bits = len(orders[0])

    f_sib = swap_along(features, "inner", 2, 1)
    kv_sib = swap_along(kv_cotangent, "inner", 2, 1)
    flipped = pltpu.VMEM((width, rows), jnp.bfloat16)
    part = jax.ShapeDtypeStruct((near, tile - EDGE, tile), jnp.float32)
    edge = jax.ShapeDtypeStruct((owners, EDGE, tile), jnp.float32)
    edges = jax.ShapeDtypeStruct((2 * owners, EDGE, tile), jnp.float32)
    f32_pair = jax.ShapeDtypeStruct((2, tile, tile), jnp.float32)
    table, own_rows = pl.pallas_call(
        functools.partial(table_kernel, owners, capacity),
        out_shape=(
            jax.ShapeDtypeStruct((4 * owners,), jnp.int32),
            jax.ShapeDtypeStruct((width, rows), jnp.bfloat16),
        ),
        in_specs=[SMEM, SMEM, VMEM],
        out_specs=(SMEM, VMEM),
        compiler_params=SMALL,
        scratch_shapes=[
            pltpu.SMEM((owners,), jnp.int32),
            pltpu.SMEM((owners * capacity,), jnp.int32),
        ],
        cost_estimate=pl.CostEstimate(flops=0, bytes_accessed=1_000_000, transcendentals=0),
        name="table",
    )(place, owner_of_block, kv_cotangent)

    def tiles_from(first, outs, *more):
        inputs = (features, f_sib, own_rows, kv_sib, *more)
        return pl.pallas_call(
            functools.partial(tiles_kernel, owners, first),
            out_shape=outs,
            grid=(1,),
            in_specs=[SMEM] + wholes(inputs),
            out_specs=tuple(wholes(outs)),
            scratch_shapes=[flipped],
            compiler_params=BIG,
            cost_estimate=pl.CostEstimate(
                flops=2 * owners * 2 * tile * tile * 2 * rows,
                bytes_accessed=3_500_000,
                transcendentals=0,
            ),
            name="tiles",
        )(table, *inputs)

    sent_a, sent_b, early = tiles_from(near, (part, part, edges))
    got_a = swap_along(sent_a, "dp", owners, 1 << orders[0][0])
    got_b = swap_along(sent_b, "dp", owners, 1 << orders[1][0])
    kept_a, kept_b, kept_c, sent_c = tiles_from(0, (part, part, edge, edge), early)
    got_c = swap_along(sent_c, "dp", owners, 1 << orders[2][0])
    quad = jax.ShapeDtypeStruct((4, tile, tile), jnp.float32)
    moment_rot, second, power = on_slots(
        rotated_kernel,
        side,
        (),
        (first_moment, second_moment, left_stat, right_stat, left_basis, right_basis),
        (f32_pair, f32_pair, quad),
        16 * 2 * tile**3,
    )

    def halved(kept, got):
        half = kept.shape[0] // 2
        return kept[:half] + got[:half], kept[half:] + got[half:]

    def after(values, *needed):
        return lax.optimization_barrier((values, *needed))[0]

    def edges_on(step, kept, got):
        kept, sent = halved(kept, got)
        return kept, sent, swap_along(sent, "dp", owners, 1 << orders[2][step])

    kept_c, sent_c, got_c = edges_on(1, kept_c, got_c)
    kept_a, sent_a = halved(kept_a, got_a)
    kept_b, sent_b = halved(kept_b, got_b)
    got_a = swap_along(sent_a, "dp", owners, 1 << orders[0][1])
    got_b = swap_along(sent_b, "dp", owners, 1 << orders[1][1])
    kept = jnp.stack([kept_a, kept_b], axis=1)
    got = jnp.stack([got_a, got_b], axis=1)
    for step in range(2, bits):
        kept, sent = halved(kept, got)
        if step > 2:
            sent = after(sent, got_c)
            kept_c, sent_c, got_c = edges_on(step - 1, kept_c, got_c)
        if step == bits - 1:
            sent, kept = sent[0], kept[0]
        got = swap_along(sent, "dp", owners, 1 << orders[0][step])
    kept_c, sent_c, got_c = edges_on(bits - 1, kept_c, got_c)
    direction, grads = on_slots(
        direction_kernel,
        side,
        (kept, got, kept_c, got_c, moment_rot, second),
        (left_basis, right_basis),
        (jax.ShapeDtypeStruct(f32_pair.shape, jnp.bfloat16), f32_pair),
        16 * 2 * tile**3,
    )

    high = owners // 4
    tiles = []
    for p in range(high):
        offset = sum(((p >> (bits - 3 - i)) & 1) << bit for i, bit in enumerate(orders[0][2:]))
        tiles.append(swap_along(direction, "dp", owners, offset) if offset else direction)
    values = on_slots(
        refresh_kernel,
        side,
        (grads, power),
        (left_basis, right_basis),
        (quad,),
        4 * (4 + 2 * STAGES[0]) * 4 * 2 * tile**3,
    )[0]
    mine = [jnp.stack([t[stream] for t in tiles]) for stream in range(2)]
    mine, values = lax.optimization_barrier((mine, values))
    other = [swap_along(m, "dp", owners, 1 << order[1]) for m, order in zip(mine, orders)]
    fresh = sweeping(finish_kernel, values, jnp.bfloat16, STAGES[1])
    mine = [jnp.concatenate(both, axis=0) for both in zip(mine, other)]
    mine, fresh = lax.optimization_barrier((mine, fresh))
    other = [swap_along(m, "dp", owners, 1 << order[0]) for m, order in zip(mine, orders)]
    fresh_sib = swap_along(fresh, "inner", 2, 1)
    basis = jax.ShapeDtypeStruct(left_basis.shape, left_basis.dtype)
    update, new_left, new_right = pl.pallas_call(
        functools.partial(begin_kernel, col_tiles, (0, owners)),
        out_shape=(jax.ShapeDtypeStruct((d_win, width), jnp.bfloat16), basis, basis),
        in_specs=[SMEM, SMEM] + [VMEM] * 4,
        out_specs=(HBM, HBM, HBM),
        scratch_shapes=[pltpu.SemaphoreType.DMA((2 * near + 8,))],
        compiler_params=SMALL,
        cost_estimate=pl.CostEstimate(flops=0, bytes_accessed=800_000, transcendentals=0),
        name="begin",
    )(table, place, fresh, fresh_sib, *mine)
    update, other = lax.optimization_barrier((update, other))
    mine_sib = [swap_along(m, "inner", 2, 1) for m in mine]
    other_sib = [swap_along(o, "inner", 2, 1) for o in other]
    update = place_more(
        update,
        table,
        col_tiles,
        (2 * owners, 3 * owners, near, owners + near),
        mine_sib + other,
    )
    update = place_more(
        update, table, col_tiles, (2 * owners + near, 3 * owners + near), other_sib
    )
    return update, new_left, new_right


def solution(mesh):
    owners = mesh.shape["dp"]
    inner = mesh.shape["inner"]

    def per_device(*args):
        capacity = args[-1].shape[1]
        full = args[2].shape[0] == owners * capacity
        if full and inner == 2 and capacity == 4 and owners >= 16 and owners & (owners - 1) == 0:
            return per_device_dealt(owners, *args)
        return per_device_plain(*args)

    return jax.shard_map(
        per_device,
        mesh=mesh,
        in_specs=(
            P(("dp", "inner"), None),
            P(("dp", "inner"), None),
            P(),
            P("dp", None, None, None),
            P("dp", None, None, None),
            P("dp", None, None, None),
            P("dp", None, None, None),
            P("dp", None, None, None),
            P("dp", None, None, None),
        ),
        out_specs=(P(), P("dp", None, None, None), P("dp", None, None, None)),
        check_vma=False,
    )
```

```python
import functools

import jax
import jax.numpy as jnp
from jax import lax
from jax.experimental import pallas as pl
from jax.experimental.pallas import tpu as pltpu
from jax.sharding import PartitionSpec as P

NS_STEPS = 12


highest = lax.Precision.HIGHEST


def rotate_in(basis_left, matrix, basis_right):
    half = jnp.einsum("sji,sjk->sik", basis_left, matrix, precision=highest)
    return jnp.einsum("sij,sjk->sik", half, basis_right, precision=highest)


def rotate_out(basis_left, matrix, basis_right):
    half = jnp.einsum("sij,sjk->sik", basis_left, matrix, precision=highest)
    return jnp.einsum("sij,skj->sik", half, basis_right, precision=highest)


def orthogonalize(stat, basis):
    power = jnp.einsum("sij,sjk->sik", stat, basis, precision=highest)
    scale = jnp.sqrt(jnp.sum(power * power, axis=(1, 2), keepdims=True) + 1e-06)
    iterate = power / scale
    for sweep in range(NS_STEPS):
        gram = jnp.einsum("sji,sjk->sik", iterate, iterate, precision=highest)
        iterate = 1.5 * iterate - 0.5 * jnp.einsum("sij,sjk->sik", iterate, gram, precision=highest)
    return iterate


def soap_tiles(grads, first, second, stat_left, stat_right, basis_left, basis_right):
    rotated = rotate_in(basis_left, grads, basis_right)
    moment = 0.95 * first + 0.05 * grads
    moment_rot = rotate_in(basis_left, moment, basis_right)
    second_new = 0.95 * second + 0.05 * rotated * rotated
    direction = rotate_out(basis_left, moment_rot / (jnp.sqrt(second_new) + 1e-08), basis_right)
    left_new = 0.95 * stat_left + 0.05 * jnp.einsum("sij,skj->sik", grads, grads, precision=highest)
    right_new = 0.95 * stat_right + 0.05 * jnp.einsum(
        "sji,sjk->sik", grads, grads, precision=highest
    )
    return (direction, orthogonalize(left_new, basis_left), orthogonalize(right_new, basis_right))


def per_device_plain(
    features,
    kv_cotangent,
    owner_of_block,
    first_moment,
    second_moment,
    left_stat,
    right_stat,
    left_basis,
    right_basis,
):
    tile = left_basis.shape[-1]
    capacity = left_basis.shape[1]
    d_win = features.shape[1]
    width = kv_cotangent.shape[1]
    row_tiles = d_win // tile
    col_tiles = width // tile
    nblocks = owner_of_block.shape[0]
    owner_here = lax.axis_index("dp")
    block_ids = jnp.arange(nblocks, dtype=jnp.int32)
    same = owner_of_block[:, None] == owner_of_block[None, :]
    earlier = block_ids[None, :] < block_ids[:, None]
    slot = jnp.sum((same & earlier).astype(jnp.int32), axis=1)
    slot_ids = jnp.arange(capacity, dtype=jnp.int32)
    match = (owner_of_block[None, :] == owner_here) & (slot[None, :] == slot_ids[:, None])
    live = jnp.any(match, axis=1)
    which = jnp.sum(jnp.where(match, block_ids[None, :], 0), axis=1)
    row_start = which // col_tiles * tile
    col_start = which % col_tiles * tile
    partial_grad = lax.dot_general(
        features, kv_cotangent, (((0,), (0,)), ((), ())), preferred_element_type=jnp.float32
    )
    grad = lax.psum(partial_grad, ("dp", "inner"))
    fetched = [
        lax.dynamic_slice(grad, (row_start[slot_index], col_start[slot_index]), (tile, tile))
        for slot_index in range(capacity)
    ]
    grads = jnp.stack(fetched)
    basis_left = left_basis[0].astype(jnp.float32)
    basis_right = right_basis[0].astype(jnp.float32)
    direction, left_iter, right_iter = soap_tiles(
        grads,
        first_moment[0],
        second_moment[0],
        left_stat[0],
        right_stat[0],
        basis_left,
        basis_right,
    )
    direction_low = direction.astype(jnp.bfloat16)
    everyone = lax.all_gather(direction_low[None], "dp", axis=0, tiled=True)
    tiles = everyone[owner_of_block, slot]
    update = (
        tiles.reshape(row_tiles, col_tiles, tile, tile).transpose(0, 2, 1, 3).reshape(d_win, width)
    )
    keep = live[:, None, None]
    new_left = jnp.where(keep, left_iter.astype(jnp.bfloat16), left_basis[0])
    new_right = jnp.where(keep, right_iter.astype(jnp.bfloat16), right_basis[0])
    return (update, new_left[None], new_right[None])


MM = ((1,), (0,))
MT = ((1,), (1,))
TM = ((0,), (0,))


def swap_along(values, axis, size, bit):
    return lax.ppermute(values, axis, [(i, i ^ bit) for i in range(size)])


def dot(left, right, dims):
    return lax.dot_general(left, right, (dims, ((), ())), preferred_element_type=jnp.float32)


def halves(x):
    high = x.astype(jnp.bfloat16)
    return high, (x - high.astype(jnp.float32)).astype(jnp.bfloat16)


def beside(a, b):
    return jnp.concatenate([a, b], axis=1)


def above(a, b):
    return jnp.concatenate([a, b], axis=0)


def folded(both):
    n = both.shape[1] // 2
    return both[:, :n] + both[:, n:]


def pair_product(left, right, dims):
    if dims == TM:
        rows = above(*left)
    else:
        rows = beside(*left)
    if dims == MT:
        return folded(dot(rows, above(beside(right[0], right[0]), beside(right[1], right[1])), MT))
    return folded(dot(rows, above(beside(*right), beside(*right)), dims))


def low_times(low, x, dims):
    high, rest = halves(x)
    if dims == MT:
        return dot(beside(low, low), beside(high, rest), MT)
    return dot(beside(low, low), above(high, rest), MM)


def times_low(x, low):
    high, rest = halves(x)
    return dot(beside(high, rest), above(low, low), MM)


def stream_offsets(owners):
    bits = owners.bit_length() - 1
    highs = list(range(2, bits))
    orders = ([0, 1] + highs, [1, 0] + highs, highs + [0, 1])
    offsets = [
        [sum(((p >> (bits - 1 - i)) & 1) << bit for i, bit in enumerate(order)) for p in range(owners)]
        for order in orders
    ]
    return orders, offsets


def table_kernel(owners, capacity, place_ref, owner_ref, kv_ref, *rest):
    table_ref, own_rows, count, held = rest
    own_rows[...] = kv_ref[...].T

    for o in range(owners):
        count[o] = 0

    def enter(b, carry):
        o = owner_ref[b]
        s = count[o]
        count[o] = s + 1
        held[o * capacity + s] = b
        return carry

    lax.fori_loop(0, owners * capacity, enter, 0, unroll=8)
    here, core = place_ref[0], place_ref[1]
    offsets = stream_offsets(owners)[1]
    for side in range(2):
        first_slot = 2 * (core ^ side)
        for stream in range(2):
            for p in range(owners):
                entry = (side * 2 + stream) * owners + p
                table_ref[entry] = held[(here ^ offsets[stream][p]) * capacity + first_slot + stream]


EDGE = 40


def tiles_kernel(owners, first, table_ref, f_own, f_sib, own_rows, kv_sib, *rest):
    sib_rows = rest[-1]
    out_a, out_b = rest[-5:-3] if first == 0 else rest[:2]
    tile = out_a.shape[-1]
    body = tile - EDGE
    near = owners // 2
    col_tiles = own_rows.shape[0] // tile
    offsets = stream_offsets(owners)[1]
    sib_rows[...] = kv_sib[...].T
    for stream, out in enumerate((out_a, out_b)):
        for i in range(near):
            block = table_ref[stream * owners + first + i]
            at = pl.ds(pl.multiple_of(block // col_tiles * tile, tile), tile)
            cots = pl.ds(pl.multiple_of(block % col_tiles * tile, tile), tile)
            total = dot(own_rows[cots, :], f_own[:, at], MM) + dot(
                sib_rows[cots, :], f_sib[:, at], MM
            )
            out[i] = total[:body]
            place = 2 * offsets[2].index(offsets[stream][first + i]) + stream
            if first:
                rest[2][place] = total[body:]
            elif place < owners:
                rest[-3][place] = total[body:]
            else:
                rest[-2][place - owners] = total[body:]
            if first == 0:
                place = 2 * offsets[2].index(offsets[stream][near + i]) + stream
                if place < owners:
                    rest[-3][place] = rest[0][place]
                else:
                    rest[-2][place - owners] = rest[0][place]


SMEM = pl.BlockSpec(memory_space=pltpu.SMEM)
HBM = pl.BlockSpec(memory_space=pltpu.HBM)
VMEM = pl.BlockSpec(memory_space=pltpu.VMEM)


def whole(shape):
    return pl.BlockSpec(shape, lambda *g: (0,) * len(shape))


def wholes(arrays):
    return [whole(a.shape) for a in arrays]


BIG = pltpu.CompilerParams(vmem_limit_bytes=24 * 2**20)
SMALL = pltpu.CompilerParams(vmem_limit_bytes=12 * 2**20)


def rotated_kernel(side_ref, m_ref, v_ref, l_ref, r_ref, ql_ref, qr_ref, *outs):
    rot_ref, second_ref, power_ref = outs
    for k in range(2):
        left = ql_ref[0, k]
        right = qr_ref[0, k]
        half = times_low(m_ref[0, k].T, left)
        rot_ref[k] = 0.95 * low_times(right.T, half, MM)
        second_ref[k] = 0.95 * v_ref[0, k].T
        power_ref[2 * k] = 0.95 * times_low(l_ref[0, k], left)
        power_ref[2 * k + 1] = 0.95 * times_low(r_ref[0, k], right)


def direction_kernel(side_ref, a_ref, b_ref, c_ref, d_ref, m_ref, v_ref, *rest):
    ql_ref, qr_ref, dir_ref, grad_ref = rest
    pair = range(2)
    lefts = [ql_ref[0, k] for k in pair]
    rights = [qr_ref[0, k] for k in pair]
    turned = [right.T for right in rights]
    grads = [above(a_ref[k] + b_ref[k], c_ref[k] + d_ref[k]) for k in pair]
    rots = [times_low(grads[k], lefts[k]) for k in pair]
    rots = [low_times(turned[k], rots[k], MM) for k in pair]
    scaled = []
    for k in pair:
        moment_rot = m_ref[k] + 0.05 * rots[k]
        second = v_ref[k] + 0.05 * rots[k] * rots[k]
        scaled.append(moment_rot / (jnp.sqrt(second) + 1e-08))
    outs = [low_times(rights[k], scaled[k], MM) for k in pair]
    outs = [low_times(lefts[k], outs[k], MT) for k in pair]
    for k in pair:
        dir_ref[k] = outs[k].astype(dir_ref.dtype)
        grad_ref[k] = grads[k]


def slots_of(*arrays):
    tile = arrays[0].shape[-1]
    return [pl.BlockSpec((1, 2, tile, tile), lambda i, s: (0, s[0], 0, 0)) for _ in arrays]


def on_slots(kernel, side, plain, slotted, outs, flops):
    return pl.pallas_call(
        kernel,
        out_shape=tuple(outs),
        grid_spec=pltpu.PrefetchScalarGridSpec(
            num_scalar_prefetch=1,
            grid=(1,),
            in_specs=wholes(plain) + slots_of(*slotted),
            out_specs=tuple(wholes(outs)),
        ),
        compiler_params=SMALL,
        cost_estimate=pl.CostEstimate(flops=flops, bytes_accessed=800_000, transcendentals=0),
        name=kernel.__name__.removesuffix("_kernel"),
    )(side, *plain, *slotted)


def sweep(values):
    pairs = [halves(y) for y in values]
    grams = [halves(pair_product(p, p, MT)) for p in pairs]
    return tuple(
        1.5 * y - 0.5 * pair_product(g, p, MM) for y, g, p in zip(values, grams, pairs)
    )


def sweeps(values, count):
    return lax.fori_loop(0, count, lambda i, v: sweep(v), tuple(values), unroll=2)


STAGES = (5, NS_STEPS - 5)


def refresh_kernel(side_ref, g_ref, power_ref, ql_ref, qr_ref, iter_ref):
    values = []
    for k in range(2):
        turned = g_ref[k]
        grad = turned.T
        for i, rows, columns, basis in ((0, grad, turned, ql_ref), (1, turned, grad, qr_ref)):
            half = times_low(columns, basis[0, k])
            power = power_ref[2 * k + i] + 0.05 * pair_product(halves(rows), halves(half), MM)
            values.append((power / jnp.sqrt(jnp.sum(power * power) + 1e-06)).T)
    for i, y in enumerate(sweeps(values, STAGES[0])):
        iter_ref[i] = y


def finish_kernel(iter_ref, out_ref):
    for i, y in enumerate(sweeps([iter_ref[i] for i in range(4)], STAGES[1])):
        out_ref[i] = y.T.astype(out_ref.dtype)


def sweeping(kernel, values, dtype, count):
    tile = values.shape[-1]
    return pl.pallas_call(
        kernel,
        out_shape=jax.ShapeDtypeStruct(values.shape, dtype),
        compiler_params=SMALL,
        cost_estimate=pl.CostEstimate(
            flops=4 * 2 * count * 4 * 2 * tile**3, bytes_accessed=400_000, transcendentals=0
        ),
        name=kernel.__name__.removesuffix("_kernel"),
    )(values)


def place_tiles(col_tiles, entries, table_ref, sources, out, sems):
    tile = sources[0].shape[-1]
    copies = []
    for entry, source in zip(entries, sources):
        for i in range(source.shape[0]):
            block = table_ref[entry + i]
            rows = pl.ds(pl.multiple_of(block // col_tiles * tile, tile), tile)
            columns = pl.ds(pl.multiple_of(block % col_tiles * tile, tile), tile)
            copies.append(
                pltpu.make_async_copy(source.at[i], out.at[rows, columns], sems.at[len(copies)])
            )
            copies[-1].start()
    return copies


def begin_kernel(col_tiles, entries, table_ref, place_ref, own_ref, sib_ref, *refs):
    sources = refs[:-4]
    out, left, right, sems = refs[-4:]
    copies = place_tiles(col_tiles, entries, table_ref, sources, out, sems)
    core = place_ref[1]
    for source, first in ((own_ref, 2 * core), (sib_ref, 2 - 2 * core)):
        for k in range(2):
            for i, target in enumerate((left, right)):
                copies.append(
                    pltpu.make_async_copy(
                        source.at[2 * k + i], target.at[0, first + k], sems.at[len(copies)]
                    )
                )
                copies[-1].start()
    for copy in copies:
        copy.wait()


def more_kernel(col_tiles, entries, table_ref, *refs):
    out, sems = refs[-2:]
    for copy in place_tiles(col_tiles, entries, table_ref, refs[:-3], out, sems):
        copy.wait()


def place_more(update, table, col_tiles, entries, sources):
    count = sum(x.shape[0] for x in sources)
    return pl.pallas_call(
        functools.partial(more_kernel, col_tiles, entries),
        out_shape=jax.ShapeDtypeStruct(update.shape, update.dtype),
        in_specs=[SMEM] + [VMEM] * len(sources) + [HBM],
        out_specs=HBM,
        scratch_shapes=[pltpu.SemaphoreType.DMA((count,))],
        input_output_aliases={1 + len(sources): 0},
        compiler_params=SMALL,
        cost_estimate=pl.CostEstimate(flops=0, bytes_accessed=1_000_000, transcendentals=0),
        name="more",
    )(table, *sources, update)


def per_device_dealt(
    owners,
    features,
    kv_cotangent,
    owner_of_block,
    first_moment,
    second_moment,
    left_stat,
    right_stat,
    left_basis,
    right_basis,
):
    tile = left_basis.shape[-1]
    capacity = left_basis.shape[1]
    rows, d_win = features.shape
    width = kv_cotangent.shape[1]
    col_tiles = width // tile
    here = lax.axis_index("dp")
    core = lax.axis_index("inner")
    place = jnp.stack([here, core]).astype(jnp.int32)
    side = core.reshape(1).astype(jnp.int32)
    orders = stream_offsets(owners)[0]
    near = owners // 2
    bits = len(orders[0])

    f_sib = swap_along(features, "inner", 2, 1)
    kv_sib = swap_along(kv_cotangent, "inner", 2, 1)
    flipped = pltpu.VMEM((width, rows), jnp.bfloat16)
    part = jax.ShapeDtypeStruct((near, tile - EDGE, tile), jnp.float32)
    edge = jax.ShapeDtypeStruct((owners, EDGE, tile), jnp.float32)
    edges = jax.ShapeDtypeStruct((2 * owners, EDGE, tile), jnp.float32)
    f32_pair = jax.ShapeDtypeStruct((2, tile, tile), jnp.float32)
    table, own_rows = pl.pallas_call(
        functools.partial(table_kernel, owners, capacity),
        out_shape=(
            jax.ShapeDtypeStruct((4 * owners,), jnp.int32),
            jax.ShapeDtypeStruct((width, rows), jnp.bfloat16),
        ),
        in_specs=[SMEM, SMEM, VMEM],
        out_specs=(SMEM, VMEM),
        compiler_params=SMALL,
        scratch_shapes=[
            pltpu.SMEM((owners,), jnp.int32),
            pltpu.SMEM((owners * capacity,), jnp.int32),
        ],
        cost_estimate=pl.CostEstimate(flops=0, bytes_accessed=1_000_000, transcendentals=0),
        name="table",
    )(place, owner_of_block, kv_cotangent)

    def tiles_from(first, outs, *more):
        inputs = (features, f_sib, own_rows, kv_sib, *more)
        return pl.pallas_call(
            functools.partial(tiles_kernel, owners, first),
            out_shape=outs,
            grid=(1,),
            in_specs=[SMEM] + wholes(inputs),
            out_specs=tuple(wholes(outs)),
            scratch_shapes=[flipped],
            compiler_params=BIG,
            cost_estimate=pl.CostEstimate(
                flops=2 * owners * 2 * tile * tile * 2 * rows,
                bytes_accessed=3_500_000,
                transcendentals=0,
            ),
            name="tiles",
        )(table, *inputs)

    sent_a, sent_b, early = tiles_from(near, (part, part, edges))
    got_a = swap_along(sent_a, "dp", owners, 1 << orders[0][0])
    got_b = swap_along(sent_b, "dp", owners, 1 << orders[1][0])
    kept_a, kept_b, kept_c, sent_c = tiles_from(0, (part, part, edge, edge), early)
    got_c = swap_along(sent_c, "dp", owners, 1 << orders[2][0])
    quad = jax.ShapeDtypeStruct((4, tile, tile), jnp.float32)
    moment_rot, second, power = on_slots(
        rotated_kernel,
        side,
        (),
        (first_moment, second_moment, left_stat, right_stat, left_basis, right_basis),
        (f32_pair, f32_pair, quad),
        16 * 2 * tile**3,
    )

    def halved(kept, got):
        half = kept.shape[0] // 2
        return kept[:half] + got[:half], kept[half:] + got[half:]

    def after(values, *needed):
        return lax.optimization_barrier((values, *needed))[0]

    def edges_on(step, kept, got):
        kept, sent = halved(kept, got)
        return kept, sent, swap_along(sent, "dp", owners, 1 << orders[2][step])

    kept_c, sent_c, got_c = edges_on(1, kept_c, got_c)
    kept_a, sent_a = halved(kept_a, got_a)
    kept_b, sent_b = halved(kept_b, got_b)
    got_a = swap_along(sent_a, "dp", owners, 1 << orders[0][1])
    got_b = swap_along(sent_b, "dp", owners, 1 << orders[1][1])
    kept = jnp.stack([kept_a, kept_b], axis=1)
    got = jnp.stack([got_a, got_b], axis=1)
    for step in range(2, bits):
        kept, sent = halved(kept, got)
        if step > 2:
            sent = after(sent, got_c)
            kept_c, sent_c, got_c = edges_on(step - 1, kept_c, got_c)
        if step == bits - 1:
            sent, kept = sent[0], kept[0]
        got = swap_along(sent, "dp", owners, 1 << orders[0][step])
    kept_c, sent_c, got_c = edges_on(bits - 1, kept_c, got_c)
    direction, grads = on_slots(
        direction_kernel,
        side,
        (kept, got, kept_c, got_c, moment_rot, second),
        (left_basis, right_basis),
        (jax.ShapeDtypeStruct(f32_pair.shape, jnp.bfloat16), f32_pair),
        16 * 2 * tile**3,
    )

    high = owners // 4
    tiles = []
    for p in range(high):
        offset = sum(((p >> (bits - 3 - i)) & 1) << bit for i, bit in enumerate(orders[0][2:]))
        tiles.append(swap_along(direction, "dp", owners, offset) if offset else direction)
    values = on_slots(
        refresh_kernel,
        side,
        (grads, power),
        (left_basis, right_basis),
        (quad,),
        4 * (4 + 2 * STAGES[0]) * 4 * 2 * tile**3,
    )[0]
    mine = [jnp.stack([t[stream] for t in tiles]) for stream in range(2)]
    mine, values = lax.optimization_barrier((mine, values))
    other = [swap_along(m, "dp", owners, 1 << order[1]) for m, order in zip(mine, orders)]
    fresh = sweeping(finish_kernel, values, jnp.bfloat16, STAGES[1])
    mine = [jnp.concatenate(both, axis=0) for both in zip(mine, other)]
    mine, fresh = lax.optimization_barrier((mine, fresh))
    other = [swap_along(m, "dp", owners, 1 << order[0]) for m, order in zip(mine, orders)]
    fresh_sib = swap_along(fresh, "inner", 2, 1)
    basis = jax.ShapeDtypeStruct(left_basis.shape, left_basis.dtype)
    update, new_left, new_right = pl.pallas_call(
        functools.partial(begin_kernel, col_tiles, (0, owners)),
        out_shape=(jax.ShapeDtypeStruct((d_win, width), jnp.bfloat16), basis, basis),
        in_specs=[SMEM, SMEM] + [VMEM] * 4,
        out_specs=(HBM, HBM, HBM),
        scratch_shapes=[pltpu.SemaphoreType.DMA((2 * near + 8,))],
        compiler_params=SMALL,
        cost_estimate=pl.CostEstimate(flops=0, bytes_accessed=800_000, transcendentals=0),
        name="begin",
    )(table, place, fresh, fresh_sib, *mine)
    update, other = lax.optimization_barrier((update, other))
    mine_sib = [swap_along(m, "inner", 2, 1) for m in mine]
    other_sib = [swap_along(o, "inner", 2, 1) for o in other]
    update = place_more(
        update,
        table,
        col_tiles,
        (2 * owners, 3 * owners, near, owners + near),
        mine_sib + other,
    )
    update = place_more(
        update, table, col_tiles, (2 * owners + near, 3 * owners + near), other_sib
    )
    return update, new_left, new_right


def solution(mesh):
    owners = mesh.shape["dp"]
    inner = mesh.shape["inner"]

    def per_device(*args):
        capacity = args[-1].shape[1]
        full = args[2].shape[0] == owners * capacity
        if full and inner == 2 and capacity == 4 and owners >= 8 and owners & (owners - 1) == 0:
            return per_device_dealt(owners, *args)
        return per_device_plain(*args)

    return jax.shard_map(
        per_device,
        mesh=mesh,
        in_specs=(
            P(("dp", "inner"), None),
            P(("dp", "inner"), None),
            P(),
            P("dp", None, None, None),
            P("dp", None, None, None),
            P("dp", None, None, None),
            P("dp", None, None, None),
            P("dp", None, None, None),
            P("dp", None, None, None),
        ),
        out_specs=(P(), P("dp", None, None, None), P("dp", None, None, None)),
        check_vma=False,
    )
```

```python
import functools

import jax
import jax.numpy as jnp
from jax import lax
from jax.experimental import pallas as pl
from jax.experimental.pallas import tpu as pltpu
from jax.sharding import PartitionSpec as P

NS_STEPS = 12


highest = lax.Precision.HIGHEST


def rotate_in(basis_left, matrix, basis_right):
    half = jnp.einsum("sji,sjk->sik", basis_left, matrix, precision=highest)
    return jnp.einsum("sij,sjk->sik", half, basis_right, precision=highest)


def rotate_out(basis_left, matrix, basis_right):
    half = jnp.einsum("sij,sjk->sik", basis_left, matrix, precision=highest)
    return jnp.einsum("sij,skj->sik", half, basis_right, precision=highest)


def orthogonalize(stat, basis):
    power = jnp.einsum("sij,sjk->sik", stat, basis, precision=highest)
    scale = jnp.sqrt(jnp.sum(power * power, axis=(1, 2), keepdims=True) + 1e-06)
    iterate = power / scale
    for sweep in range(NS_STEPS):
        gram = jnp.einsum("sji,sjk->sik", iterate, iterate, precision=highest)
        iterate = 1.5 * iterate - 0.5 * jnp.einsum("sij,sjk->sik", iterate, gram, precision=highest)
    return iterate


def soap_tiles(grads, first, second, stat_left, stat_right, basis_left, basis_right):
    rotated = rotate_in(basis_left, grads, basis_right)
    moment = 0.95 * first + 0.05 * grads
    moment_rot = rotate_in(basis_left, moment, basis_right)
    second_new = 0.95 * second + 0.05 * rotated * rotated
    direction = rotate_out(basis_left, moment_rot / (jnp.sqrt(second_new) + 1e-08), basis_right)
    left_new = 0.95 * stat_left + 0.05 * jnp.einsum("sij,skj->sik", grads, grads, precision=highest)
    right_new = 0.95 * stat_right + 0.05 * jnp.einsum(
        "sji,sjk->sik", grads, grads, precision=highest
    )
    return (direction, orthogonalize(left_new, basis_left), orthogonalize(right_new, basis_right))


def per_device_plain(
    features,
    kv_cotangent,
    owner_of_block,
    first_moment,
    second_moment,
    left_stat,
    right_stat,
    left_basis,
    right_basis,
):
    tile = left_basis.shape[-1]
    capacity = left_basis.shape[1]
    d_win = features.shape[1]
    width = kv_cotangent.shape[1]
    row_tiles = d_win // tile
    col_tiles = width // tile
    nblocks = owner_of_block.shape[0]
    owner_here = lax.axis_index("dp")
    block_ids = jnp.arange(nblocks, dtype=jnp.int32)
    same = owner_of_block[:, None] == owner_of_block[None, :]
    earlier = block_ids[None, :] < block_ids[:, None]
    slot = jnp.sum((same & earlier).astype(jnp.int32), axis=1)
    slot_ids = jnp.arange(capacity, dtype=jnp.int32)
    match = (owner_of_block[None, :] == owner_here) & (slot[None, :] == slot_ids[:, None])
    live = jnp.any(match, axis=1)
    which = jnp.sum(jnp.where(match, block_ids[None, :], 0), axis=1)
    row_start = which // col_tiles * tile
    col_start = which % col_tiles * tile
    partial_grad = lax.dot_general(
        features, kv_cotangent, (((0,), (0,)), ((), ())), preferred_element_type=jnp.float32
    )
    grad = lax.psum(partial_grad, ("dp", "inner"))
    fetched = [
        lax.dynamic_slice(grad, (row_start[slot_index], col_start[slot_index]), (tile, tile))
        for slot_index in range(capacity)
    ]
    grads = jnp.stack(fetched)
    basis_left = left_basis[0].astype(jnp.float32)
    basis_right = right_basis[0].astype(jnp.float32)
    direction, left_iter, right_iter = soap_tiles(
        grads,
        first_moment[0],
        second_moment[0],
        left_stat[0],
        right_stat[0],
        basis_left,
        basis_right,
    )
    direction_low = direction.astype(jnp.bfloat16)
    everyone = lax.all_gather(direction_low[None], "dp", axis=0, tiled=True)
    tiles = everyone[owner_of_block, slot]
    update = (
        tiles.reshape(row_tiles, col_tiles, tile, tile).transpose(0, 2, 1, 3).reshape(d_win, width)
    )
    keep = live[:, None, None]
    new_left = jnp.where(keep, left_iter.astype(jnp.bfloat16), left_basis[0])
    new_right = jnp.where(keep, right_iter.astype(jnp.bfloat16), right_basis[0])
    return (update, new_left[None], new_right[None])


MM = ((1,), (0,))
MT = ((1,), (1,))
TM = ((0,), (0,))


def swap_along(values, axis, size, bit):
    return lax.ppermute(values, axis, [(i, i ^ bit) for i in range(size)])


def dot(left, right, dims):
    return lax.dot_general(left, right, (dims, ((), ())), preferred_element_type=jnp.float32)


def halves(x):
    high = x.astype(jnp.bfloat16)
    return high, (x - high.astype(jnp.float32)).astype(jnp.bfloat16)


def beside(a, b):
    return jnp.concatenate([a, b], axis=1)


def above(a, b):
    return jnp.concatenate([a, b], axis=0)


def folded(both):
    n = both.shape[1] // 2
    return both[:, :n] + both[:, n:]


def pair_product(left, right, dims):
    if dims == TM:
        rows = above(*left)
    else:
        rows = beside(*left)
    if dims == MT:
        return folded(dot(rows, above(beside(right[0], right[0]), beside(right[1], right[1])), MT))
    return folded(dot(rows, above(beside(*right), beside(*right)), dims))


def low_times(low, x, dims):
    high, rest = halves(x)
    if dims == MT:
        return dot(beside(low, low), beside(high, rest), MT)
    return dot(beside(low, low), above(high, rest), MM)


def times_low(x, low):
    high, rest = halves(x)
    return dot(beside(high, rest), above(low, low), MM)


def stream_offsets(owners):
    bits = owners.bit_length() - 1
    highs = list(range(2, bits))
    orders = ([0, 1] + highs, [1, 0] + highs, highs + [0, 1])
    offsets = [
        [sum(((p >> (bits - 1 - i)) & 1) << bit for i, bit in enumerate(order)) for p in range(owners)]
        for order in orders
    ]
    return orders, offsets


def table_kernel(owners, capacity, place_ref, owner_ref, kv_ref, *rest):
    table_ref, own_rows, count, held = rest
    own_rows[...] = kv_ref[...].T

    for o in range(owners):
        count[o] = 0

    def enter(b, carry):
        o = owner_ref[b]
        s = count[o]
        count[o] = s + 1
        held[o * capacity + s] = b
        return carry

    lax.fori_loop(0, owners * capacity, enter, 0, unroll=8)
    here, core = place_ref[0], place_ref[1]
    offsets = stream_offsets(owners)[1]
    for side in range(2):
        first_slot = 2 * (core ^ side)
        for stream in range(2):
            for p in range(owners):
                entry = (side * 2 + stream) * owners + p
                table_ref[entry] = held[(here ^ offsets[stream][p]) * capacity + first_slot + stream]


EDGE = 48


def tiles_kernel(owners, first, table_ref, f_own, f_sib, own_rows, kv_sib, *rest):
    sib_rows = rest[-1]
    out_a, out_b = rest[-5:-3] if first == 0 else rest[:2]
    tile = out_a.shape[-1]
    body = tile - EDGE
    near = owners // 2
    col_tiles = own_rows.shape[0] // tile
    offsets = stream_offsets(owners)[1]
    sib_rows[...] = kv_sib[...].T
    for stream, out in enumerate((out_a, out_b)):
        for i in range(near):
            block = table_ref[stream * owners + first + i]
            at = pl.ds(pl.multiple_of(block // col_tiles * tile, tile), tile)
            cots = pl.ds(pl.multiple_of(block % col_tiles * tile, tile), tile)
            total = dot(own_rows[cots, :], f_own[:, at], MM) + dot(
                sib_rows[cots, :], f_sib[:, at], MM
            )
            out[i] = total[:body]
            place = 2 * offsets[2].index(offsets[stream][first + i]) + stream
            if first:
                rest[2][place] = total[body:]
            elif place < owners:
                rest[-3][place] = total[body:]
            else:
                rest[-2][place - owners] = total[body:]
            if first == 0:
                place = 2 * offsets[2].index(offsets[stream][near + i]) + stream
                if place < owners:
                    rest[-3][place] = rest[0][place]
                else:
                    rest[-2][place - owners] = rest[0][place]


SMEM = pl.BlockSpec(memory_space=pltpu.SMEM)
HBM = pl.BlockSpec(memory_space=pltpu.HBM)
VMEM = pl.BlockSpec(memory_space=pltpu.VMEM)


def whole(shape):
    return pl.BlockSpec(shape, lambda *g: (0,) * len(shape))


def wholes(arrays):
    return [whole(a.shape) for a in arrays]


BIG = pltpu.CompilerParams(vmem_limit_bytes=24 * 2**20)
SMALL = pltpu.CompilerParams(vmem_limit_bytes=12 * 2**20)


def rotated_kernel(side_ref, m_ref, v_ref, l_ref, r_ref, ql_ref, qr_ref, *outs):
    rot_ref, second_ref, power_ref = outs
    for k in range(2):
        left = ql_ref[0, k]
        right = qr_ref[0, k]
        half = times_low(m_ref[0, k].T, left)
        rot_ref[k] = 0.95 * low_times(right.T, half, MM)
        second_ref[k] = 0.95 * v_ref[0, k].T
        power_ref[2 * k] = 0.95 * times_low(l_ref[0, k], left)
        power_ref[2 * k + 1] = 0.95 * times_low(r_ref[0, k], right)


def direction_kernel(side_ref, a_ref, b_ref, c_ref, d_ref, m_ref, v_ref, *rest):
    ql_ref, qr_ref, dir_ref, grad_ref = rest
    pair = range(2)
    lefts = [ql_ref[0, k] for k in pair]
    rights = [qr_ref[0, k] for k in pair]
    turned = [right.T for right in rights]
    grads = [above(a_ref[k] + b_ref[k], c_ref[k] + d_ref[k]) for k in pair]
    rots = [times_low(grads[k], lefts[k]) for k in pair]
    rots = [low_times(turned[k], rots[k], MM) for k in pair]
    scaled = []
    for k in pair:
        moment_rot = m_ref[k] + 0.05 * rots[k]
        second = v_ref[k] + 0.05 * rots[k] * rots[k]
        scaled.append(moment_rot / (jnp.sqrt(second) + 1e-08))
    outs = [low_times(rights[k], scaled[k], MM) for k in pair]
    outs = [low_times(lefts[k], outs[k], MT) for k in pair]
    for k in pair:
        dir_ref[k] = outs[k].astype(dir_ref.dtype)
        grad_ref[k] = grads[k]


def slots_of(*arrays):
    tile = arrays[0].shape[-1]
    return [pl.BlockSpec((1, 2, tile, tile), lambda i, s: (0, s[0], 0, 0)) for _ in arrays]


def on_slots(kernel, side, plain, slotted, outs, flops):
    return pl.pallas_call(
        kernel,
        out_shape=tuple(outs),
        grid_spec=pltpu.PrefetchScalarGridSpec(
            num_scalar_prefetch=1,
            grid=(1,),
            in_specs=wholes(plain) + slots_of(*slotted),
            out_specs=tuple(wholes(outs)),
        ),
        compiler_params=SMALL,
        cost_estimate=pl.CostEstimate(flops=flops, bytes_accessed=800_000, transcendentals=0),
        name=kernel.__name__.removesuffix("_kernel"),
    )(side, *plain, *slotted)


def sweep(values):
    pairs = [halves(y) for y in values]
    grams = [halves(pair_product(p, p, MT)) for p in pairs]
    return tuple(
        1.5 * y - 0.5 * pair_product(g, p, MM) for y, g, p in zip(values, grams, pairs)
    )


def sweeps(values, count):
    return lax.fori_loop(0, count, lambda i, v: sweep(v), tuple(values), unroll=2)


STAGES = (5, NS_STEPS - 5)


def refresh_kernel(side_ref, g_ref, power_ref, ql_ref, qr_ref, iter_ref):
    values = []
    for k in range(2):
        turned = g_ref[k]
        grad = turned.T
        for i, rows, columns, basis in ((0, grad, turned, ql_ref), (1, turned, grad, qr_ref)):
            half = times_low(columns, basis[0, k])
            power = power_ref[2 * k + i] + 0.05 * pair_product(halves(rows), halves(half), MM)
            values.append((power / jnp.sqrt(jnp.sum(power * power) + 1e-06)).T)
    for i, y in enumerate(sweeps(values, STAGES[0])):
        iter_ref[i] = y


def finish_kernel(iter_ref, out_ref):
    for i, y in enumerate(sweeps([iter_ref[i] for i in range(4)], STAGES[1])):
        out_ref[i] = y.T.astype(out_ref.dtype)


def sweeping(kernel, values, dtype, count):
    tile = values.shape[-1]
    return pl.pallas_call(
        kernel,
        out_shape=jax.ShapeDtypeStruct(values.shape, dtype),
        compiler_params=SMALL,
        cost_estimate=pl.CostEstimate(
            flops=4 * 2 * count * 4 * 2 * tile**3, bytes_accessed=400_000, transcendentals=0
        ),
        name=kernel.__name__.removesuffix("_kernel"),
    )(values)


def place_tiles(col_tiles, entries, table_ref, sources, out, sems):
    tile = sources[0].shape[-1]
    copies = []
    for entry, source in zip(entries, sources):
        for i in range(source.shape[0]):
            block = table_ref[entry + i]
            rows = pl.ds(pl.multiple_of(block // col_tiles * tile, tile), tile)
            columns = pl.ds(pl.multiple_of(block % col_tiles * tile, tile), tile)
            copies.append(
                pltpu.make_async_copy(source.at[i], out.at[rows, columns], sems.at[len(copies)])
            )
            copies[-1].start()
    return copies


def begin_kernel(col_tiles, entries, table_ref, place_ref, own_ref, sib_ref, *refs):
    sources = refs[:-4]
    out, left, right, sems = refs[-4:]
    copies = place_tiles(col_tiles, entries, table_ref, sources, out, sems)
    core = place_ref[1]
    for source, first in ((own_ref, 2 * core), (sib_ref, 2 - 2 * core)):
        for k in range(2):
            for i, target in enumerate((left, right)):
                copies.append(
                    pltpu.make_async_copy(
                        source.at[2 * k + i], target.at[0, first + k], sems.at[len(copies)]
                    )
                )
                copies[-1].start()
    for copy in copies:
        copy.wait()


def more_kernel(col_tiles, entries, table_ref, *refs):
    out, sems = refs[-2:]
    for copy in place_tiles(col_tiles, entries, table_ref, refs[:-3], out, sems):
        copy.wait()


def place_more(update, table, col_tiles, entries, sources):
    count = sum(x.shape[0] for x in sources)
    return pl.pallas_call(
        functools.partial(more_kernel, col_tiles, entries),
        out_shape=jax.ShapeDtypeStruct(update.shape, update.dtype),
        in_specs=[SMEM] + [VMEM] * len(sources) + [HBM],
        out_specs=HBM,
        scratch_shapes=[pltpu.SemaphoreType.DMA((count,))],
        input_output_aliases={1 + len(sources): 0},
        compiler_params=SMALL,
        cost_estimate=pl.CostEstimate(flops=0, bytes_accessed=1_000_000, transcendentals=0),
        name="more",
    )(table, *sources, update)


def per_device_dealt(
    owners,
    features,
    kv_cotangent,
    owner_of_block,
    first_moment,
    second_moment,
    left_stat,
    right_stat,
    left_basis,
    right_basis,
):
    tile = left_basis.shape[-1]
    capacity = left_basis.shape[1]
    rows, d_win = features.shape
    width = kv_cotangent.shape[1]
    col_tiles = width // tile
    here = lax.axis_index("dp")
    core = lax.axis_index("inner")
    place = jnp.stack([here, core]).astype(jnp.int32)
    side = core.reshape(1).astype(jnp.int32)
    orders = stream_offsets(owners)[0]
    near = owners // 2
    bits = len(orders[0])

    f_sib = swap_along(features, "inner", 2, 1)
    kv_sib = swap_along(kv_cotangent, "inner", 2, 1)
    flipped = pltpu.VMEM((width, rows), jnp.bfloat16)
    part = jax.ShapeDtypeStruct((near, tile - EDGE, tile), jnp.float32)
    edge = jax.ShapeDtypeStruct((owners, EDGE, tile), jnp.float32)
    edges = jax.ShapeDtypeStruct((2 * owners, EDGE, tile), jnp.float32)
    f32_pair = jax.ShapeDtypeStruct((2, tile, tile), jnp.float32)
    table, own_rows = pl.pallas_call(
        functools.partial(table_kernel, owners, capacity),
        out_shape=(
            jax.ShapeDtypeStruct((4 * owners,), jnp.int32),
            jax.ShapeDtypeStruct((width, rows), jnp.bfloat16),
        ),
        in_specs=[SMEM, SMEM, VMEM],
        out_specs=(SMEM, VMEM),
        compiler_params=SMALL,
        scratch_shapes=[
            pltpu.SMEM((owners,), jnp.int32),
            pltpu.SMEM((owners * capacity,), jnp.int32),
        ],
        cost_estimate=pl.CostEstimate(flops=0, bytes_accessed=1_000_000, transcendentals=0),
        name="table",
    )(place, owner_of_block, kv_cotangent)

    def tiles_from(first, outs, *more):
        inputs = (features, f_sib, own_rows, kv_sib, *more)
        return pl.pallas_call(
            functools.partial(tiles_kernel, owners, first),
            out_shape=outs,
            grid=(1,),
            in_specs=[SMEM] + wholes(inputs),
            out_specs=tuple(wholes(outs)),
            scratch_shapes=[flipped],
            compiler_params=BIG,
            cost_estimate=pl.CostEstimate(
                flops=2 * owners * 2 * tile * tile * 2 * rows,
                bytes_accessed=3_500_000,
                transcendentals=0,
            ),
            name="tiles",
        )(table, *inputs)

    sent_a, sent_b, early = tiles_from(near, (part, part, edges))
    got_a = swap_along(sent_a, "dp", owners, 1 << orders[0][0])
    got_b = swap_along(sent_b, "dp", owners, 1 << orders[1][0])
    kept_a, kept_b, kept_c, sent_c = tiles_from(0, (part, part, edge, edge), early)
    got_c = swap_along(sent_c, "dp", owners, 1 << orders[2][0])
    quad = jax.ShapeDtypeStruct((4, tile, tile), jnp.float32)
    moment_rot, second, power = on_slots(
        rotated_kernel,
        side,
        (),
        (first_moment, second_moment, left_stat, right_stat, left_basis, right_basis),
        (f32_pair, f32_pair, quad),
        16 * 2 * tile**3,
    )

    def halved(kept, got):
        half = kept.shape[0] // 2
        return kept[:half] + got[:half], kept[half:] + got[half:]

    def after(values, *needed):
        return lax.optimization_barrier((values, *needed))[0]

    def edges_on(step, kept, got):
        kept, sent = halved(kept, got)
        return kept, sent, swap_along(sent, "dp", owners, 1 << orders[2][step])

    kept_c, sent_c, got_c = edges_on(1, kept_c, got_c)
    kept_a, sent_a = halved(kept_a, got_a)
    kept_b, sent_b = halved(kept_b, got_b)
    got_a = swap_along(sent_a, "dp", owners, 1 << orders[0][1])
    got_b = swap_along(sent_b, "dp", owners, 1 << orders[1][1])
    kept = jnp.stack([kept_a, kept_b], axis=1)
    got = jnp.stack([got_a, got_b], axis=1)
    for step in range(2, bits):
        kept, sent = halved(kept, got)
        if step > 2:
            sent = after(sent, got_c)
            kept_c, sent_c, got_c = edges_on(step - 1, kept_c, got_c)
        if step == bits - 1:
            sent, kept = sent[0], kept[0]
        got = swap_along(sent, "dp", owners, 1 << orders[0][step])
    kept_c, sent_c, got_c = edges_on(bits - 1, kept_c, got_c)
    direction, grads = on_slots(
        direction_kernel,
        side,
        (kept, got, kept_c, got_c, moment_rot, second),
        (left_basis, right_basis),
        (jax.ShapeDtypeStruct(f32_pair.shape, jnp.bfloat16), f32_pair),
        16 * 2 * tile**3,
    )

    high = owners // 4
    tiles = []
    for p in range(high):
        offset = sum(((p >> (bits - 3 - i)) & 1) << bit for i, bit in enumerate(orders[0][2:]))
        tiles.append(swap_along(direction, "dp", owners, offset) if offset else direction)
    values = on_slots(
        refresh_kernel,
        side,
        (grads, power),
        (left_basis, right_basis),
        (quad,),
        4 * (4 + 2 * STAGES[0]) * 4 * 2 * tile**3,
    )[0]
    mine = [jnp.stack([t[stream] for t in tiles]) for stream in range(2)]
    mine, values = lax.optimization_barrier((mine, values))
    other = [swap_along(m, "dp", owners, 1 << order[1]) for m, order in zip(mine, orders)]
    fresh = sweeping(finish_kernel, values, jnp.bfloat16, STAGES[1])
    mine = [jnp.concatenate(both, axis=0) for both in zip(mine, other)]
    mine, fresh = lax.optimization_barrier((mine, fresh))
    other = [swap_along(m, "dp", owners, 1 << order[0]) for m, order in zip(mine, orders)]
    fresh_sib = swap_along(fresh, "inner", 2, 1)
    basis = jax.ShapeDtypeStruct(left_basis.shape, left_basis.dtype)
    update, new_left, new_right = pl.pallas_call(
        functools.partial(begin_kernel, col_tiles, (0, owners)),
        out_shape=(jax.ShapeDtypeStruct((d_win, width), jnp.bfloat16), basis, basis),
        in_specs=[SMEM, SMEM] + [VMEM] * 4,
        out_specs=(HBM, HBM, HBM),
        scratch_shapes=[pltpu.SemaphoreType.DMA((2 * near + 8,))],
        compiler_params=SMALL,
        cost_estimate=pl.CostEstimate(flops=0, bytes_accessed=800_000, transcendentals=0),
        name="begin",
    )(table, place, fresh, fresh_sib, *mine)
    update, other = lax.optimization_barrier((update, other))
    mine_sib = [swap_along(m, "inner", 2, 1) for m in mine]
    other_sib = [swap_along(o, "inner", 2, 1) for o in other]
    update = place_more(
        update,
        table,
        col_tiles,
        (2 * owners, 3 * owners, near, owners + near),
        mine_sib + other,
    )
    update = place_more(
        update, table, col_tiles, (2 * owners + near, 3 * owners + near), other_sib
    )
    return update, new_left, new_right


def solution(mesh):
    owners = mesh.shape["dp"]
    inner = mesh.shape["inner"]

    def per_device(*args):
        capacity = args[-1].shape[1]
        full = args[2].shape[0] == owners * capacity
        if full and inner == 2 and capacity == 4 and owners >= 8 and owners & (owners - 1) == 0:
            return per_device_dealt(owners, *args)
        return per_device_plain(*args)

    return jax.shard_map(
        per_device,
        mesh=mesh,
        in_specs=(
            P(("dp", "inner"), None),
            P(("dp", "inner"), None),
            P(),
            P("dp", None, None, None),
            P("dp", None, None, None),
            P("dp", None, None, None),
            P("dp", None, None, None),
            P("dp", None, None, None),
            P("dp", None, None, None),
        ),
        out_specs=(P(), P("dp", None, None, None), P("dp", None, None, None)),
        check_vma=False,
    )
```
